128 devices in a mesh: gx: 8 (over x_lo, y), gy: 16 (over x_hi, z, core).
Axes of the slice: x: 4 (x_hi: 2, x_lo: 2; x = x_hi * 2 + x_lo), y: 4, z: 4, core: 2. Of those that a mesh axis runs over, the one named last changes fastest.
Arguments:
- east_wind: bfloat16 [4096, 4096], P('gy', 'gx'), may hold values from -6 to 6
- north_wind: bfloat16 [4096, 4096], P('gy', 'gx'), may hold values from -6 to 6
- height: bfloat16 [4096, 4096], P('gy', 'gx'), may hold values from -6 to 6
- tracer: bfloat16 [4096, 4096], P('gy', 'gx'), may hold values from -6 to 6
Outputs:
- east_next: bfloat16 [4096, 4096], P('gy', 'gx')
- north_next: bfloat16 [4096, 4096], P('gy', 'gx')
- height_next: bfloat16 [4096, 4096], P('gy', 'gx')
- tracer_next: bfloat16 [4096, 4096], P('gy', 'gx')
The draws below stay inside these ranges and needn't reach their ends.
All inputs are finite; a program needn't handle non-finite values.
Results may differ from the reference program's by a relative error of at most 0.0014.
Values may be sent and summed in bfloat16 or wider, within the bound.
A program may use at most 128 MiB of HBM per device.

```python
import math
import jax
import jax.numpy as jnp
from jax import lax

NG = 4096


def block_levels(key, extent, pieces, low, largest):
    factor_of = 1.0
    for position, shards_of in pieces:
        draws = jax.random.uniform(jax.random.fold_in(jax.random.fold_in(key, 6), position), (shards_of,), jnp.float32, low / len(pieces), largest / len(pieces))
        factor_of = factor_of * jnp.repeat(jnp.exp(draws), extent[position] // shards_of).reshape((-1,) + (1,) * (len(extent) - 1 - position))
    return factor_of


def bell_draw(rng, shape, spread, reach, pieces=(), held_as=jnp.bfloat16):
    result = spread * jax.random.normal(rng, shape, jnp.float32)
    if pieces:
        result = result * block_levels(rng, shape, pieces, -0.22, 0.18)
    return jnp.clip(result, -reach, reach).astype(held_as)


def setup_inputs(seed: int = 0) -> dict:
    streams_of = jax.random.split(jax.random.key(seed), 5)
    east_wind = bell_draw(streams_of[0], (NG, NG), 1.0, 6.0, ((0, 16), (1, 8)))
    north_wind = bell_draw(streams_of[1], (NG, NG), 1.0, 6.0, ((0, 16), (1, 8)))
    height = bell_draw(streams_of[2], (NG, NG), 1.0, 6.0, ((0, 16), (1, 8)))
    tracer = bell_draw(streams_of[3], (NG, NG), 1.0, 6.0, ((0, 16), (1, 8)))
    return {"east_wind": east_wind, "north_wind": north_wind, "height": height, "tracer": tracer}


coriolis = 0.25
gravity_step = 2.0
depth_step = 2.0
diffusion = 0.02


def evolve(real_parts, imaginary_parts, wave_row, wave_column, points):
    nyquist = points // 2
    signed_row = jnp.where(wave_row < nyquist, wave_row, wave_row - points)
    signed_column = jnp.where(wave_column < nyquist, wave_column, wave_column - points)
    cutoff = points // 3
    inside = signed_row * signed_row + signed_column * signed_column <= cutoff * cutoff
    number_row = signed_row.astype(jnp.float32) * (2.0 * math.pi / points)
    number_column = signed_column.astype(jnp.float32) * (2.0 * math.pi / points)
    square = number_row * number_row + number_column * number_column
    filter_gain = jnp.where(inside, 1.0 / (1.0 + diffusion * square * square), 0.0)
    east_real, north_real, height_real, tracer_real = real_parts
    east_imaginary, north_imaginary, height_imaginary, tracer_imaginary = imaginary_parts
    diverge_real = -(number_column * east_imaginary + number_row * north_imaginary)
    diverge_imaginary = number_column * east_real + number_row * north_real
    vortex_real = -(number_column * north_imaginary - number_row * east_imaginary)
    vortex_imaginary = number_column * north_real - number_row * east_real
    stiffness = gravity_step * depth_step * square
    denominator = 1.0 + coriolis * coriolis + stiffness
    numerator_gain = 1.0 - coriolis * coriolis - stiffness
    spread_real = (diverge_real * numerator_gain + 2.0 * coriolis * vortex_real + 2.0 * gravity_step * square * height_real) / denominator
    spread_imaginary = (diverge_imaginary * numerator_gain + 2.0 * coriolis * vortex_imaginary + 2.0 * gravity_step * square * height_imaginary) / denominator
    summed_real = diverge_real + spread_real
    summed_imaginary = diverge_imaginary + spread_imaginary
    curl_real = vortex_real - coriolis * summed_real
    curl_imaginary = vortex_imaginary - coriolis * summed_imaginary
    level_real = height_real - depth_step * summed_real
    level_imaginary = height_imaginary - depth_step * summed_imaginary
    anchor = square == 0.0
    safe_square = jnp.where(anchor, 1.0, square)
    across_real = number_row * curl_real - number_column * spread_real
    across_imaginary = number_row * curl_imaginary - number_column * spread_imaginary
    along_real = number_column * curl_real + number_row * spread_real
    along_imaginary = number_column * curl_imaginary + number_row * spread_imaginary
    rotate_total = 1.0 + coriolis * coriolis
    keep_gain = 1.0 - coriolis * coriolis
    east_new_real = jnp.where(anchor, (keep_gain * east_real + 2.0 * coriolis * north_real) / rotate_total, -across_imaginary / safe_square)
    east_new_imaginary = jnp.where(anchor, (keep_gain * east_imaginary + 2.0 * coriolis * north_imaginary) / rotate_total, across_real / safe_square)
    north_new_real = jnp.where(anchor, (keep_gain * north_real - 2.0 * coriolis * east_real) / rotate_total, along_imaginary / safe_square)
    north_new_imaginary = jnp.where(anchor, (keep_gain * north_imaginary - 2.0 * coriolis * east_imaginary) / rotate_total, -along_real / safe_square)
    new_real = [east_new_real * filter_gain, north_new_real * filter_gain, level_real * filter_gain, tracer_real * filter_gain]
    new_imaginary = [east_new_imaginary * filter_gain, north_new_imaginary * filter_gain, level_imaginary * filter_gain, tracer_imaginary * filter_gain]
    return new_real, new_imaginary


def reference(east_wind, north_wind, height, tracer):
    points = NG
    spectra = [jnp.fft.rfft2(source.astype(jnp.float32)) for source in (east_wind, north_wind, height, tracer)]
    wave_row = lax.broadcasted_iota(jnp.int32, (points, 1), 0)
    wave_column = lax.broadcasted_iota(jnp.int32, (1, points // 2 + 1), 1)
    new_real, new_imaginary = evolve([jnp.real(member) for member in spectra], [jnp.imag(member) for member in spectra], wave_row, wave_column, points)
    results = [jnp.fft.irfft2(lax.complex(real_part, imaginary), s=(points, points)).astype(jnp.bfloat16) for real_part, imaginary in zip(new_real, new_imaginary)]
    return (results[0], results[1], results[2], results[3])
```

```python
import math

import jax
import jax.numpy as jnp
import numpy as np
from jax import lax
from jax.experimental import pallas as pl
from jax.experimental.pallas import tpu as pltpu
from jax.sharding import PartitionSpec as P

NG = 4096
FIELDS = 4
GX = 8
GY = 16
DEVICES = GX * GY
KX = 11
SLAB = 24
ROWS = 32
COLS = 512
POWER = 11

coriolis = 0.25
gravity_step = 2.0
depth_step = 2.0
diffusion = 0.02

F32 = jnp.float32
BF16 = jnp.bfloat16
MESH = pl.DeviceIdType.MESH


def split_const(matrix):
    whole = matrix.astype(np.float32)
    high = np.dtype(jnp.bfloat16)
    head = whole.astype(high)
    tail = (whole - head.astype(np.float32)).astype(high)
    return head, tail


def wave_of(slot, place):
    if slot == 0:
        return 32 * place if place < 43 else 16 + 32 * (place - 43)
    return slot + 32 * (place - 43)


def tables():
    turn = 2.0 * np.pi
    lane = np.arange(128)
    forward = np.zeros((2, GX, 2, SLAB // 2, 256))
    inverse = np.zeros((2, GX, 2, SLAB // 2, 256))
    for place in range(86):
        octant, member = place // KX, place % KX
        low = place - 43
        cosine, sine = np.cos(turn * lane * low / 128), np.sin(turn * lane * low / 128)
        forward[1, octant, 0, member] = np.concatenate([cosine, sine])
        forward[1, octant, 1, member] = np.concatenate([-sine, cosine])
        inverse[1, octant, 0, member] = np.concatenate([cosine, sine])
        inverse[1, octant, 1, member] = np.concatenate([-sine, cosine])
        wave = wave_of(0, place)
        cosine, sine = np.cos(turn * lane * wave / NG), np.sin(turn * lane * wave / NG)
        half = 0 if place < 43 else 128
        weight = 1.0 if wave == 0 else 2.0
        forward[0, octant, 0, member, half : half + 128] = cosine
        forward[0, octant, 1, member, half : half + 128] = -sine
        inverse[0, octant, 0, member, half : half + 128] = weight * cosine
        inverse[0, octant, 1, member, half : half + 128] = -weight * sine
    forward = forward.reshape(2, GX * SLAB, 256)
    inverse = inverse.reshape(2, GX * SLAB, 256)
    angle = turn * np.outer(np.arange(GY), lane) / NG
    twist = np.stack([np.cos(angle), np.sin(angle)], axis=1)[:, :, None, :]
    twist = np.broadcast_to(twist, (GY, 2, 16, 128)).astype(np.float32)
    angle = turn * np.outer(lane, lane) / 128
    cosine, sine = np.cos(angle), np.sin(angle)
    gather = np.block([[cosine, sine], [-sine, cosine]])
    scatter = np.block([[cosine, -sine], [sine, cosine]])
    angle = turn * np.outer(np.arange(ROWS), np.arange(ROWS)) / ROWS
    cosine, sine = np.kron(np.eye(4), np.cos(angle)), np.kron(np.eye(4), np.sin(angle))
    fan_in = np.block([[cosine, -sine], [sine, cosine]])
    fan_out = np.block([[cosine, sine], [-sine, cosine]])
    angle = turn * np.outer(lane, lane % ROWS) / NG
    spin = np.stack([np.cos(angle), np.sin(angle)]).astype(np.float32)
    pairs = []
    for matrix in (forward, inverse, gather, scatter, fan_in, fan_out):
        pairs.extend(split_const(matrix))
    return pairs + [twist, spin]


def real_transform(values):
    count = len(values)
    if count == 2:
        return [(values[0] + values[1], None), (values[0] - values[1], None)]
    even = real_transform(values[0::2])
    odd = real_transform(values[1::2])
    half = count // 2
    result = [None] * (half + 1)
    for index in range(count // 4 + 1):
        even_real, even_imag = even[index]
        odd_real, odd_imag = odd[index]
        if index == 0:
            result[0] = (even_real + odd_real, None)
            result[half] = (even_real - odd_real, None)
        elif index == count // 4:
            result[index] = (even_real, -odd_real)
        else:
            cosine = math.cos(2.0 * math.pi * index / count)
            sine = math.sin(2.0 * math.pi * index / count)
            turned_real = odd_real * cosine + odd_imag * sine
            turned_imag = odd_imag * cosine - odd_real * sine
            result[index] = (even_real + turned_real, even_imag + turned_imag)
            result[half - index] = (even_real - turned_real, turned_imag - even_imag)
    return result


def real_inverse(waves):
    half = len(waves) - 1
    count = 2 * half
    if count == 2:
        return [waves[0][0] + waves[1][0], waves[0][0] - waves[1][0]]
    even = []
    odd = []
    for index in range(count // 4 + 1):
        real, imag = waves[index]
        other_real, other_imag = waves[half - index]
        if index == 0:
            even.append((real + other_real, None))
            odd.append((real - other_real, None))
        elif index == count // 4:
            even.append((real + real, None))
            odd.append((-(imag + imag), None))
        else:
            cosine = math.cos(2.0 * math.pi * index / count)
            sine = math.sin(2.0 * math.pi * index / count)
            even.append((real + other_real, imag - other_imag))
            gap_real = real - other_real
            gap_imag = imag + other_imag
            odd.append((gap_real * cosine - gap_imag * sine, gap_real * sine + gap_imag * cosine))
    outputs = [None] * count
    outputs[0::2] = real_inverse(even)
    outputs[1::2] = real_inverse(odd)
    return outputs


def parts(values):
    head = values.astype(BF16)
    return head, (values - head.astype(F32)).astype(BF16)


def product(left, right, dims):
    return lax.dot_general(left, right, (dims, ((), ())), preferred_element_type=F32)


def product3(left, right, dims):
    left_head, left_tail = left
    right_head, right_tail = right
    return (
        product(left_head, right_head, dims)
        + product(left_head, right_tail, dims)
        + product(left_tail, right_head, dims)
    )


NN = ((1,), (0,))
NT = ((1,), (1,))
TN = ((0,), (0,))


def fill_gains(gains, octant, slot):
    chunk = 32

    def body(step, carry):
        member = step // (128 // chunk)
        top = (step % (128 // chunk)) * chunk
        place = KX * octant + member
        zero_slot = jnp.where(place < 43, 32 * place, 16 + 32 * (place - 43))
        mode_x = jnp.where(slot == 0, zero_slot, slot + 32 * (place - 43))
        lane = lax.broadcasted_iota(jnp.int32, (chunk, 128), 1)
        row = lax.broadcasted_iota(jnp.int32, (chunk, 128), 0) + top
        field = lane // 32
        mode_y = row + 128 * (lane % 32)
        mode_y = jnp.where(mode_y < NG // 2, mode_y, mode_y - NG)
        cutoff = NG // 3
        inside = mode_y * mode_y + mode_x * mode_x <= cutoff * cutoff
        unit = 2.0 * math.pi / NG
        wave_x = mode_x.astype(F32) * unit
        wave_y = mode_y.astype(F32) * unit
        square = wave_x * wave_x + wave_y * wave_y
        scale = 1.0 / (NG * NG)
        gain = jnp.where(inside, scale / (1.0 + diffusion * square * square), 0.0)
        stiffness = gravity_step * depth_step * square
        below = 1.0 / (1.0 + coriolis * coriolis + stiffness)
        above = (1.0 - coriolis * coriolis - stiffness) * below
        twice = (2.0 * coriolis) * below
        push_u = above * wave_x - twice * wave_y
        push_v = above * wave_y + twice * wave_x
        push_h = (2.0 * gravity_step) * square * below
        sum_u = wave_x + push_u
        sum_v = wave_y + push_v
        curl_u = -wave_y - coriolis * sum_u
        curl_v = wave_x - coriolis * sum_v
        curl_h = -coriolis * push_h
        anchor = square == 0.0
        over = 1.0 / jnp.where(anchor, 1.0, square)
        first = field == 0
        second = field == 1
        third = field == 2
        lead = jnp.where(first, -wave_y, wave_x)
        trail = jnp.where(first, wave_x, wave_y)
        from_u = (lead * curl_u + trail * push_u) * over
        from_v = (lead * curl_v + trail * push_v) * over
        from_h = -(lead * curl_h + trail * push_h) * over
        rotate = 1.0 / (1.0 + coriolis * coriolis)
        keep = (1.0 - coriolis * coriolis) * rotate
        cross = 2.0 * coriolis * rotate
        from_u = jnp.where(anchor, jnp.where(first, keep, -cross), from_u)
        from_v = jnp.where(anchor, jnp.where(first, cross, keep), from_v)
        zero = jnp.zeros_like(gain)
        same = jnp.where(
            first,
            from_u,
            jnp.where(second, from_v, jnp.where(third, 1.0 - depth_step * push_h, 1.0)),
        )
        one = jnp.where(second, from_u, jnp.where(third, -depth_step * sum_v, zero))
        two = jnp.where(first, from_h, jnp.where(third, -depth_step * sum_u, zero))
        three = jnp.where(first, from_v, jnp.where(second, from_h, zero))
        place_rows = pl.ds(pl.multiple_of(top, chunk), chunk)
        gains[member, 0, place_rows, :] = same * gain
        gains[member, 1, place_rows, :] = one * gain
        gains[member, 2, place_rows, :] = two * gain
        gains[member, 3, place_rows, :] = three * gain
        return carry

    lax.fori_loop(0, KX * (128 // chunk), body, 0)


def apply_gains(gains, member, real, imag):
    lane = lax.broadcasted_iota(jnp.int32, (128, 128), 1)
    field = lane // 32
    second = field == 1
    third = field == 2
    gain = gains[member, 0]
    out_real = real * gain
    out_imag = imag * gain
    crossed = [third, None, second]
    for turn in (1, 2, 3):
        gain = gains[member, turn]
        moved_real = pltpu.roll(real, 32 * turn, 1)
        moved_imag = pltpu.roll(imag, 32 * turn, 1)
        swap = crossed[turn - 1]
        if swap is None:
            use_real, use_imag = -moved_imag, moved_real
        else:
            use_real = jnp.where(swap, -moved_imag, moved_real)
            use_imag = jnp.where(swap, moved_real, moved_imag)
        out_real = out_real + gain * use_real
        out_imag = out_imag + gain * use_imag
    return out_real, out_imag


def step_kernel(*refs):
    sources = refs[0:4]
    (fwd_h, fwd_l, inv_h, inv_l, gat_h, gat_l, sca_h, sca_l, fin_h, fin_l, fout_h, fout_l) = refs[4:16]
    twist, spin = refs[16:18]
    results = refs[18:22]
    (
        grid_rows,
        head,
        tail,
        slabs,
        landed,
        columns,
        gains,
        returned,
        waves,
        new_rows,
        sem_rows_out,
        sem_rows_in,
        sem_out,
        sem_in,
        sem_back_out,
        sem_back_in,
        sem_last_out,
        sem_last_in,
    ) = refs[22:]
    octant = lax.axis_index("gx")
    slot_own = lax.axis_index("gy")
    own = slot_own * GX + octant

    barrier = pltpu.get_barrier_semaphore()

    def greet(step, carry):
        other = (own + step) % DEVICES
        pl.semaphore_signal(
            barrier, inc=1, device_id=(other % GX, other // GX), device_id_type=MESH
        )
        return carry

    lax.fori_loop(1, DEVICES, greet, 0)
    fill_gains(gains, octant, slot_own)
    pl.semaphore_wait(barrier, DEVICES - 1)

    for field in range(FIELDS):
        for step in range(1, GX):
            other = (octant + step) % GX
            pltpu.make_async_remote_copy(
                src_ref=sources[field].at[pl.ds(pl.multiple_of(other * ROWS, ROWS), ROWS), :],
                dst_ref=grid_rows.at[field, octant],
                send_sem=sem_rows_out.at[field],
                recv_sem=sem_rows_in.at[field],
                device_id=(other, slot_own),
                device_id_type=MESH,
            ).start()
        pltpu.make_async_copy(
            sources[field].at[pl.ds(pl.multiple_of(octant * ROWS, ROWS), ROWS), :],
            grid_rows.at[field, octant],
            sem_rows_in.at[field],
        ).start()

    def row_body(step, carry):
        field = step // 2
        part = step % 2
        top = pl.multiple_of(part * 16, 16)
        chunk = [
            grid_rows[field, c // 4, pl.ds(top, 16), (c % 4) * 128 : (c % 4) * 128 + 128].astype(F32)
            for c in range(32)
        ]
        spectrum = real_transform(chunk)
        rows = pl.ds(pl.multiple_of(step * 16, 16), 16)
        for slot in range(GY):
            if slot == 0:
                real, imag = spectrum[0][0], spectrum[16][0]
            else:
                wave_real, wave_imag = spectrum[slot]
                cosine, sine = twist[slot, 0], twist[slot, 1]
                real = wave_real * cosine + wave_imag * sine
                imag = wave_imag * cosine - wave_real * sine
            for side, value in ((0, real), (128, imag)):
                high, low = parts(value)
                head[slot, rows, side : side + 128] = high
                tail[slot, rows, side : side + 128] = low
        return carry

    for field in range(FIELDS):
        pltpu.make_async_copy(
            grid_rows.at[field], grid_rows.at[field], sem_rows_in.at[field]
        ).wait()
        lax.fori_loop(2 * field, 2 * field + 2, row_body, 0)

    def send(place, target, out_sem, in_sem):
        pltpu.make_async_remote_copy(
            src_ref=slabs.at[place],
            dst_ref=target.at[own],
            send_sem=out_sem,
            recv_sem=in_sem,
            device_id=(place % GX, place // GX),
            device_id_type=MESH,
        ).start()

    def slot_product(slot):
        which = (slot + GY - 1) // GY
        spectrum = product3(
            (fwd_h[which], fwd_l[which]), (head[slot], tail[slot]), NT
        )
        slabs[pl.ds(pl.multiple_of(slot * GX, GX), GX)] = spectrum.reshape(GX, SLAB, 128)

    slot_product(slot_own)
    for step in range(1, GX):
        send(slot_own * GX + (octant + step) % GX, landed, sem_out, sem_in)
    pltpu.make_async_copy(slabs.at[own], landed.at[own], sem_in).start()

    def slot_body(step, carry):
        slot = (slot_own + step) % GY
        slot_product(slot)
        for other in range(GX):
            send(slot * GX + (octant + other) % GX, landed, sem_out, sem_in)
        return carry

    lax.fori_loop(1, GY, slot_body, 0)

    pltpu.make_async_copy(landed, landed, sem_in).wait()

    def spread(source, carry):
        columns[pl.ds(source, SLAB, stride=128), :] = landed[source]
        return carry

    lax.fori_loop(0, DEVICES, spread, 0)

    def column_body(member, carry):
        real_rows = pl.ds(pl.multiple_of(member * 128, 128), 128)
        imag_rows = pl.ds(pl.multiple_of((member + SLAB // 2) * 128, 128), 128)
        values = jnp.concatenate([columns[real_rows, :], columns[imag_rows, :]], axis=0)
        mixed = product3((gat_h[...], gat_l[...]), parts(values), NN)
        real, imag = mixed[:128], mixed[128:]
        cosine, sine = spin[0], spin[1]
        turned = jnp.concatenate(
            [real * cosine + imag * sine, imag * cosine - real * sine], axis=1
        )
        modes = product3(parts(turned), (fin_h[...], fin_l[...]), NN)
        real, imag = apply_gains(gains, member, modes[:, :128], modes[:, 128:])
        modes = jnp.concatenate([real, imag], axis=1)
        mixed = product3(parts(modes), (fout_h[...], fout_l[...]), NN)
        real, imag = mixed[:, :128], mixed[:, 128:]
        values = jnp.concatenate(
            [real * cosine - imag * sine, imag * cosine + real * sine], axis=0
        )
        values = product3((sca_h[...], sca_l[...]), parts(values), NN)
        columns[real_rows, :] = values[:128]
        columns[imag_rows, :] = values[128:]
        return carry

    lax.fori_loop(0, KX, column_body, 0)

    sent = slabs.at[pl.ds(0, DEVICES - 1)]
    pltpu.make_async_copy(sent, sent, sem_out).wait()

    def collect(place):
        slabs[place] = columns[pl.ds(place, SLAB, stride=128), :]

    collect(own)
    pltpu.make_async_copy(slabs.at[own], returned.at[own], sem_back_in).start()

    def back_body(step, carry):
        place = (own + step) % DEVICES
        collect(place)
        send(place, returned, sem_back_out, sem_back_in)
        return carry

    lax.fori_loop(1, DEVICES, back_body, 0)
    pltpu.make_async_copy(returned, returned, sem_back_in).wait()

    def wave_body(slot, carry):
        which = (slot + GY - 1) // GY
        block = returned[pl.ds(pl.multiple_of(slot * GX, GX), GX)].reshape(GX * SLAB, 128)
        values = product3(parts(block), (inv_h[which], inv_l[which]), TN)
        real, imag = values[:, :128], values[:, 128:]
        cosine, sine = twist[slot, 0, 0:1, :], twist[slot, 1, 0:1, :]
        waves[slot, :, 0:128] = real * cosine - imag * sine
        waves[slot, :, 128:256] = imag * cosine + real * sine
        return carry

    lax.fori_loop(0, GY, wave_body, 0)

    def grid_body(step, carry):
        field = step // 2
        part = step % 2
        rows = pl.ds(pl.multiple_of(step * 16, 16), 16)
        spectrum = [(waves[0, rows, 0:128], None)]
        for slot in range(1, GY):
            spectrum.append((waves[slot, rows, 0:128], waves[slot, rows, 128:256]))
        spectrum.append((waves[0, rows, 128:256], None))
        values = real_inverse(spectrum)
        top = pl.ds(pl.multiple_of(part * 16, 16), 16)
        for c in range(32):
            new_rows[field, c // 4, top, (c % 4) * 128 : (c % 4) * 128 + 128] = values[c].astype(BF16)
        return carry

    for field in range(FIELDS):
        lax.fori_loop(2 * field, 2 * field + 2, grid_body, 0)
        own_rows = pl.ds(pl.multiple_of(octant * ROWS, ROWS), ROWS)
        for step in range(1, GX):
            other = (octant + step) % GX
            pltpu.make_async_remote_copy(
                src_ref=new_rows.at[field, other],
                dst_ref=results[field].at[own_rows, :],
                send_sem=sem_last_out.at[field],
                recv_sem=sem_last_in.at[field],
                device_id=(other, slot_own),
                device_id_type=MESH,
            ).start()
        pltpu.make_async_copy(
            new_rows.at[field, octant], results[field].at[own_rows, :], sem_last_in.at[field]
        ).start()

    sent = slabs.at[pl.ds(0, DEVICES - 1)]
    pltpu.make_async_copy(sent, sent, sem_back_out).wait()
    for field in range(FIELDS):
        moved = new_rows.at[field, pl.ds(0, GX - 1)]
        pltpu.make_async_copy(moved, moved, sem_rows_out.at[field]).wait()
        pltpu.make_async_copy(moved, moved, sem_last_out.at[field]).wait()
        pltpu.make_async_copy(results[field], results[field], sem_last_in.at[field]).wait()


def per_device(east_wind, north_wind, height, tracer):
    constants = [jnp.asarray(value) for value in tables()]
    anywhere = pl.BlockSpec(memory_space=pl.ANY)
    vmem = pl.BlockSpec(memory_space=pltpu.VMEM)
    block = jax.ShapeDtypeStruct((NG // GY, COLS), BF16)
    dma = pltpu.SemaphoreType.DMA
    return pl.pallas_call(
        step_kernel,
        out_shape=(block,) * 4,
        in_specs=[anywhere] * 4 + [vmem] * len(constants),
        out_specs=(anywhere,) * 4,
        scratch_shapes=[
            pltpu.VMEM((FIELDS, GX, ROWS, COLS), BF16),
            pltpu.VMEM((GY, 128, 256), BF16),
            pltpu.VMEM((GY, 128, 256), BF16),
            pltpu.VMEM((DEVICES, SLAB, 128), F32),
            pltpu.VMEM((DEVICES, SLAB, 128), F32),
            pltpu.VMEM((SLAB * 128, 128), F32),
            pltpu.VMEM((KX, 4, 128, 128), F32),
            pltpu.VMEM((DEVICES, SLAB, 128), F32),
            pltpu.VMEM((GY, 128, 256), F32),
            pltpu.VMEM((FIELDS, GX, ROWS, COLS), BF16),
            dma((FIELDS,)),
            dma((FIELDS,)),
            dma,
            dma,
            dma,
            dma,
            dma((FIELDS,)),
            dma((FIELDS,)),
        ],
        compiler_params=pltpu.CompilerParams(collective_id=0, has_side_effects=True),
    )(east_wind, north_wind, height, tracer, *constants)


def solution(mesh):
    placed = (P("gy", "gx"),) * 4
    return jax.shard_map(
        per_device, mesh=mesh, in_specs=placed, out_specs=placed, check_vma=False
    )
```

```python
import math

import jax
import jax.numpy as jnp
import numpy as np
from jax import lax
from jax.experimental import pallas as pl
from jax.experimental.pallas import tpu as pltpu
from jax.sharding import PartitionSpec as P

NG = 4096
FIELDS = 4
GX = 8
GY = 16
DEVICES = GX * GY
KX = 11
SLAB = 24
ROWS = 32
COLS = 512
POWER = 11

coriolis = 0.25
gravity_step = 2.0
depth_step = 2.0
diffusion = 0.02

F32 = jnp.float32
BF16 = jnp.bfloat16
MESH = pl.DeviceIdType.MESH


def split_const(matrix):
    whole = matrix.astype(np.float32)
    high = np.dtype(jnp.bfloat16)
    head = whole.astype(high)
    tail = (whole - head.astype(np.float32)).astype(high)
    return head, tail


def wave_of(slot, place):
    if slot == 0:
        return 32 * place if place < 43 else 16 + 32 * (place - 43)
    return slot + 32 * (place - 43)


def tables():
    turn = 2.0 * np.pi
    lane = np.arange(128)
    forward = np.zeros((2, GX, 2, SLAB // 2, 256))
    inverse = np.zeros((2, GX, 2, SLAB // 2, 256))
    for place in range(86):
        octant, member = place // KX, place % KX
        low = place - 43
        cosine, sine = np.cos(turn * lane * low / 128), np.sin(turn * lane * low / 128)
        forward[1, octant, 0, member] = np.concatenate([cosine, sine])
        forward[1, octant, 1, member] = np.concatenate([-sine, cosine])
        inverse[1, octant, 0, member] = np.concatenate([cosine, sine])
        inverse[1, octant, 1, member] = np.concatenate([-sine, cosine])
        wave = wave_of(0, place)
        cosine, sine = np.cos(turn * lane * wave / NG), np.sin(turn * lane * wave / NG)
        half = 0 if place < 43 else 128
        weight = 1.0 if wave == 0 else 2.0
        forward[0, octant, 0, member, half : half + 128] = cosine
        forward[0, octant, 1, member, half : half + 128] = -sine
        inverse[0, octant, 0, member, half : half + 128] = weight * cosine
        inverse[0, octant, 1, member, half : half + 128] = -weight * sine
    forward = forward.reshape(2, GX * SLAB, 256)
    inverse = inverse.reshape(2, GX * SLAB, 256)
    angle = turn * np.outer(np.arange(GY), lane) / NG
    twist = np.stack([np.cos(angle), np.sin(angle)], axis=1)[:, :, None, :]
    twist = np.broadcast_to(twist, (GY, 2, 16, 128)).astype(np.float32)
    angle = turn * np.outer(lane, lane) / 128
    cosine, sine = np.cos(angle), np.sin(angle)
    gather = np.block([[cosine, sine], [-sine, cosine]])
    scatter = np.block([[cosine, -sine], [sine, cosine]])
    angle = turn * np.outer(np.arange(ROWS), np.arange(ROWS)) / ROWS
    cosine, sine = np.kron(np.eye(4), np.cos(angle)), np.kron(np.eye(4), np.sin(angle))
    fan_in = np.block([[cosine, -sine], [sine, cosine]])
    fan_out = np.block([[cosine, sine], [-sine, cosine]])
    angle = turn * np.outer(lane, lane % ROWS) / NG
    spin = np.stack([np.cos(angle), np.sin(angle)]).astype(np.float32)
    pieces = []
    for matrix in (forward.reshape(-1, 256), inverse.reshape(-1, 256) / NG, gather, scatter, fan_in, fan_out):
        pieces.extend(split_const(matrix))
    floats = np.concatenate([twist.reshape(-1, 128), spin.reshape(-1, 128)], axis=0)
    return np.concatenate(pieces, axis=0), floats


FWD_AT = 0
INV_AT = 4 * GX * SLAB
SQUARE_AT = 8 * GX * SLAB
MATRIX_ROWS = SQUARE_AT + 8 * 256
SPIN_AT = GY * 2 * 16
FLOAT_ROWS = SPIN_AT + 256


def matrix_pair(matrices, start, which):
    count = GX * SLAB
    first = pl.multiple_of(start + which * count, 64)
    second = pl.multiple_of(start + (which + 2) * count, 64)
    return matrices[pl.ds(first, count), :], matrices[pl.ds(second, count), :]


def square_pair(matrices, which):
    first = SQUARE_AT + which * 512
    return matrices[first : first + 256, :], matrices[first + 256 : first + 512, :]


def encode(values):
    largest = jnp.max(jnp.abs(values), axis=1, keepdims=True)
    scale = (jnp.maximum(largest, 1e-34) * 1.01).astype(BF16).astype(F32)
    level = values * (2048.0 / scale)
    second = level * level
    fourth = second * second
    eighth = fourth * fourth
    code = eighth * second * level
    row = lax.broadcasted_iota(jnp.int32, values.shape, 1)
    code = jnp.where(row == KX, scale, code)
    return code.reshape(values.shape[0], SLAB // 8, 8, 128).astype(BF16)


def decode(codes):
    code = codes.astype(F32).reshape(codes.shape[0], SLAB, 128)
    scale = code[:, KX : KX + 1, :] * (1.0 / 2048.0)
    level = jnp.exp2(jnp.log2(jnp.abs(code)) * (1.0 / POWER))
    level = jnp.where(code < 0.0, -level, level)
    return jnp.where(code == 0.0, 0.0, level) * scale


def real_transform(values):
    count = len(values)
    if count == 2:
        return [(values[0] + values[1], None), (values[0] - values[1], None)]
    even = real_transform(values[0::2])
    odd = real_transform(values[1::2])
    half = count // 2
    result = [None] * (half + 1)
    for index in range(count // 4 + 1):
        even_real, even_imag = even[index]
        odd_real, odd_imag = odd[index]
        if index == 0:
            result[0] = (even_real + odd_real, None)
            result[half] = (even_real - odd_real, None)
        elif index == count // 4:
            result[index] = (even_real, -odd_real)
        else:
            cosine = math.cos(2.0 * math.pi * index / count)
            sine = math.sin(2.0 * math.pi * index / count)
            turned_real = odd_real * cosine + odd_imag * sine
            turned_imag = odd_imag * cosine - odd_real * sine
            result[index] = (even_real + turned_real, even_imag + turned_imag)
            result[half - index] = (even_real - turned_real, turned_imag - even_imag)
    return result


def real_inverse(waves):
    half = len(waves) - 1
    count = 2 * half
    if count == 2:
        return [waves[0][0] + waves[1][0], waves[0][0] - waves[1][0]]
    even = []
    odd = []
    for index in range(count // 4 + 1):
        real, imag = waves[index]
        other_real, other_imag = waves[half - index]
        if index == 0:
            even.append((real + other_real, None))
            odd.append((real - other_real, None))
        elif index == count // 4:
            even.append((real + real, None))
            odd.append((-(imag + imag), None))
        else:
            cosine = math.cos(2.0 * math.pi * index / count)
            sine = math.sin(2.0 * math.pi * index / count)
            even.append((real + other_real, imag - other_imag))
            gap_real = real - other_real
            gap_imag = imag + other_imag
            odd.append((gap_real * cosine - gap_imag * sine, gap_real * sine + gap_imag * cosine))
    outputs = [None] * count
    outputs[0::2] = real_inverse(even)
    outputs[1::2] = real_inverse(odd)
    return outputs


def parts(values):
    head = values.astype(BF16)
    return head, (values - head.astype(F32)).astype(BF16)


def product(left, right, dims):
    return lax.dot_general(left, right, (dims, ((), ())), preferred_element_type=F32)


def product3(left, right, dims):
    left_head, left_tail = left
    right_head, right_tail = right
    return (
        product(left_head, right_head, dims)
        + product(left_head, right_tail, dims)
        + product(left_tail, right_head, dims)
    )


NN = ((1,), (0,))
NT = ((1,), (1,))
TN = ((0,), (0,))


def fill_gains(gains, octant, slot):
    chunk = 32

    def body(step, carry):
        member = step // (128 // chunk)
        top = (step % (128 // chunk)) * chunk
        place = KX * octant + member
        zero_slot = jnp.where(place < 43, 32 * place, 16 + 32 * (place - 43))
        mode_x = jnp.where(slot == 0, zero_slot, slot + 32 * (place - 43))
        lane = lax.broadcasted_iota(jnp.int32, (chunk, 128), 1)
        row = lax.broadcasted_iota(jnp.int32, (chunk, 128), 0) + top
        field = lane // 32
        mode_y = row + 128 * (lane % 32)
        mode_y = jnp.where(mode_y < NG // 2, mode_y, mode_y - NG)
        cutoff = NG // 3
        inside = mode_y * mode_y + mode_x * mode_x <= cutoff * cutoff
        unit = 2.0 * math.pi / NG
        wave_x = mode_x.astype(F32) * unit
        wave_y = mode_y.astype(F32) * unit
        square = wave_x * wave_x + wave_y * wave_y
        scale = 1.0 / NG
        gain = jnp.where(inside, scale / (1.0 + diffusion * square * square), 0.0)
        stiffness = gravity_step * depth_step * square
        below = 1.0 / (1.0 + coriolis * coriolis + stiffness)
        above = (1.0 - coriolis * coriolis - stiffness) * below
        twice = (2.0 * coriolis) * below
        push_u = above * wave_x - twice * wave_y
        push_v = above * wave_y + twice * wave_x
        push_h = (2.0 * gravity_step) * square * below
        sum_u = wave_x + push_u
        sum_v = wave_y + push_v
        curl_u = -wave_y - coriolis * sum_u
        curl_v = wave_x - coriolis * sum_v
        curl_h = -coriolis * push_h
        anchor = square == 0.0
        over = 1.0 / jnp.where(anchor, 1.0, square)
        first = field == 0
        second = field == 1
        third = field == 2
        lead = jnp.where(first, -wave_y, wave_x)
        trail = jnp.where(first, wave_x, wave_y)
        from_u = (lead * curl_u + trail * push_u) * over
        from_v = (lead * curl_v + trail * push_v) * over
        from_h = -(lead * curl_h + trail * push_h) * over
        rotate = 1.0 / (1.0 + coriolis * coriolis)
        keep = (1.0 - coriolis * coriolis) * rotate
        cross = 2.0 * coriolis * rotate
        from_u = jnp.where(anchor, jnp.where(first, keep, -cross), from_u)
        from_v = jnp.where(anchor, jnp.where(first, cross, keep), from_v)
        zero = jnp.zeros_like(gain)
        same = jnp.where(
            first,
            from_u,
            jnp.where(second, from_v, jnp.where(third, 1.0 - depth_step * push_h, 1.0)),
        )
        one = jnp.where(second, from_u, jnp.where(third, -depth_step * sum_v, zero))
        two = jnp.where(first, from_h, jnp.where(third, -depth_step * sum_u, zero))
        three = jnp.where(first, from_v, jnp.where(second, from_h, zero))
        place_rows = pl.ds(pl.multiple_of(top, chunk), chunk)
        gains[member, 0, place_rows, :] = same * gain
        gains[member, 1, place_rows, :] = one * gain
        gains[member, 2, place_rows, :] = two * gain
        gains[member, 3, place_rows, :] = three * gain
        return carry

    lax.fori_loop(0, KX * (128 // chunk), body, 0)
    gains[KX] = jnp.zeros((4, 128, 128), F32)


def apply_gains(gains, member, real, imag):
    lane = lax.broadcasted_iota(jnp.int32, (128, 128), 1)
    field = lane // 32
    second = field == 1
    third = field == 2
    gain = gains[member, 0]
    out_real = real * gain
    out_imag = imag * gain
    crossed = [third, None, second]
    for turn in (1, 2, 3):
        gain = gains[member, turn]
        moved_real = pltpu.roll(real, 32 * turn, 1)
        moved_imag = pltpu.roll(imag, 32 * turn, 1)
        swap = crossed[turn - 1]
        if swap is None:
            use_real, use_imag = -moved_imag, moved_real
        else:
            use_real = jnp.where(swap, -moved_imag, moved_real)
            use_imag = jnp.where(swap, moved_real, moved_imag)
        out_real = out_real + gain * use_real
        out_imag = out_imag + gain * use_imag
    return out_real, out_imag


def step_kernel(*refs):
    sources = refs[0:4]
    matrix_source, float_source = refs[4:6]
    results = refs[6:10]
    (
        matrices,
        floats,
        grid_rows,
        head,
        tail,
        slabs,
        landed,
        columns,
        gains,
        returned,
        waves,
        new_rows,
        sem_table,
        sem_rows_out,
        sem_rows_in,
        sem_out,
        sem_in,
        sem_back_out,
        sem_back_in,
        sem_last_out,
        sem_last_in,
        sem_leaders,
        sem_all,
    ) = refs[10:]
    octant = lax.axis_index("gx")
    slot_own = lax.axis_index("gy")
    own = slot_own * GX + octant
    octants = [(octant + step) % GX for step in range(GX)]

    def slot_at(step):
        slot = slot_own + step
        return jnp.where(slot >= GY, slot - GY, slot)

    def slot_before(step):
        slot = slot_own - step
        return jnp.where(slot < 0, slot + GY, slot)

    barrier = pltpu.get_barrier_semaphore()
    for step in range(1, GX):
        pl.semaphore_signal(
            barrier, inc=1, device_id=(octants[step], slot_own), device_id_type=MESH
        )

    @pl.when(octant == 0)
    def greet_leaders():
        for step in range(1, GY):
            pl.semaphore_signal(
                barrier, inc=1, device_id=(octant, slot_at(step)), device_id_type=MESH
            )

    table_copies = [
        pltpu.make_async_copy(matrix_source, matrices, sem_table.at[0]),
        pltpu.make_async_copy(float_source, floats, sem_table.at[1]),
    ]
    for copy in table_copies:
        copy.start()
    own_rows = pl.ds(pl.multiple_of(octant * ROWS, ROWS), ROWS)
    for field in range(FIELDS):
        pltpu.make_async_copy(
            sources[field].at[own_rows, :], grid_rows.at[field, octant], sem_rows_in.at[field]
        ).start()

    @pl.when(octant == 0)
    def wait_leader():
        pl.semaphore_wait(barrier, GX - 1 + GY - 1)

    @pl.when(octant != 0)
    def wait_member():
        pl.semaphore_wait(barrier, GX - 1)

    for field in range(FIELDS):
        for step in range(1, GX):
            other = octants[step]
            pltpu.make_async_remote_copy(
                src_ref=sources[field].at[pl.ds(pl.multiple_of(other * ROWS, ROWS), ROWS), :],
                dst_ref=grid_rows.at[field, octant],
                send_sem=sem_rows_out.at[field],
                recv_sem=sem_rows_in.at[field],
                device_id=(other, slot_own),
                device_id_type=MESH,
            ).start()

    @pl.when(octant == 0)
    def tell_leaders():
        for step in range(1, GY):
            pl.semaphore_signal(
                sem_leaders, inc=1, device_id=(octant, slot_at(step)), device_id_type=MESH
            )

    fill_gains(gains, octant, slot_own)

    @pl.when(octant == 0)
    def tell_members():
        pl.semaphore_wait(sem_leaders, GY - 1)
        for step in range(1, GX):
            pl.semaphore_signal(
                sem_all, inc=1, device_id=(octants[step], slot_own), device_id_type=MESH
            )

    for copy in table_copies:
        copy.wait()

    def row_body(step, carry):
        field = step // 2
        part = step % 2
        top = pl.multiple_of(part * 16, 16)
        chunk = [
            grid_rows[field, c // 4, pl.ds(top, 16), (c % 4) * 128 : (c % 4) * 128 + 128].astype(F32)
            for c in range(32)
        ]
        spectrum = real_transform(chunk)
        rows = pl.ds(pl.multiple_of(step * 16, 16), 16)
        for slot in range(GY):
            if slot == 0:
                real, imag = spectrum[0][0], spectrum[16][0]
            else:
                wave_real, wave_imag = spectrum[slot]
                cosine = floats[32 * slot : 32 * slot + 16, :]
                sine = floats[32 * slot + 16 : 32 * slot + 32, :]
                real = wave_real * cosine + wave_imag * sine
                imag = wave_imag * cosine - wave_real * sine
            for side, value in ((0, real), (128, imag)):
                high, low = parts(value)
                head[slot, rows, side : side + 128] = high
                tail[slot, rows, side : side + 128] = low
        return carry

    for field in range(FIELDS):
        pltpu.make_async_copy(
            grid_rows.at[field], grid_rows.at[field], sem_rows_in.at[field]
        ).wait()
        lax.fori_loop(2 * field, 2 * field + 2, row_body, 0)

    @pl.when(octant != 0)
    def wait_all():
        pl.semaphore_wait(sem_all, 1)

    def send(slot, other, target, out_sem, in_sem):
        pltpu.make_async_remote_copy(
            src_ref=slabs.at[slot * GX + other],
            dst_ref=target.at[own],
            send_sem=out_sem,
            recv_sem=in_sem.at[slot_own],
            device_id=(other, slot),
            device_id_type=MESH,
        ).start()

    def slot_product(slot):
        which = jnp.minimum(slot, 1)
        spectrum = product3(
            matrix_pair(matrices, FWD_AT, which), (head[slot], tail[slot]), NT
        )
        slabs[pl.ds(slot * GX, GX)] = encode(spectrum.reshape(GX, SLAB, 128))

    slot_product(slot_own)
    for step in range(1, GX):
        send(slot_own, octants[step], landed, sem_out, sem_in)
    pltpu.make_async_copy(slabs.at[own], landed.at[own], sem_in.at[slot_own]).start()

    def slot_body(step, carry):
        slot = slot_at(step)
        slot_product(slot)
        for other in octants:
            send(slot, other, landed, sem_out, sem_in)
        return carry

    lax.fori_loop(1, GY, slot_body, 0)

    def spread(step, carry):
        slot = slot_before(step)
        group = landed.at[pl.ds(slot * GX, GX)]
        pltpu.make_async_copy(group, group, sem_in.at[slot]).wait()
        values = decode(landed[pl.ds(slot * GX, GX)])
        for source in range(GX):
            columns[pl.ds(slot * GX + source, SLAB, stride=128), :] = values[source]
        return carry

    lax.fori_loop(0, GY, spread, 0)

    def column_body(pair, carry):
        real_rows = pl.ds(pl.multiple_of(pair * 256, 256), 256)
        imag_rows = pl.ds(pl.multiple_of(pair * 256 + SLAB // 2 * 128, 256), 256)
        real, imag = columns[real_rows, :], columns[imag_rows, :]
        values = jnp.concatenate(
            [
                jnp.concatenate([real[:128], real[128:]], axis=1),
                jnp.concatenate([imag[:128], imag[128:]], axis=1),
            ],
            axis=0,
        )
        mixed = product3(square_pair(matrices, 0), parts(values), NN)
        cosine = floats[SPIN_AT : SPIN_AT + 128, :]
        sine = floats[SPIN_AT + 128 : SPIN_AT + 256, :]
        turned = []
        for side in (0, 128):
            real, imag = mixed[:128, side : side + 128], mixed[128:, side : side + 128]
            turned.append(
                jnp.concatenate([real * cosine + imag * sine, imag * cosine - real * sine], axis=1)
            )
        turned = jnp.concatenate(turned, axis=0)
        modes = product3(parts(turned), square_pair(matrices, 2), NN)
        changed = []
        for member in range(2):
            piece = modes[128 * member : 128 * member + 128]
            real, imag = apply_gains(gains, 2 * pair + member, piece[:, :128], piece[:, 128:])
            changed.append(jnp.concatenate([real, imag], axis=1))
        changed = jnp.concatenate(changed, axis=0)
        mixed = product3(parts(changed), square_pair(matrices, 3), NN)
        reals, imags = [], []
        for member in range(2):
            piece = mixed[128 * member : 128 * member + 128]
            real, imag = piece[:, :128], piece[:, 128:]
            reals.append(real * cosine - imag * sine)
            imags.append(imag * cosine + real * sine)
        values = jnp.concatenate(
            [jnp.concatenate(reals, axis=1), jnp.concatenate(imags, axis=1)], axis=0
        )
        values = product3(square_pair(matrices, 1), parts(values), NN)
        columns[real_rows, :] = jnp.concatenate([values[:128, :128], values[:128, 128:]], axis=0)
        columns[imag_rows, :] = jnp.concatenate([values[128:, :128], values[128:, 128:]], axis=0)
        return carry

    lax.fori_loop(0, (KX + 1) // 2, column_body, 0)

    sent = slabs.at[pl.ds(0, DEVICES - 1)]
    pltpu.make_async_copy(sent, sent, sem_out).wait()

    def collect(slot):
        first = slot * GX
        values = jnp.stack(
            [columns[pl.ds(first + source, SLAB, stride=128), :] for source in range(GX)]
        )
        slabs[pl.ds(first, GX)] = encode(values)

    collect(slot_own)
    for step in range(1, GX):
        send(slot_own, octants[step], returned, sem_back_out, sem_back_in)
    pltpu.make_async_copy(slabs.at[own], returned.at[own], sem_back_in.at[slot_own]).start()

    def back_body(step, carry):
        slot = slot_at(step)
        collect(slot)
        for other in octants:
            send(slot, other, returned, sem_back_out, sem_back_in)
        return carry

    lax.fori_loop(1, GY, back_body, 0)

    def wave_body(step, carry):
        slot = slot_before(step)
        group = returned.at[pl.ds(slot * GX, GX)]
        pltpu.make_async_copy(group, group, sem_back_in.at[slot]).wait()
        which = jnp.minimum(slot, 1)
        block = decode(returned[pl.ds(slot * GX, GX)]).reshape(GX * SLAB, 128)
        values = product3(parts(block), matrix_pair(matrices, INV_AT, which), TN)
        real, imag = values[:, :128], values[:, 128:]
        cosine = floats[pl.ds(32 * slot, 1), :]
        sine = floats[pl.ds(32 * slot + 16, 1), :]
        waves[slot, :, 0:128] = real * cosine - imag * sine
        waves[slot, :, 128:256] = imag * cosine + real * sine
        return carry

    lax.fori_loop(0, GY, wave_body, 0)

    def grid_body(step, carry):
        field = step // 2
        part = step % 2
        rows = pl.ds(pl.multiple_of(step * 16, 16), 16)
        spectrum = [(waves[0, rows, 0:128], None)]
        for slot in range(1, GY):
            spectrum.append((waves[slot, rows, 0:128], waves[slot, rows, 128:256]))
        spectrum.append((waves[0, rows, 128:256], None))
        values = real_inverse(spectrum)
        top = pl.ds(pl.multiple_of(part * 16, 16), 16)
        for c in range(32):
            new_rows[field, c // 4, top, (c % 4) * 128 : (c % 4) * 128 + 128] = values[c].astype(BF16)
        return carry

    for field in range(FIELDS):
        lax.fori_loop(2 * field, 2 * field + 2, grid_body, 0)
        for step in range(1, GX):
            other = octants[step]
            pltpu.make_async_remote_copy(
                src_ref=new_rows.at[field, other],
                dst_ref=results[field].at[own_rows, :],
                send_sem=sem_last_out.at[field],
                recv_sem=sem_last_in.at[field],
                device_id=(other, slot_own),
                device_id_type=MESH,
            ).start()
        pltpu.make_async_copy(
            new_rows.at[field, octant], results[field].at[own_rows, :], sem_last_in.at[field]
        ).start()

    pltpu.make_async_copy(sent, sent, sem_back_out).wait()
    for field in range(FIELDS):
        moved = new_rows.at[field, pl.ds(0, GX - 1)]
        pltpu.make_async_copy(moved, moved, sem_rows_out.at[field]).wait()
        pltpu.make_async_copy(moved, moved, sem_last_out.at[field]).wait()
        pltpu.make_async_copy(results[field], results[field], sem_last_in.at[field]).wait()


def per_device(east_wind, north_wind, height, tracer):
    constants = [jnp.asarray(value) for value in tables()]
    anywhere = pl.BlockSpec(memory_space=pl.ANY)
    block = jax.ShapeDtypeStruct((NG // GY, COLS), BF16)
    dma = pltpu.SemaphoreType.DMA
    return pl.pallas_call(
        step_kernel,
        out_shape=(block,) * 4,
        in_specs=[anywhere] * 6,
        out_specs=(anywhere,) * 4,
        scratch_shapes=[
            pltpu.VMEM((MATRIX_ROWS, 256), BF16),
            pltpu.VMEM((FLOAT_ROWS, 128), F32),
            pltpu.VMEM((FIELDS, GX, ROWS, COLS), BF16),
            pltpu.VMEM((GY, 128, 256), BF16),
            pltpu.VMEM((GY, 128, 256), BF16),
            pltpu.VMEM((DEVICES, SLAB // 8, 8, 128), BF16),
            pltpu.VMEM((DEVICES, SLAB // 8, 8, 128), BF16),
            pltpu.VMEM((SLAB * 128, 128), F32),
            pltpu.VMEM((KX + 1, 4, 128, 128), F32),
            pltpu.VMEM((DEVICES, SLAB // 8, 8, 128), BF16),
            pltpu.VMEM((GY, 128, 256), F32),
            pltpu.VMEM((FIELDS, GX, ROWS, COLS), BF16),
            dma((2,)),
            dma((FIELDS,)),
            dma((FIELDS,)),
            dma,
            dma((GY,)),
            dma,
            dma((GY,)),
            dma((FIELDS,)),
            dma((FIELDS,)),
            pltpu.SemaphoreType.REGULAR,
            pltpu.SemaphoreType.REGULAR,
        ],
        compiler_params=pltpu.CompilerParams(collective_id=0, has_side_effects=True),
    )(east_wind, north_wind, height, tracer, *constants)


def solution(mesh):
    placed = (P("gy", "gx"),) * 4
    return jax.shard_map(
        per_device, mesh=mesh, in_specs=placed, out_specs=placed, check_vma=False
    )
```

```python
import math

import jax
import jax.numpy as jnp
import numpy as np
from jax import lax
from jax.experimental import pallas as pl
from jax.experimental.pallas import tpu as pltpu
from jax.sharding import PartitionSpec as P

NG = 4096
FIELDS = 4
GX = 8
GY = 16
DEVICES = GX * GY
KX = 11
SLAB = 24
ROWS = 32
COLS = 512
POWER = 11
UNROLL = 2

coriolis = 0.25
gravity_step = 2.0
depth_step = 2.0
diffusion = 0.02

F32 = jnp.float32
BF16 = jnp.bfloat16
MESH = pl.DeviceIdType.MESH


def split_const(matrix):
    whole = matrix.astype(np.float32)
    high = np.dtype(jnp.bfloat16)
    head = whole.astype(high)
    tail = (whole - head.astype(np.float32)).astype(high)
    return head, tail


def wave_of(slot, place):
    if slot == 0:
        return 32 * place if place < 43 else 16 + 32 * (place - 43)
    return slot + 32 * (place - 43)


def tables():
    turn = 2.0 * np.pi
    lane = np.arange(128)
    forward = np.zeros((2, GX, 2, SLAB // 2, 256))
    inverse = np.zeros((2, GX, 2, SLAB // 2, 256))
    for place in range(86):
        octant, member = place // KX, place % KX
        low = place - 43
        cosine, sine = np.cos(turn * lane * low / 128), np.sin(turn * lane * low / 128)
        forward[1, octant, 0, member] = np.concatenate([cosine, sine])
        forward[1, octant, 1, member] = np.concatenate([-sine, cosine])
        inverse[1, octant, 0, member] = np.concatenate([cosine, sine])
        inverse[1, octant, 1, member] = np.concatenate([-sine, cosine])
        wave = wave_of(0, place)
        cosine, sine = np.cos(turn * lane * wave / NG), np.sin(turn * lane * wave / NG)
        half = 0 if place < 43 else 128
        weight = 1.0 if wave == 0 else 2.0
        forward[0, octant, 0, member, half : half + 128] = cosine
        forward[0, octant, 1, member, half : half + 128] = -sine
        inverse[0, octant, 0, member, half : half + 128] = weight * cosine
        inverse[0, octant, 1, member, half : half + 128] = -weight * sine
    forward = forward.reshape(2, GX * SLAB, 256)
    inverse = inverse.reshape(2, GX * SLAB, 256)
    angle = turn * np.outer(np.arange(GY), lane) / NG
    twist = np.stack([np.cos(angle), np.sin(angle)], axis=1)[:, :, None, :]
    twist = np.broadcast_to(twist, (GY, 2, 16, 128)).astype(np.float32)
    angle = turn * np.outer(lane, lane) / 128
    cosine, sine = np.cos(angle), np.sin(angle)
    gather = np.block([[cosine, sine], [-sine, cosine]])
    scatter = np.block([[cosine, -sine], [sine, cosine]])
    angle = turn * np.outer(np.arange(ROWS), np.arange(ROWS)) / ROWS
    cosine, sine = np.kron(np.eye(4), np.cos(angle)), np.kron(np.eye(4), np.sin(angle))
    fan_in = np.block([[cosine, -sine], [sine, cosine]])
    fan_out = np.block([[cosine, sine], [-sine, cosine]])
    angle = turn * np.outer(lane, lane % ROWS) / NG
    spin = np.stack([np.cos(angle), np.sin(angle)]).astype(np.float32)
    pieces = []
    for matrix in (forward.reshape(-1, 256), inverse.reshape(-1, 256) / NG, gather, scatter, fan_in, fan_out):
        pieces.extend(split_const(matrix))
    floats = np.concatenate([twist.reshape(-1, 128), spin.reshape(-1, 128)], axis=0)
    return np.concatenate(pieces, axis=0), floats


FWD_AT = 0
INV_AT = 4 * GX * SLAB
SQUARE_AT = 8 * GX * SLAB
MATRIX_ROWS = SQUARE_AT + 8 * 256
SPIN_AT = GY * 2 * 16
FLOAT_ROWS = SPIN_AT + 256


def matrix_pair(matrices, start, which):
    count = GX * SLAB
    first = pl.multiple_of(start + which * count, 64)
    second = pl.multiple_of(start + (which + 2) * count, 64)
    return matrices[pl.ds(first, count), :], matrices[pl.ds(second, count), :]


def square_pair(matrices, which):
    first = SQUARE_AT + which * 512
    return matrices[first : first + 256, :], matrices[first + 256 : first + 512, :]


def encode(values):
    largest = jnp.max(jnp.abs(values), axis=1, keepdims=True)
    scale = (jnp.maximum(largest, 1e-34) * 1.01).astype(BF16).astype(F32)
    level = values * (2048.0 / scale)
    second = level * level
    fourth = second * second
    eighth = fourth * fourth
    code = eighth * second * level
    row = lax.broadcasted_iota(jnp.int32, values.shape, 1)
    code = jnp.where(row == KX, scale, code)
    return code.reshape(values.shape[0], SLAB // 8, 8, 128).astype(BF16)


def decode(codes):
    code = codes.astype(F32).reshape(codes.shape[0], SLAB, 128)
    scale = code[:, KX : KX + 1, :] * (1.0 / 2048.0)
    level = jnp.exp2(jnp.log2(jnp.abs(code)) * (1.0 / POWER))
    level = jnp.where(code < 0.0, -level, level)
    return jnp.where(code == 0.0, 0.0, level) * scale


def real_transform(values):
    count = len(values)
    if count == 2:
        return [(values[0] + values[1], None), (values[0] - values[1], None)]
    even = real_transform(values[0::2])
    odd = real_transform(values[1::2])
    half = count // 2
    result = [None] * (half + 1)
    for index in range(count // 4 + 1):
        even_real, even_imag = even[index]
        odd_real, odd_imag = odd[index]
        if index == 0:
            result[0] = (even_real + odd_real, None)
            result[half] = (even_real - odd_real, None)
        elif index == count // 4:
            result[index] = (even_real, -odd_real)
        else:
            cosine = math.cos(2.0 * math.pi * index / count)
            sine = math.sin(2.0 * math.pi * index / count)
            turned_real = odd_real * cosine + odd_imag * sine
            turned_imag = odd_imag * cosine - odd_real * sine
            result[index] = (even_real + turned_real, even_imag + turned_imag)
            result[half - index] = (even_real - turned_real, turned_imag - even_imag)
    return result


def real_inverse(waves):
    half = len(waves) - 1
    count = 2 * half
    if count == 2:
        return [waves[0][0] + waves[1][0], waves[0][0] - waves[1][0]]
    even = []
    odd = []
    for index in range(count // 4 + 1):
        real, imag = waves[index]
        other_real, other_imag = waves[half - index]
        if index == 0:
            even.append((real + other_real, None))
            odd.append((real - other_real, None))
        elif index == count // 4:
            even.append((real + real, None))
            odd.append((-(imag + imag), None))
        else:
            cosine = math.cos(2.0 * math.pi * index / count)
            sine = math.sin(2.0 * math.pi * index / count)
            even.append((real + other_real, imag - other_imag))
            gap_real = real - other_real
            gap_imag = imag + other_imag
            odd.append((gap_real * cosine - gap_imag * sine, gap_real * sine + gap_imag * cosine))
    outputs = [None] * count
    outputs[0::2] = real_inverse(even)
    outputs[1::2] = real_inverse(odd)
    return outputs


def parts(values):
    head = values.astype(BF16)
    return head, (values - head.astype(F32)).astype(BF16)


def product(left, right, dims):
    return lax.dot_general(left, right, (dims, ((), ())), preferred_element_type=F32)


def product3(left, right, dims):
    left_head, left_tail = left
    right_head, right_tail = right
    left_all = jnp.concatenate([left_head, left_head, left_tail], axis=dims[0][0])
    right_all = jnp.concatenate([right_head, right_tail, right_head], axis=dims[1][0])
    return product(left_all, right_all, dims)


NN = ((1,), (0,))
NT = ((1,), (1,))
TN = ((0,), (0,))


def fill_gains(gains, octant, slot):
    chunk = 32

    def body(step, carry):
        member = step // (128 // chunk)
        top = (step % (128 // chunk)) * chunk
        place = KX * octant + member
        zero_slot = jnp.where(place < 43, 32 * place, 16 + 32 * (place - 43))
        mode_x = jnp.where(slot == 0, zero_slot, slot + 32 * (place - 43))
        lane = lax.broadcasted_iota(jnp.int32, (chunk, 128), 1)
        row = lax.broadcasted_iota(jnp.int32, (chunk, 128), 0) + top
        field = lane // 32
        mode_y = row + 128 * (lane % 32)
        mode_y = jnp.where(mode_y < NG // 2, mode_y, mode_y - NG)
        cutoff = NG // 3
        inside = mode_y * mode_y + mode_x * mode_x <= cutoff * cutoff
        unit = 2.0 * math.pi / NG
        wave_x = mode_x.astype(F32) * unit
        wave_y = mode_y.astype(F32) * unit
        square = wave_x * wave_x + wave_y * wave_y
        scale = 1.0 / NG
        gain = jnp.where(inside, scale / (1.0 + diffusion * square * square), 0.0)
        stiffness = gravity_step * depth_step * square
        below = 1.0 / (1.0 + coriolis * coriolis + stiffness)
        above = (1.0 - coriolis * coriolis - stiffness) * below
        twice = (2.0 * coriolis) * below
        push_u = above * wave_x - twice * wave_y
        push_v = above * wave_y + twice * wave_x
        push_h = (2.0 * gravity_step) * square * below
        sum_u = wave_x + push_u
        sum_v = wave_y + push_v
        curl_u = -wave_y - coriolis * sum_u
        curl_v = wave_x - coriolis * sum_v
        curl_h = -coriolis * push_h
        anchor = square == 0.0
        over = 1.0 / jnp.where(anchor, 1.0, square)
        first = field == 0
        second = field == 1
        third = field == 2
        lead = jnp.where(first, -wave_y, wave_x)
        trail = jnp.where(first, wave_x, wave_y)
        from_u = (lead * curl_u + trail * push_u) * over
        from_v = (lead * curl_v + trail * push_v) * over
        from_h = -(lead * curl_h + trail * push_h) * over
        rotate = 1.0 / (1.0 + coriolis * coriolis)
        keep = (1.0 - coriolis * coriolis) * rotate
        cross = 2.0 * coriolis * rotate
        from_u = jnp.where(anchor, jnp.where(first, keep, -cross), from_u)
        from_v = jnp.where(anchor, jnp.where(first, cross, keep), from_v)
        zero = jnp.zeros_like(gain)
        same = jnp.where(
            first,
            from_u,
            jnp.where(second, from_v, jnp.where(third, 1.0 - depth_step * push_h, 1.0)),
        )
        one = jnp.where(second, from_u, jnp.where(third, -depth_step * sum_v, zero))
        two = jnp.where(first, from_h, jnp.where(third, -depth_step * sum_u, zero))
        three = jnp.where(first, from_v, jnp.where(second, from_h, zero))
        place_rows = pl.ds(pl.multiple_of(top, chunk), chunk)
        gains[member, 0, place_rows, :] = same * gain
        gains[member, 1, place_rows, :] = one * gain
        gains[member, 2, place_rows, :] = two * gain
        gains[member, 3, place_rows, :] = three * gain
        return carry

    lax.fori_loop(0, KX * (128 // chunk), body, 0)
    gains[KX] = jnp.zeros((4, 128, 128), F32)


def apply_gains(gains, member, real, imag):
    lane = lax.broadcasted_iota(jnp.int32, (128, 128), 1)
    field = lane // 32
    second = field == 1
    third = field == 2
    gain = gains[member, 0]
    out_real = real * gain
    out_imag = imag * gain
    crossed = [third, None, second]
    for turn in (1, 2, 3):
        gain = gains[member, turn]
        moved_real = pltpu.roll(real, 32 * turn, 1)
        moved_imag = pltpu.roll(imag, 32 * turn, 1)
        swap = crossed[turn - 1]
        if swap is None:
            use_real, use_imag = -moved_imag, moved_real
        else:
            use_real = jnp.where(swap, -moved_imag, moved_real)
            use_imag = jnp.where(swap, moved_real, moved_imag)
        out_real = out_real + gain * use_real
        out_imag = out_imag + gain * use_imag
    return out_real, out_imag


def step_kernel(*refs):
    sources = refs[0:4]
    matrix_source, float_source = refs[4:6]
    results = refs[6:10]
    (
        matrices,
        floats,
        grid_rows,
        head,
        tail,
        slabs,
        landed,
        columns,
        gains,
        returned,
        waves,
        new_rows,
        sem_table,
        sem_rows_out,
        sem_rows_in,
        sem_out,
        sem_in,
        sem_back_out,
        sem_back_in,
        sem_last_out,
        sem_last_in,
        sem_leaders,
        sem_all,
    ) = refs[10:]
    octant = lax.axis_index("gx")
    slot_own = lax.axis_index("gy")
    own = slot_own * GX + octant
    octants = [(octant + step) % GX for step in range(GX)]

    def slot_at(step):
        return (slot_own + 9 * step) % GY

    def slot_before(step):
        return (slot_own + 16 * GY - 9 * step) % GY

    barrier = pltpu.get_barrier_semaphore()
    for step in range(1, GX):
        pl.semaphore_signal(
            barrier, inc=1, device_id=(octants[step], slot_own), device_id_type=MESH
        )

    @pl.when(octant == 0)
    def greet_leaders():
        for step in range(1, GY):
            pl.semaphore_signal(
                barrier, inc=1, device_id=(octant, slot_at(step)), device_id_type=MESH
            )

    table_copies = [
        pltpu.make_async_copy(matrix_source, matrices, sem_table.at[0]),
        pltpu.make_async_copy(float_source, floats, sem_table.at[1]),
    ]
    for copy in table_copies:
        copy.start()
    own_rows = pl.ds(pl.multiple_of(octant * ROWS, ROWS), ROWS)
    for field in range(FIELDS):
        pltpu.make_async_copy(
            sources[field].at[own_rows, :], grid_rows.at[field, octant], sem_rows_in.at[field]
        ).start()

    @pl.when(octant == 0)
    def wait_leader():
        pl.semaphore_wait(barrier, GX - 1 + GY - 1)

    @pl.when(octant != 0)
    def wait_member():
        pl.semaphore_wait(barrier, GX - 1)

    for field in range(FIELDS):
        for step in range(1, GX):
            other = octants[step]
            pltpu.make_async_remote_copy(
                src_ref=sources[field].at[pl.ds(pl.multiple_of(other * ROWS, ROWS), ROWS), :],
                dst_ref=grid_rows.at[field, octant],
                send_sem=sem_rows_out.at[field],
                recv_sem=sem_rows_in.at[field],
                device_id=(other, slot_own),
                device_id_type=MESH,
            ).start()

    @pl.when(octant == 0)
    def tell_leaders():
        for step in range(1, GY):
            pl.semaphore_signal(
                sem_leaders, inc=1, device_id=(octant, slot_at(step)), device_id_type=MESH
            )

    fill_gains(gains, octant, slot_own)

    @pl.when(octant == 0)
    def tell_members():
        pl.semaphore_wait(sem_leaders, GY - 1)
        for step in range(1, GX):
            pl.semaphore_signal(
                sem_all, inc=1, device_id=(octants[step], slot_own), device_id_type=MESH
            )

    for copy in table_copies:
        copy.wait()

    def row_body(step, carry):
        field = step // 2
        part = step % 2
        top = pl.multiple_of(part * 16, 16)
        chunk = [
            grid_rows[field, c // 4, pl.ds(top, 16), (c % 4) * 128 : (c % 4) * 128 + 128].astype(F32)
            for c in range(32)
        ]
        spectrum = real_transform(chunk)
        rows = pl.ds(pl.multiple_of(step * 16, 16), 16)
        for slot in range(GY):
            if slot == 0:
                real, imag = spectrum[0][0], spectrum[16][0]
            else:
                wave_real, wave_imag = spectrum[slot]
                cosine = floats[32 * slot : 32 * slot + 16, :]
                sine = floats[32 * slot + 16 : 32 * slot + 32, :]
                real = wave_real * cosine + wave_imag * sine
                imag = wave_imag * cosine - wave_real * sine
            for side, value in ((0, real), (128, imag)):
                high, low = parts(value)
                head[slot, rows, side : side + 128] = high
                tail[slot, rows, side : side + 128] = low
        return carry

    for field in range(FIELDS):
        pltpu.make_async_copy(
            grid_rows.at[field], grid_rows.at[field], sem_rows_in.at[field]
        ).wait()
        lax.fori_loop(2 * field, 2 * field + 2, row_body, 0)

    @pl.when(octant != 0)
    def wait_all():
        pl.semaphore_wait(sem_all, 1)

    def send(slot, other, target, out_sem, in_sem):
        pltpu.make_async_remote_copy(
            src_ref=slabs.at[slot * GX + other],
            dst_ref=target.at[own],
            send_sem=out_sem,
            recv_sem=in_sem.at[slot_own],
            device_id=(other, slot),
            device_id_type=MESH,
        ).start()

    def slot_products(slots):
        loaded = [
            (matrix_pair(matrices, FWD_AT, jnp.minimum(slot, 1)), (head[slot], tail[slot]))
            for slot in slots
        ]
        codes = [
            encode(product3(left, right, NT).reshape(GX, SLAB, 128)) for left, right in loaded
        ]
        for slot, code in zip(slots, codes):
            slabs[pl.ds(slot * GX, GX)] = code

    def slot_body(step, carry):
        slots = [slot_at(2 * step + 1), slot_at(2 * step + 2)]
        slot_products(slots)
        for slot in slots:
            for other in octants:
                send(slot, other, landed, sem_out, sem_in)
        return carry

    lax.fori_loop(0, GY // 2 - 1, slot_body, 0)
    far = slot_at(GY - 1)
    slot_products([far, slot_own])
    for other in octants:
        send(far, other, landed, sem_out, sem_in)
    for step in range(1, GX):
        send(slot_own, octants[step], landed, sem_out, sem_in)
    pltpu.make_async_copy(slabs.at[own], landed.at[own], sem_in.at[slot_own]).start()

    def spread(step, carry):
        slot = slot_before(step + 1)
        group = landed.at[pl.ds(slot * GX, GX)]
        pltpu.make_async_copy(group, group, sem_in.at[slot]).wait()
        values = decode(landed[pl.ds(slot * GX, GX)])
        for source in range(GX):
            columns[pl.ds(slot * GX + source, SLAB, stride=128), :] = values[source]
        return carry

    lax.fori_loop(0, GY, spread, 0)

    def row_pairs(pair):
        real_rows = pl.ds(pl.multiple_of(pair * 256, 256), 256)
        imag_rows = pl.ds(pl.multiple_of(pair * 256 + SLAB // 2 * 128, 256), 256)
        return real_rows, imag_rows

    def column_math(pair, real, imag):
        values = jnp.concatenate(
            [
                jnp.concatenate([real[:128], real[128:]], axis=1),
                jnp.concatenate([imag[:128], imag[128:]], axis=1),
            ],
            axis=0,
        )
        mixed = product3(square_pair(matrices, 0), parts(values), NN)
        cosine = floats[SPIN_AT : SPIN_AT + 128, :]
        sine = floats[SPIN_AT + 128 : SPIN_AT + 256, :]
        turned = []
        for side in (0, 128):
            real, imag = mixed[:128, side : side + 128], mixed[128:, side : side + 128]
            turned.append(
                jnp.concatenate([real * cosine + imag * sine, imag * cosine - real * sine], axis=1)
            )
        turned = jnp.concatenate(turned, axis=0)
        modes = product3(parts(turned), square_pair(matrices, 2), NN)
        changed = []
        for member in range(2):
            piece = modes[128 * member : 128 * member + 128]
            real, imag = apply_gains(gains, 2 * pair + member, piece[:, :128], piece[:, 128:])
            changed.append(jnp.concatenate([real, imag], axis=1))
        changed = jnp.concatenate(changed, axis=0)
        mixed = product3(parts(changed), square_pair(matrices, 3), NN)
        reals, imags = [], []
        for member in range(2):
            piece = mixed[128 * member : 128 * member + 128]
            real, imag = piece[:, :128], piece[:, 128:]
            reals.append(real * cosine - imag * sine)
            imags.append(imag * cosine + real * sine)
        values = jnp.concatenate(
            [jnp.concatenate(reals, axis=1), jnp.concatenate(imags, axis=1)], axis=0
        )
        values = product3(square_pair(matrices, 1), parts(values), NN)
        return (
            jnp.concatenate([values[:128, :128], values[:128, 128:]], axis=0),
            jnp.concatenate([values[128:, :128], values[128:, 128:]], axis=0),
        )

    def column_body(step, carry):
        pairs = [UNROLL * step + index for index in range(UNROLL)]
        loaded = [[columns[rows, :] for rows in row_pairs(pair)] for pair in pairs]
        done = [column_math(pair, *values) for pair, values in zip(pairs, loaded)]
        for pair, values in zip(pairs, done):
            for rows, value in zip(row_pairs(pair), values):
                columns[rows, :] = value
        return carry

    lax.fori_loop(0, (KX + 1) // 2 // UNROLL, column_body, 0)

    sent = slabs.at[pl.ds(0, DEVICES - 1)]
    pltpu.make_async_copy(sent, sent, sem_out).wait()

    def collect(slot):
        first = slot * GX
        values = jnp.stack(
            [columns[pl.ds(first + source, SLAB, stride=128), :] for source in range(GX)]
        )
        slabs[pl.ds(first, GX)] = encode(values)

    collect(slot_own)
    for step in range(1, GX):
        send(slot_own, octants[step], returned, sem_back_out, sem_back_in)
    pltpu.make_async_copy(slabs.at[own], returned.at[own], sem_back_in.at[slot_own]).start()

    def back_body(step, carry):
        slot = slot_at(step)
        collect(slot)
        for other in octants:
            send(slot, other, returned, sem_back_out, sem_back_in)
        return carry

    lax.fori_loop(1, GY, back_body, 0)

    def wave_body(step, carry):
        slot = slot_before(step)
        group = returned.at[pl.ds(slot * GX, GX)]
        pltpu.make_async_copy(group, group, sem_back_in.at[slot]).wait()
        which = jnp.minimum(slot, 1)
        block = decode(returned[pl.ds(slot * GX, GX)]).reshape(GX * SLAB, 128)
        values = product3(parts(block), matrix_pair(matrices, INV_AT, which), TN)
        real, imag = values[:, :128], values[:, 128:]
        cosine = floats[pl.ds(32 * slot, 1), :]
        sine = floats[pl.ds(32 * slot + 16, 1), :]
        waves[slot, :, 0:128] = real * cosine - imag * sine
        waves[slot, :, 128:256] = imag * cosine + real * sine
        return carry

    lax.fori_loop(0, GY, wave_body, 0)

    def grid_body(step, carry):
        field = step // 2
        part = step % 2
        rows = pl.ds(pl.multiple_of(step * 16, 16), 16)
        spectrum = [(waves[0, rows, 0:128], None)]
        for slot in range(1, GY):
            spectrum.append((waves[slot, rows, 0:128], waves[slot, rows, 128:256]))
        spectrum.append((waves[0, rows, 128:256], None))
        values = real_inverse(spectrum)
        top = pl.ds(pl.multiple_of(part * 16, 16), 16)
        for c in range(32):
            new_rows[field, c // 4, top, (c % 4) * 128 : (c % 4) * 128 + 128] = values[c].astype(BF16)
        return carry

    for field in range(FIELDS):
        lax.fori_loop(2 * field, 2 * field + 2, grid_body, 0)
        for step in range(1, GX):
            other = octants[step]
            pltpu.make_async_remote_copy(
                src_ref=new_rows.at[field, other],
                dst_ref=results[field].at[own_rows, :],
                send_sem=sem_last_out.at[field],
                recv_sem=sem_last_in.at[field],
                device_id=(other, slot_own),
                device_id_type=MESH,
            ).start()
        pltpu.make_async_copy(
            new_rows.at[field, octant], results[field].at[own_rows, :], sem_last_in.at[field]
        ).start()

    pltpu.make_async_copy(sent, sent, sem_back_out).wait()
    for field in range(FIELDS):
        moved = new_rows.at[field, pl.ds(0, GX - 1)]
        pltpu.make_async_copy(moved, moved, sem_rows_out.at[field]).wait()
        pltpu.make_async_copy(moved, moved, sem_last_out.at[field]).wait()
        pltpu.make_async_copy(results[field], results[field], sem_last_in.at[field]).wait()


def place_kernel(*refs):
    copies = [
        pltpu.make_async_copy(refs[field], refs[FIELDS + field], refs[2 * FIELDS].at[field])
        for field in range(FIELDS)
    ]
    for copy in copies:
        copy.start()
    for copy in copies:
        copy.wait()


def per_device(east_wind, north_wind, height, tracer):
    constants = [jnp.asarray(value) for value in tables()]
    anywhere = pl.BlockSpec(memory_space=pl.ANY)
    block = jax.ShapeDtypeStruct((NG // GY, COLS), BF16)
    dma = pltpu.SemaphoreType.DMA
    landed = pl.pallas_call(
        step_kernel,
        out_shape=(block,) * 4,
        in_specs=[pl.BlockSpec(memory_space=pltpu.HBM)] * 6,
        out_specs=(anywhere,) * 4,
        scratch_shapes=[
            pltpu.VMEM((MATRIX_ROWS, 256), BF16),
            pltpu.VMEM((FLOAT_ROWS, 128), F32),
            pltpu.VMEM((FIELDS, GX, ROWS, COLS), BF16),
            pltpu.VMEM((GY, 128, 256), BF16),
            pltpu.VMEM((GY, 128, 256), BF16),
            pltpu.VMEM((DEVICES, SLAB // 8, 8, 128), BF16),
            pltpu.VMEM((DEVICES, SLAB // 8, 8, 128), BF16),
            pltpu.VMEM((SLAB * 128, 128), F32),
            pltpu.VMEM((KX + 1, 4, 128, 128), F32),
            pltpu.VMEM((DEVICES, SLAB // 8, 8, 128), BF16),
            pltpu.VMEM((GY, 128, 256), F32),
            pltpu.VMEM((FIELDS, GX, ROWS, COLS), BF16),
            dma((2,)),
            dma((FIELDS,)),
            dma((FIELDS,)),
            dma,
            dma((GY,)),
            dma,
            dma((GY,)),
            dma((FIELDS,)),
            dma((FIELDS,)),
            pltpu.SemaphoreType.REGULAR,
            pltpu.SemaphoreType.REGULAR,
        ],
        compiler_params=pltpu.CompilerParams(
            collective_id=0, has_side_effects=True, vmem_limit_bytes=32 * 1024 * 1024
        ),
    )(*[
        pltpu.with_memory_space_constraint(value, pltpu.HBM)
        for value in (east_wind, north_wind, height, tracer, *constants)
    ])
    return pl.pallas_call(
        place_kernel,
        out_shape=(block,) * 4,
        in_specs=[anywhere] * 4,
        out_specs=(pl.BlockSpec(memory_space=pltpu.HBM),) * 4,
        scratch_shapes=[dma((FIELDS,))],
        compiler_params=pltpu.CompilerParams(vmem_limit_bytes=1024 * 1024),
    )(*landed)


def solution(mesh):
    placed = (P("gy", "gx"),) * 4
    return jax.shard_map(
        per_device, mesh=mesh, in_specs=placed, out_specs=placed, check_vma=False
    )
```

```python
import math

import jax
import jax.numpy as jnp
import numpy as np
from jax import lax
from jax.experimental import pallas as pl
from jax.experimental.pallas import tpu as pltpu
from jax.sharding import PartitionSpec as P

NG = 4096
FIELDS = 4
GX = 8
GY = 16
DEVICES = GX * GY
KX = 11
SLAB = 24
FIRST = 16
PLANE = 136
REAL_ROWS = (0, 1, 2, 3, 4, 5, 6, 7, 17, 18, 19)
IMAG_ROWS = (8, 9, 10, 11, 12, 13, 14, 16, 20, 21, 22)
ROWS = 32
COLS = 512
POWER = 11

coriolis = 0.25
gravity_step = 2.0
depth_step = 2.0
diffusion = 0.02

F32 = jnp.float32
BF16 = jnp.bfloat16
MESH = pl.DeviceIdType.MESH


def split_const(matrix):
    whole = matrix.astype(np.float32)
    high = np.dtype(jnp.bfloat16)
    head = whole.astype(high)
    tail = (whole - head.astype(np.float32)).astype(high)
    return head, tail


def wave_of(slot, place):
    if slot == 0:
        return 32 * place if place < 43 else 16 + 32 * (place - 43)
    return slot + 32 * (place - 43)


def tables():
    turn = 2.0 * np.pi
    lane = np.arange(128)
    forward = np.zeros((2, GX, SLAB, 256))
    inverse = np.zeros((2, GX, SLAB, 256))
    for place in range(86):
        octant, member = place // KX, place % KX
        real_row, imag_row = REAL_ROWS[member], IMAG_ROWS[member]
        low = place - 43
        cosine, sine = np.cos(turn * lane * low / 128), np.sin(turn * lane * low / 128)
        forward[1, octant, real_row] = np.concatenate([cosine, sine])
        forward[1, octant, imag_row] = np.concatenate([-sine, cosine])
        inverse[1, octant, real_row] = np.concatenate([cosine, sine])
        inverse[1, octant, imag_row] = np.concatenate([-sine, cosine])
        wave = wave_of(0, place)
        cosine, sine = np.cos(turn * lane * wave / NG), np.sin(turn * lane * wave / NG)
        half = 0 if place < 43 else 128
        weight = 1.0 if wave == 0 else 2.0
        forward[0, octant, real_row, half : half + 128] = cosine
        forward[0, octant, imag_row, half : half + 128] = -sine
        inverse[0, octant, real_row, half : half + 128] = weight * cosine
        inverse[0, octant, imag_row, half : half + 128] = -weight * sine
    forward = forward.reshape(2, GX * SLAB, 256)
    inverse = inverse.reshape(2, GX * SLAB, 256)
    angle = turn * np.outer(np.arange(GY), lane) / NG
    twist = np.stack([np.cos(angle), np.sin(angle)], axis=1)[:, :, None, :]
    twist = np.broadcast_to(twist, (GY, 2, 16, 128)).astype(np.float32)
    angle = turn * np.outer(lane, lane) / 128
    cosine, sine = np.cos(angle), np.sin(angle)
    gather = np.block([[cosine, sine], [-sine, cosine]])
    scatter = np.block([[cosine, -sine], [sine, cosine]])
    angle = turn * np.outer(np.arange(ROWS), np.arange(ROWS)) / ROWS
    cosine, sine = np.kron(np.eye(4), np.cos(angle)), np.kron(np.eye(4), np.sin(angle))
    fan_in = np.block([[cosine, -sine], [sine, cosine]])
    fan_out = np.block([[cosine, sine], [-sine, cosine]])
    angle = turn * np.outer(lane, lane % ROWS) / NG
    spin = np.stack([np.cos(angle), np.sin(angle)]).astype(np.float32)
    pieces = []
    for matrix in (forward.reshape(-1, 256), inverse.reshape(-1, 256) / NG, gather, scatter, fan_in, fan_out):
        pieces.extend(split_const(matrix))
    floats = np.concatenate([twist.reshape(-1, 128), spin.reshape(-1, 128)], axis=0)
    return np.concatenate(pieces, axis=0), floats


FWD_AT = 0
INV_AT = 4 * GX * SLAB
SQUARE_AT = 8 * GX * SLAB
MATRIX_ROWS = SQUARE_AT + 8 * 256
SPIN_AT = GY * 2 * 16
FLOAT_ROWS = SPIN_AT + 256


def matrix_pair(matrices, start, which):
    count = GX * SLAB
    first = pl.multiple_of(start + which * count, 64)
    second = pl.multiple_of(start + (which + 2) * count, 64)
    return matrices[pl.ds(first, count), :], matrices[pl.ds(second, count), :]


def square_pair(matrices, which):
    first = SQUARE_AT + which * 512
    return matrices[first : first + 256, :], matrices[first + 256 : first + 512, :]


def encode(values):
    rows = values.shape[1]
    last = lax.broadcasted_iota(jnp.int32, values.shape, 1) == rows - 1
    values = jnp.where(last, 0.0, values)
    largest = jnp.max(jnp.abs(values), axis=1, keepdims=True)
    scale = (jnp.maximum(largest, 1e-34) * 1.01).astype(BF16).astype(F32)
    level = values * (2048.0 / scale)
    second = level * level
    fourth = second * second
    eighth = fourth * fourth
    code = jnp.where(last, scale, eighth * second * level)
    return code.reshape(values.shape[0], rows // 8, 8, 128).astype(BF16)


def decode(codes):
    rows = codes.shape[1] * 8
    code = codes.astype(F32).reshape(codes.shape[0], rows, 128)
    scale = code[:, rows - 1 : rows, :] * (1.0 / 2048.0)
    level = jnp.exp2(jnp.log2(jnp.abs(code)) * (1.0 / POWER))
    level = jnp.where(code < 0.0, -level, level)
    return jnp.where(code == 0.0, 0.0, level) * scale


def real_transform(values):
    count = len(values)
    if count == 2:
        return [(values[0] + values[1], None), (values[0] - values[1], None)]
    even = real_transform(values[0::2])
    odd = real_transform(values[1::2])
    half = count // 2
    result = [None] * (half + 1)
    for index in range(count // 4 + 1):
        even_real, even_imag = even[index]
        odd_real, odd_imag = odd[index]
        if index == 0:
            result[0] = (even_real + odd_real, None)
            result[half] = (even_real - odd_real, None)
        elif index == count // 4:
            result[index] = (even_real, -odd_real)
        else:
            cosine = math.cos(2.0 * math.pi * index / count)
            sine = math.sin(2.0 * math.pi * index / count)
            turned_real = odd_real * cosine + odd_imag * sine
            turned_imag = odd_imag * cosine - odd_real * sine
            result[index] = (even_real + turned_real, even_imag + turned_imag)
            result[half - index] = (even_real - turned_real, turned_imag - even_imag)
    return result


def real_inverse(waves):
    half = len(waves) - 1
    count = 2 * half
    if count == 2:
        return [waves[0][0] + waves[1][0], waves[0][0] - waves[1][0]]
    even = []
    odd = []
    for index in range(count // 4 + 1):
        real, imag = waves[index]
        other_real, other_imag = waves[half - index]
        if index == 0:
            even.append((real + other_real, None))
            odd.append((real - other_real, None))
        elif index == count // 4:
            even.append((real + real, None))
            odd.append((-(imag + imag), None))
        else:
            cosine = math.cos(2.0 * math.pi * index / count)
            sine = math.sin(2.0 * math.pi * index / count)
            even.append((real + other_real, imag - other_imag))
            gap_real = real - other_real
            gap_imag = imag + other_imag
            odd.append((gap_real * cosine - gap_imag * sine, gap_real * sine + gap_imag * cosine))
    outputs = [None] * count
    outputs[0::2] = real_inverse(even)
    outputs[1::2] = real_inverse(odd)
    return outputs


def parts(values):
    head = values.astype(BF16)
    return head, (values - head.astype(F32)).astype(BF16)


def product(left, right, dims):
    return lax.dot_general(left, right, (dims, ((), ())), preferred_element_type=F32)


def product3(left, right, dims):
    left_head, left_tail = left
    right_head, right_tail = right
    left_all = jnp.concatenate([left_head, left_head, left_tail], axis=dims[0][0])
    right_all = jnp.concatenate([right_head, right_tail, right_head], axis=dims[1][0])
    return product(left_all, right_all, dims)


NN = ((1,), (0,))
NT = ((1,), (1,))
TN = ((0,), (0,))


def fill_gains(gains, octant, slot):
    chunk = 32

    def body(step, carry):
        member = step // (128 // chunk)
        top = (step % (128 // chunk)) * chunk
        place = KX * octant + member
        zero_slot = jnp.where(place < 43, 32 * place, 16 + 32 * (place - 43))
        mode_x = jnp.where(slot == 0, zero_slot, slot + 32 * (place - 43))
        lane = lax.broadcasted_iota(jnp.int32, (chunk, 128), 1)
        row = lax.broadcasted_iota(jnp.int32, (chunk, 128), 0) + top
        field = lane // 32
        mode_y = row + 128 * (lane % 32)
        mode_y = jnp.where(mode_y < NG // 2, mode_y, mode_y - NG)
        cutoff = NG // 3
        inside = mode_y * mode_y + mode_x * mode_x <= cutoff * cutoff
        unit = 2.0 * math.pi / NG
        wave_x = mode_x.astype(F32) * unit
        wave_y = mode_y.astype(F32) * unit
        square = wave_x * wave_x + wave_y * wave_y
        scale = 1.0 / NG
        gain = jnp.where(inside, scale / (1.0 + diffusion * square * square), 0.0)
        stiffness = gravity_step * depth_step * square
        below = 1.0 / (1.0 + coriolis * coriolis + stiffness)
        above = (1.0 - coriolis * coriolis - stiffness) * below
        twice = (2.0 * coriolis) * below
        push_u = above * wave_x - twice * wave_y
        push_v = above * wave_y + twice * wave_x
        push_h = (2.0 * gravity_step) * square * below
        sum_u = wave_x + push_u
        sum_v = wave_y + push_v
        curl_u = -wave_y - coriolis * sum_u
        curl_v = wave_x - coriolis * sum_v
        curl_h = -coriolis * push_h
        anchor = square == 0.0
        over = 1.0 / jnp.where(anchor, 1.0, square)
        first = field == 0
        second = field == 1
        third = field == 2
        lead = jnp.where(first, -wave_y, wave_x)
        trail = jnp.where(first, wave_x, wave_y)
        from_u = (lead * curl_u + trail * push_u) * over
        from_v = (lead * curl_v + trail * push_v) * over
        from_h = -(lead * curl_h + trail * push_h) * over
        rotate = 1.0 / (1.0 + coriolis * coriolis)
        keep = (1.0 - coriolis * coriolis) * rotate
        cross = 2.0 * coriolis * rotate
        from_u = jnp.where(anchor, jnp.where(first, keep, -cross), from_u)
        from_v = jnp.where(anchor, jnp.where(first, cross, keep), from_v)
        zero = jnp.zeros_like(gain)
        same = jnp.where(
            first,
            from_u,
            jnp.where(second, from_v, jnp.where(third, 1.0 - depth_step * push_h, 1.0)),
        )
        one = jnp.where(second, from_u, jnp.where(third, -depth_step * sum_v, zero))
        two = jnp.where(first, from_h, jnp.where(third, -depth_step * sum_u, zero))
        three = jnp.where(first, from_v, jnp.where(second, from_h, zero))
        place_rows = pl.ds(pl.multiple_of(top, chunk), chunk)
        gains[member, 0, place_rows, :] = same * gain
        gains[member, 1, place_rows, :] = one * gain
        gains[member, 2, place_rows, :] = two * gain
        gains[member, 3, place_rows, :] = three * gain
        return carry

    lax.fori_loop(0, KX * (128 // chunk), body, 0)


def apply_gains(gains, member, real, imag):
    lane = lax.broadcasted_iota(jnp.int32, (128, 128), 1)
    field = lane // 32
    second = field == 1
    third = field == 2
    gain = gains[member, 0]
    out_real = real * gain
    out_imag = imag * gain
    crossed = [third, None, second]
    for turn in (1, 2, 3):
        gain = gains[member, turn]
        moved_real = pltpu.roll(real, 32 * turn, 1)
        moved_imag = pltpu.roll(imag, 32 * turn, 1)
        swap = crossed[turn - 1]
        if swap is None:
            use_real, use_imag = -moved_imag, moved_real
        else:
            use_real = jnp.where(swap, -moved_imag, moved_real)
            use_imag = jnp.where(swap, moved_real, moved_imag)
        out_real = out_real + gain * use_real
        out_imag = out_imag + gain * use_imag
    return out_real, out_imag


def step_kernel(*refs):
    sources = refs[0:4]
    matrix_source, float_source = refs[4:6]
    results = refs[6:10]
    (
        matrices,
        floats,
        grid_rows,
        head,
        tail,
        slabs,
        landed,
        columns,
        gains,
        returned,
        waves,
        new_rows,
        sem_table,
        sem_rows_out,
        sem_rows_in,
        sem_out,
        sem_in,
        sem_back_out,
        sem_back_in,
        sem_last_out,
        sem_last_in,
        sem_leaders,
        sem_all,
    ) = refs[10:]
    octant = lax.axis_index("gx")
    slot_own = lax.axis_index("gy")
    own = slot_own * GX + octant
    octants = [
        4 * ((octant // 4 + across) % 2) + (octant % 4 + along) % 4
        for across, along in ((1, 2), (1, 1), (1, 3), (0, 2), (1, 0), (0, 1), (0, 3), (0, 0))
    ]
    half_own = slot_own // 8
    level_own = (slot_own // 2) % 4
    core_own = slot_own % 2

    def distance(step):
        turn = step % 4
        level = jnp.where(turn == 3, 0, jnp.where(turn == 2, 3, 2 - turn))
        return 1 - step // 4, level

    def slots_at(step):
        half, level = distance(step)
        base = 8 * ((half_own + half) % 2) + 2 * ((level_own + level) % 4)
        return [base + 1 - core_own, base + core_own]

    def slots_before(step):
        half, level = distance(GY // 2 - 1 - step)
        base = 8 * ((half_own + half) % 2) + 2 * ((level_own + 4 - level) % 4)
        return [base + 1 - core_own, base + core_own]

    barrier = pltpu.get_barrier_semaphore()
    for other in octants[:-1]:
        pl.semaphore_signal(
            barrier, inc=1, device_id=(other, slot_own), device_id_type=MESH
        )

    @pl.when(octant == 0)
    def greet_leaders():
        for step in range(1, GY):
            pl.semaphore_signal(
                barrier, inc=1, device_id=(octant, (slot_own + step) % GY), device_id_type=MESH
            )

    table_copies = [
        pltpu.make_async_copy(matrix_source, matrices, sem_table.at[0]),
        pltpu.make_async_copy(float_source, floats, sem_table.at[1]),
    ]
    for copy in table_copies:
        copy.start()
    own_rows = pl.ds(pl.multiple_of(octant * ROWS, ROWS), ROWS)
    for field in range(FIELDS):
        pltpu.make_async_copy(
            sources[field].at[own_rows, :], grid_rows.at[field, octant], sem_rows_in.at[field]
        ).start()

    @pl.when(octant == 0)
    def wait_leader():
        pl.semaphore_wait(barrier, GX - 1 + GY - 1)

    @pl.when(octant != 0)
    def wait_member():
        pl.semaphore_wait(barrier, GX - 1)

    for field in range(FIELDS):
        for other in octants[:-1]:
            pltpu.make_async_remote_copy(
                src_ref=sources[field].at[pl.ds(pl.multiple_of(other * ROWS, ROWS), ROWS), :],
                dst_ref=grid_rows.at[field, octant],
                send_sem=sem_rows_out.at[field],
                recv_sem=sem_rows_in.at[field],
                device_id=(other, slot_own),
                device_id_type=MESH,
            ).start()

    @pl.when(octant == 0)
    def tell_leaders():
        for step in range(1, GY):
            pl.semaphore_signal(
                sem_leaders, inc=1, device_id=(octant, (slot_own + step) % GY), device_id_type=MESH
            )

    fill_gains(gains, octant, slot_own)

    @pl.when(octant == 0)
    def tell_members():
        pl.semaphore_wait(sem_leaders, GY - 1)
        for other in octants[:-1]:
            pl.semaphore_signal(
                sem_all, inc=1, device_id=(other, slot_own), device_id_type=MESH
            )

    for copy in table_copies:
        copy.wait()

    def row_body(step, carry):
        field = step // 2
        part = step % 2
        top = pl.multiple_of(part * 16, 16)
        chunk = [
            grid_rows[field, c // 4, pl.ds(top, 16), (c % 4) * 128 : (c % 4) * 128 + 128].astype(F32)
            for c in range(32)
        ]
        spectrum = real_transform(chunk)
        rows = pl.ds(pl.multiple_of(step * 16, 16), 16)
        for slot in range(GY):
            if slot == 0:
                real, imag = spectrum[0][0], spectrum[16][0]
            else:
                wave_real, wave_imag = spectrum[slot]
                cosine = floats[32 * slot : 32 * slot + 16, :]
                sine = floats[32 * slot + 16 : 32 * slot + 32, :]
                real = wave_real * cosine + wave_imag * sine
                imag = wave_imag * cosine - wave_real * sine
            for side, value in ((0, real), (128, imag)):
                high, low = parts(value)
                head[slot, rows, side : side + 128] = high
                tail[slot, rows, side : side + 128] = low
        return carry

    for field in range(FIELDS):
        pltpu.make_async_copy(
            grid_rows.at[field], grid_rows.at[field], sem_rows_in.at[field]
        ).wait()
        lax.fori_loop(2 * field, 2 * field + 2, row_body, 0)

    @pl.when(octant != 0)
    def wait_all():
        pl.semaphore_wait(sem_all, 1)

    sides = (pl.ds(0, FIRST // 8), pl.ds(FIRST // 8, (SLAB - FIRST) // 8))

    def send_slot(side, slot, others, target, out_sem, in_sem):
        for other in others:
            pltpu.make_async_remote_copy(
                src_ref=slabs.at[slot * GX + other, sides[side]],
                dst_ref=target.at[own, sides[side]],
                send_sem=out_sem.at[side],
                recv_sem=in_sem.at[side, slot_own],
                device_id=(other, slot),
                device_id_type=MESH,
            ).start()

    def keep_own(side, target, in_sem):
        pltpu.make_async_copy(
            slabs.at[own, sides[side]], target.at[own, sides[side]], in_sem.at[side, slot_own]
        ).start()

    def wait_group(side, slot, target, in_sem):
        group = target.at[pl.ds(slot * GX, GX), sides[side]]
        pltpu.make_async_copy(group, group, in_sem.at[side, slot]).wait()

    def wait_sent(side, out_sem):
        sent = slabs.at[pl.ds(0, DEVICES - 1), sides[side]]
        pltpu.make_async_copy(sent, sent, out_sem.at[side]).wait()

    def slot_products(slots):
        loaded = [
            (matrix_pair(matrices, FWD_AT, jnp.minimum(slot, 1)), (head[slot], tail[slot]))
            for slot in slots
        ]
        codes = []
        for left, right in loaded:
            spectrum = product3(left, right, NT).reshape(GX, SLAB, 128)
            codes.append([encode(spectrum[:, :FIRST]), encode(spectrum[:, FIRST:])])
        for slot, pieces in zip(slots, codes):
            for side in range(2):
                slabs[pl.ds(slot * GX, GX), sides[side]] = pieces[side]

    steps = GY // 2

    def slot_body(step, carry):
        slots = slots_at(step)
        slot_products(slots)
        for slot in slots:
            send_slot(0, slot, octants, landed, sem_out, sem_in)
        return carry

    lax.fori_loop(0, steps - 1, slot_body, 0)
    twin = slots_at(steps - 1)[0]
    slot_products([twin, slot_own])
    send_slot(0, twin, octants, landed, sem_out, sem_in)
    send_slot(0, slot_own, octants[:-1], landed, sem_out, sem_in)
    keep_own(0, landed, sem_in)

    def second_body(step, carry):
        for slot in slots_at(step):
            send_slot(1, slot, octants, landed, sem_out, sem_in)
        return carry

    lax.fori_loop(0, steps - 1, second_body, 0)
    send_slot(1, twin, octants, landed, sem_out, sem_in)
    send_slot(1, slot_own, octants[:-1], landed, sem_out, sem_in)
    keep_own(1, landed, sem_in)

    def spread(side):
        first = 0 if side == 0 else FIRST
        count = FIRST if side == 0 else SLAB - FIRST

        def body(step, carry):
            for slot in slots_before(step):
                wait_group(side, slot, landed, sem_in)
                values = decode(landed[pl.ds(slot * GX, GX), sides[side]])
                for source in range(GX):
                    columns[
                        pl.ds(first * PLANE + slot * GX + source, count, stride=PLANE), :
                    ] = values[source]
            return carry

        return body

    def plane(row):
        return slice(row * 128, row * 128 + 128)

    def column_rows(row):
        return slice(row * PLANE, row * PLANE + 128)

    def column_math(members, reals, imags):
        values = jnp.concatenate(
            [jnp.concatenate(reals, axis=1), jnp.concatenate(imags, axis=1)], axis=0
        )
        mixed = product3(square_pair(matrices, 0), parts(values), NN)
        cosine = floats[SPIN_AT : SPIN_AT + 128, :]
        sine = floats[SPIN_AT + 128 : SPIN_AT + 256, :]
        turned = []
        for index in range(len(members)):
            real, imag = mixed[:128, plane(index)], mixed[128:, plane(index)]
            turned.append(
                jnp.concatenate([real * cosine + imag * sine, imag * cosine - real * sine], axis=1)
            )
        turned = jnp.concatenate(turned, axis=0)
        modes = product3(parts(turned), square_pair(matrices, 2), NN)
        changed = []
        for index, member in enumerate(members):
            piece = modes[plane(index)]
            real, imag = apply_gains(gains, member, piece[:, :128], piece[:, 128:])
            changed.append(jnp.concatenate([real, imag], axis=1))
        changed = jnp.concatenate(changed, axis=0)
        mixed = product3(parts(changed), square_pair(matrices, 3), NN)
        reals, imags = [], []
        for index in range(len(members)):
            piece = mixed[plane(index)]
            real, imag = piece[:, :128], piece[:, 128:]
            reals.append(real * cosine - imag * sine)
            imags.append(imag * cosine + real * sine)
        values = jnp.concatenate(
            [jnp.concatenate(reals, axis=1), jnp.concatenate(imags, axis=1)], axis=0
        )
        values = product3(square_pair(matrices, 1), parts(values), NN)
        return [
            (values[:128, plane(index)], values[128:, plane(index)])
            for index in range(len(members))
        ]

    def work_columns(groups):
        loaded = [
            [
                [columns[column_rows(rows[member]), :] for member in group]
                for rows in (REAL_ROWS, IMAG_ROWS)
            ]
            for group in groups
        ]
        done = [column_math(group, *values) for group, values in zip(groups, loaded)]
        for group, results_of in zip(groups, done):
            for member, (real, imag) in zip(group, results_of):
                columns[column_rows(REAL_ROWS[member]), :] = real
                columns[column_rows(IMAG_ROWS[member]), :] = imag

    def collect(side, slot):
        first = 0 if side == 0 else FIRST
        count = FIRST if side == 0 else SLAB - FIRST
        values = jnp.stack(
            [
                columns[pl.ds(first * PLANE + slot * GX + source, count, stride=PLANE), :]
                for source in range(GX)
            ]
        )
        slabs[pl.ds(slot * GX, GX), sides[side]] = encode(values)

    def send_back(side):
        def body(step, carry):
            slots = slots_at(step)
            for slot in slots:
                collect(side, slot)
                send_slot(side, slot, octants, returned, sem_back_out, sem_back_in)
            return carry

        wait_sent(side, sem_out)
        lax.fori_loop(0, steps - 1, body, 0)
        collect(side, twin)
        send_slot(side, twin, octants, returned, sem_back_out, sem_back_in)
        collect(side, slot_own)
        send_slot(side, slot_own, octants[:-1], returned, sem_back_out, sem_back_in)
        keep_own(side, returned, sem_back_in)

    lax.fori_loop(0, steps, spread(0), 0)
    work_columns([(0, 1), (2, 3), (4, 5)])
    lax.fori_loop(0, steps, spread(1), 0)
    work_columns([(6, 7)])
    send_back(0)
    work_columns([(8, 9), (10,)])
    send_back(1)

    def wave_body(step, carry):
        slots = slots_before(step)
        for side in range(2):
            for slot in slots:
                wait_group(side, slot, returned, sem_back_in)
        loaded = [
            (
                [returned[pl.ds(slot * GX, GX), sides[side]] for side in range(2)],
                matrix_pair(matrices, INV_AT, jnp.minimum(slot, 1)),
                floats[pl.ds(32 * slot, 1), :],
                floats[pl.ds(32 * slot + 16, 1), :],
            )
            for slot in slots
        ]
        done = []
        for codes, right, cosine, sine in loaded:
            block = jnp.concatenate([decode(code) for code in codes], axis=1)
            values = product3(parts(block.reshape(GX * SLAB, 128)), right, TN)
            real, imag = values[:, :128], values[:, 128:]
            done.append((real * cosine - imag * sine, imag * cosine + real * sine))
        for slot, (real, imag) in zip(slots, done):
            waves[slot, :, 0:128] = real
            waves[slot, :, 128:256] = imag
        return carry

    lax.fori_loop(0, steps, wave_body, 0)

    def grid_body(step, carry):
        field = step // 2
        part = step % 2
        rows = pl.ds(pl.multiple_of(step * 16, 16), 16)
        spectrum = [(waves[0, rows, 0:128], None)]
        for slot in range(1, GY):
            spectrum.append((waves[slot, rows, 0:128], waves[slot, rows, 128:256]))
        spectrum.append((waves[0, rows, 128:256], None))
        values = real_inverse(spectrum)
        top = pl.ds(pl.multiple_of(part * 16, 16), 16)
        for c in range(32):
            new_rows[field, c // 4, top, (c % 4) * 128 : (c % 4) * 128 + 128] = values[c].astype(BF16)
        return carry

    for field in range(FIELDS):
        lax.fori_loop(2 * field, 2 * field + 2, grid_body, 0)
        for other in octants[:-1]:
            pltpu.make_async_remote_copy(
                src_ref=new_rows.at[field, other],
                dst_ref=results[field].at[own_rows, :],
                send_sem=sem_last_out.at[field],
                recv_sem=sem_last_in.at[field],
                device_id=(other, slot_own),
                device_id_type=MESH,
            ).start()
        pltpu.make_async_copy(
            new_rows.at[field, octant], results[field].at[own_rows, :], sem_last_in.at[field]
        ).start()

    for side in range(2):
        wait_sent(side, sem_back_out)
    for field in range(FIELDS):
        moved = new_rows.at[field, pl.ds(0, GX - 1)]
        pltpu.make_async_copy(moved, moved, sem_rows_out.at[field]).wait()
        pltpu.make_async_copy(moved, moved, sem_last_out.at[field]).wait()
        pltpu.make_async_copy(results[field], results[field], sem_last_in.at[field]).wait()


def place_kernel(*refs):
    copies = [
        pltpu.make_async_copy(refs[field], refs[FIELDS + field], refs[2 * FIELDS].at[field])
        for field in range(FIELDS)
    ]
    for copy in copies:
        copy.start()
    for copy in copies:
        copy.wait()


def per_device(east_wind, north_wind, height, tracer):
    constants = [jnp.asarray(value) for value in tables()]
    anywhere = pl.BlockSpec(memory_space=pl.ANY)
    block = jax.ShapeDtypeStruct((NG // GY, COLS), BF16)
    dma = pltpu.SemaphoreType.DMA
    landed = pl.pallas_call(
        step_kernel,
        out_shape=(block,) * 4,
        in_specs=[pl.BlockSpec(memory_space=pltpu.HBM)] * 6,
        out_specs=(anywhere,) * 4,
        scratch_shapes=[
            pltpu.VMEM((MATRIX_ROWS, 256), BF16),
            pltpu.VMEM((FLOAT_ROWS, 128), F32),
            pltpu.VMEM((FIELDS, GX, ROWS, COLS), BF16),
            pltpu.VMEM((GY, 128, 256), BF16),
            pltpu.VMEM((GY, 128, 256), BF16),
            pltpu.VMEM((DEVICES, SLAB // 8, 8, 128), BF16),
            pltpu.VMEM((DEVICES, SLAB // 8, 8, 128), BF16),
            pltpu.VMEM((SLAB * PLANE, 128), F32),
            pltpu.VMEM((KX, 4, 128, 128), F32),
            pltpu.VMEM((DEVICES, SLAB // 8, 8, 128), BF16),
            pltpu.VMEM((GY, 128, 256), F32),
            pltpu.VMEM((FIELDS, GX, ROWS, COLS), BF16),
            dma((2,)),
            dma((FIELDS,)),
            dma((FIELDS,)),
            dma((2,)),
            dma((2, GY)),
            dma((2,)),
            dma((2, GY)),
            dma((FIELDS,)),
            dma((FIELDS,)),
            pltpu.SemaphoreType.REGULAR,
            pltpu.SemaphoreType.REGULAR,
        ],
        compiler_params=pltpu.CompilerParams(
            collective_id=0, has_side_effects=True, vmem_limit_bytes=32 * 1024 * 1024
        ),
    )(*[
        pltpu.with_memory_space_constraint(value, pltpu.HBM)
        for value in (east_wind, north_wind, height, tracer, *constants)
    ])
    return pl.pallas_call(
        place_kernel,
        out_shape=(block,) * 4,
        in_specs=[anywhere] * 4,
        out_specs=(pl.BlockSpec(memory_space=pltpu.HBM),) * 4,
        scratch_shapes=[dma((FIELDS,))],
        compiler_params=pltpu.CompilerParams(vmem_limit_bytes=1024 * 1024),
    )(*landed)


def solution(mesh):
    placed = (P("gy", "gx"),) * 4
    return jax.shard_map(
        per_device, mesh=mesh, in_specs=placed, out_specs=placed, check_vma=False
    )
```

```python
import math

import jax
import jax.numpy as jnp
import numpy as np
from jax import lax
from jax.experimental import pallas as pl
from jax.experimental.pallas import tpu as pltpu
from jax.sharding import PartitionSpec as P

NG = 4096
FIELDS = 4
GX = 8
GY = 16
DEVICES = GX * GY
KX = 11
SLAB = 24
FIRST = 16
PLANE = 136
REAL_ROWS = (0, 1, 2, 3, 4, 5, 6, 7, 17, 18, 19)
IMAG_ROWS = (8, 9, 10, 11, 12, 13, 14, 16, 20, 21, 22)
ROWS = 32
COLS = 512
POWER = 11

coriolis = 0.25
gravity_step = 2.0
depth_step = 2.0
diffusion = 0.02

F32 = jnp.float32
BF16 = jnp.bfloat16
MESH = pl.DeviceIdType.MESH


def split_const(matrix):
    whole = matrix.astype(np.float32)
    high = np.dtype(jnp.bfloat16)
    head = whole.astype(high)
    tail = (whole - head.astype(np.float32)).astype(high)
    return head, tail


def wave_of(slot, place):
    if slot == 0:
        return 32 * place if place < 43 else 16 + 32 * (place - 43)
    return slot + 32 * (place - 43)


def tables():
    turn = 2.0 * np.pi
    lane = np.arange(128)
    forward = np.zeros((2, GX, SLAB, 256))
    inverse = np.zeros((2, GX, SLAB, 256))
    for place in range(86):
        octant, member = place // KX, place % KX
        real_row, imag_row = REAL_ROWS[member], IMAG_ROWS[member]
        low = place - 43
        cosine, sine = np.cos(turn * lane * low / 128), np.sin(turn * lane * low / 128)
        forward[1, octant, real_row] = np.concatenate([cosine, sine])
        forward[1, octant, imag_row] = np.concatenate([-sine, cosine])
        inverse[1, octant, real_row] = np.concatenate([cosine, sine])
        inverse[1, octant, imag_row] = np.concatenate([-sine, cosine])
        wave = wave_of(0, place)
        cosine, sine = np.cos(turn * lane * wave / NG), np.sin(turn * lane * wave / NG)
        half = 0 if place < 43 else 128
        weight = 1.0 if wave == 0 else 2.0
        forward[0, octant, real_row, half : half + 128] = cosine
        forward[0, octant, imag_row, half : half + 128] = -sine
        inverse[0, octant, real_row, half : half + 128] = weight * cosine
        inverse[0, octant, imag_row, half : half + 128] = -weight * sine
    forward = forward.reshape(2, GX * SLAB, 256)
    inverse = np.concatenate(
        [
            inverse[:, :, :FIRST].reshape(2, GX * FIRST, 256),
            inverse[:, :, FIRST:].reshape(2, GX * (SLAB - FIRST), 256),
        ],
        axis=1,
    )
    angle = turn * np.outer(np.arange(GY), lane) / NG
    twist = np.stack([np.cos(angle), np.sin(angle)], axis=1)[:, :, None, :]
    twist = np.broadcast_to(twist, (GY, 2, 16, 128)).astype(np.float32)
    angle = turn * np.outer(lane, lane) / 128
    cosine, sine = np.cos(angle), np.sin(angle)
    gather = np.block([[cosine, sine], [-sine, cosine]])
    scatter = np.block([[cosine, -sine], [sine, cosine]])
    angle = turn * np.outer(np.arange(ROWS), np.arange(ROWS)) / ROWS
    cosine, sine = np.kron(np.eye(4), np.cos(angle)), np.kron(np.eye(4), np.sin(angle))
    fan_in = np.block([[cosine, -sine], [sine, cosine]])
    fan_out = np.block([[cosine, sine], [-sine, cosine]])
    angle = turn * np.outer(lane, lane % ROWS) / NG
    spin = np.stack([np.cos(angle), np.sin(angle)]).astype(np.float32)
    pieces = []
    for matrix in (forward.reshape(-1, 256), inverse.reshape(-1, 256) / NG, gather, scatter, fan_in, fan_out):
        pieces.extend(split_const(matrix))
    floats = np.concatenate([twist.reshape(-1, 128), spin.reshape(-1, 128)], axis=0)
    return np.concatenate(pieces, axis=0), floats


FWD_AT = 0
INV_AT = 4 * GX * SLAB
SQUARE_AT = 8 * GX * SLAB
MATRIX_ROWS = SQUARE_AT + 8 * 256
SPIN_AT = GY * 2 * 16
FLOAT_ROWS = SPIN_AT + 256


def matrix_pair(matrices, start, which, count=GX * SLAB):
    first = pl.multiple_of(start + which * (GX * SLAB), 64)
    second = pl.multiple_of(start + (which + 2) * (GX * SLAB), 64)
    return matrices[pl.ds(first, count), :], matrices[pl.ds(second, count), :]


def square_pair(matrices, which):
    first = SQUARE_AT + which * 512
    return matrices[first : first + 256, :], matrices[first + 256 : first + 512, :]


def encode(values):
    rows = values.shape[1]
    largest = jnp.max(jnp.abs(values), axis=1, keepdims=True)
    scale = (jnp.maximum(largest, 1e-34) * 1.01).astype(BF16).astype(F32)
    level = values * (2048.0 / scale)
    second = level * level
    fourth = second * second
    eighth = fourth * fourth
    code = eighth * second * level
    ending = code[:, rows - 8 :]
    last = lax.broadcasted_iota(jnp.int32, ending.shape, 1) == 7
    ending = jnp.where(last, scale, ending)
    code = jnp.concatenate([code[:, : rows - 8], ending], axis=1) if rows > 8 else ending
    return code.reshape(values.shape[0], rows // 8, 8, 128).astype(BF16)


def decode(codes):
    rows = codes.shape[1] * 8
    code = codes.astype(F32).reshape(codes.shape[0], rows, 128)
    scale = code[:, rows - 1 : rows, :] * (1.0 / 2048.0)
    size = jnp.maximum(jnp.abs(code), 2.0**-126)
    return jnp.exp2(jnp.log2(size) * (1.0 / POWER - 1.0)) * (code * scale)


def real_transform(values):
    count = len(values)
    if count == 2:
        return [(values[0] + values[1], None), (values[0] - values[1], None)]
    even = real_transform(values[0::2])
    odd = real_transform(values[1::2])
    half = count // 2
    result = [None] * (half + 1)
    for index in range(count // 4 + 1):
        even_real, even_imag = even[index]
        odd_real, odd_imag = odd[index]
        if index == 0:
            result[0] = (even_real + odd_real, None)
            result[half] = (even_real - odd_real, None)
        elif index == count // 4:
            result[index] = (even_real, -odd_real)
        else:
            cosine = math.cos(2.0 * math.pi * index / count)
            sine = math.sin(2.0 * math.pi * index / count)
            turned_real = odd_real * cosine + odd_imag * sine
            turned_imag = odd_imag * cosine - odd_real * sine
            result[index] = (even_real + turned_real, even_imag + turned_imag)
            result[half - index] = (even_real - turned_real, turned_imag - even_imag)
    return result


def real_inverse(waves):
    half = len(waves) - 1
    count = 2 * half
    if count == 2:
        return [waves[0][0] + waves[1][0], waves[0][0] - waves[1][0]]
    even = []
    odd = []
    for index in range(count // 4 + 1):
        real, imag = waves[index]
        other_real, other_imag = waves[half - index]
        if index == 0:
            even.append((real + other_real, None))
            odd.append((real - other_real, None))
        elif index == count // 4:
            even.append((real + real, None))
            odd.append((-(imag + imag), None))
        else:
            cosine = math.cos(2.0 * math.pi * index / count)
            sine = math.sin(2.0 * math.pi * index / count)
            even.append((real + other_real, imag - other_imag))
            gap_real = real - other_real
            gap_imag = imag + other_imag
            odd.append((gap_real * cosine - gap_imag * sine, gap_real * sine + gap_imag * cosine))
    outputs = [None] * count
    outputs[0::2] = real_inverse(even)
    outputs[1::2] = real_inverse(odd)
    return outputs


def parts(values):
    head = values.astype(BF16)
    return head, (values - head.astype(F32)).astype(BF16)


def product(left, right, dims):
    return lax.dot_general(left, right, (dims, ((), ())), preferred_element_type=F32)


def product3(left, right, dims):
    left_head, left_tail = left
    right_head, right_tail = right
    left_all = jnp.concatenate([left_head, left_head, left_tail], axis=dims[0][0])
    right_all = jnp.concatenate([right_head, right_tail, right_head], axis=dims[1][0])
    return product(left_all, right_all, dims)


NN = ((1,), (0,))
NT = ((1,), (1,))
TN = ((0,), (0,))


def fill_gains(gains, octant, slot):
    chunk = 32

    def body(step, carry):
        member = step // (128 // chunk)
        top = (step % (128 // chunk)) * chunk
        place = KX * octant + member
        zero_slot = jnp.where(place < 43, 32 * place, 16 + 32 * (place - 43))
        mode_x = jnp.where(slot == 0, zero_slot, slot + 32 * (place - 43))
        lane = lax.broadcasted_iota(jnp.int32, (chunk, 128), 1)
        row = lax.broadcasted_iota(jnp.int32, (chunk, 128), 0) + top
        field = lane // 32
        mode_y = row + 128 * (lane % 32)
        mode_y = jnp.where(mode_y < NG // 2, mode_y, mode_y - NG)
        cutoff = NG // 3
        inside = mode_y * mode_y + mode_x * mode_x <= cutoff * cutoff
        unit = 2.0 * math.pi / NG
        wave_x = mode_x.astype(F32) * unit
        wave_y = mode_y.astype(F32) * unit
        square = wave_x * wave_x + wave_y * wave_y
        scale = 1.0 / NG
        gain = jnp.where(inside, scale / (1.0 + diffusion * square * square), 0.0)
        stiffness = gravity_step * depth_step * square
        below = 1.0 / (1.0 + coriolis * coriolis + stiffness)
        above = (1.0 - coriolis * coriolis - stiffness) * below
        twice = (2.0 * coriolis) * below
        push_u = above * wave_x - twice * wave_y
        push_v = above * wave_y + twice * wave_x
        push_h = (2.0 * gravity_step) * square * below
        sum_u = wave_x + push_u
        sum_v = wave_y + push_v
        curl_u = -wave_y - coriolis * sum_u
        curl_v = wave_x - coriolis * sum_v
        curl_h = -coriolis * push_h
        anchor = square == 0.0
        over = 1.0 / jnp.where(anchor, 1.0, square)
        first = field == 0
        second = field == 1
        third = field == 2
        lead = jnp.where(first, -wave_y, wave_x)
        trail = jnp.where(first, wave_x, wave_y)
        from_u = (lead * curl_u + trail * push_u) * over
        from_v = (lead * curl_v + trail * push_v) * over
        from_h = -(lead * curl_h + trail * push_h) * over
        rotate = 1.0 / (1.0 + coriolis * coriolis)
        keep = (1.0 - coriolis * coriolis) * rotate
        cross = 2.0 * coriolis * rotate
        from_u = jnp.where(anchor, jnp.where(first, keep, -cross), from_u)
        from_v = jnp.where(anchor, jnp.where(first, cross, keep), from_v)
        zero = jnp.zeros_like(gain)
        same = jnp.where(
            first,
            from_u,
            jnp.where(second, from_v, jnp.where(third, 1.0 - depth_step * push_h, 1.0)),
        )
        one = jnp.where(second, from_u, jnp.where(third, -depth_step * sum_v, zero))
        two = jnp.where(first, from_h, jnp.where(third, -depth_step * sum_u, zero))
        three = jnp.where(first, from_v, jnp.where(second, from_h, zero))
        place_rows = pl.ds(pl.multiple_of(top, chunk), chunk)
        gains[member, 0, place_rows, :] = same * gain
        gains[member, 1, place_rows, :] = one * gain
        gains[member, 2, place_rows, :] = two * gain
        gains[member, 3, place_rows, :] = three * gain
        return carry

    lax.fori_loop(0, KX * (128 // chunk), body, 0)


def apply_gains(gains, member, real, imag):
    lane = lax.broadcasted_iota(jnp.int32, (128, 128), 1)
    field = lane // 32
    second = field == 1
    third = field == 2
    gain = gains[member, 0]
    out_real = real * gain
    out_imag = imag * gain
    crossed = [third, None, second]
    for turn in (1, 2, 3):
        gain = gains[member, turn]
        moved_real = pltpu.roll(real, 32 * turn, 1)
        moved_imag = pltpu.roll(imag, 32 * turn, 1)
        swap = crossed[turn - 1]
        if swap is None:
            use_real, use_imag = -moved_imag, moved_real
        else:
            use_real = jnp.where(swap, -moved_imag, moved_real)
            use_imag = jnp.where(swap, moved_real, moved_imag)
        out_real = out_real + gain * use_real
        out_imag = out_imag + gain * use_imag
    return out_real, out_imag


def step_kernel(*refs):
    sources = refs[0:4]
    matrix_source, float_source = refs[4:6]
    results = refs[6:10]
    (
        matrices,
        floats,
        grid_rows,
        head,
        tail,
        slabs,
        landed,
        columns,
        gains,
        returned,
        waves,
        new_rows,
        sem_table,
        sem_rows_out,
        sem_rows_in,
        sem_out,
        sem_in,
        sem_back_out,
        sem_back_in,
        sem_last_out,
        sem_last_in,
        sem_leaders,
        sem_all,
    ) = refs[10:]
    octant = lax.axis_index("gx")
    slot_own = lax.axis_index("gy")
    own = slot_own * GX + octant
    octants = [
        4 * ((octant // 4 + across) % 2) + (octant % 4 + along) % 4
        for across, along in ((1, 2), (1, 1), (1, 3), (0, 2), (1, 0), (0, 1), (0, 3), (0, 0))
    ]
    half_own = slot_own // 8
    level_own = (slot_own // 2) % 4
    core_own = slot_own % 2

    def distance(step):
        turn = step // 2
        odd = step % 2
        far = jnp.where(turn == 3, 0, jnp.where(turn == 2, 3, 2 - turn))
        near = jnp.where(turn == 3, 0, turn + 1)
        return 1 - odd, jnp.where(odd == 1, near, far)

    def slots_at(step):
        half, level = distance(step)
        base = 8 * ((half_own + half) % 2) + 2 * ((level_own + level) % 4)
        return [base + 1 - core_own, base + core_own]

    def slots_before(step):
        half, level = distance(step)
        base = 8 * ((half_own + half) % 2) + 2 * ((level_own + 4 - level) % 4)
        return [base + 1 - core_own, base + core_own]

    barrier = pltpu.get_barrier_semaphore()
    across_own = octant // 4
    for across, along in ((0, 1), (0, 2), (0, 3), (1, 0), (1, 1), (1, 2), (1, 3)):
        other = 4 * ((across_own + across) % 2) + (octant % 4 + along) % 4

        @pl.when(other != 0)
        def greet_member():
            pl.semaphore_signal(
                barrier, inc=1, device_id=(other, slot_own), device_id_type=MESH
            )

    @pl.when(octant == 0)
    def greet_leaders():
        for step in range(1, GY):
            pl.semaphore_signal(
                barrier, inc=1, device_id=(octant, (slot_own + step) % GY), device_id_type=MESH
            )

    table_copies = [
        pltpu.make_async_copy(matrix_source, matrices, sem_table.at[0]),
        pltpu.make_async_copy(float_source, floats, sem_table.at[1]),
    ]
    for copy in table_copies:
        copy.start()
    own_rows = pl.ds(pl.multiple_of(octant * ROWS, ROWS), ROWS)
    for field in range(FIELDS):
        pltpu.make_async_copy(
            sources[field].at[own_rows, :], grid_rows.at[field, octant], sem_rows_in.at[field]
        ).start()

    @pl.when(octant != 0)
    def wait_member():
        pl.semaphore_wait(barrier, GX - 1)

    @pl.when(octant == 1)
    def release_leader():
        pl.semaphore_signal(
            sem_all, inc=1, device_id=(octant - 1, slot_own), device_id_type=MESH
        )

    @pl.when(octant == 0)
    def wait_release():
        pl.semaphore_wait(sem_all, 1)

    for field in range(FIELDS):
        for other in octants[:-1]:
            pltpu.make_async_remote_copy(
                src_ref=sources[field].at[pl.ds(pl.multiple_of(other * ROWS, ROWS), ROWS), :],
                dst_ref=grid_rows.at[field, octant],
                send_sem=sem_rows_out.at[field],
                recv_sem=sem_rows_in.at[field],
                device_id=(other, slot_own),
                device_id_type=MESH,
            ).start()

    fill_gains(gains, octant, slot_own)

    @pl.when(octant == 0)
    def tell_members():
        pl.semaphore_wait(barrier, GY - 1)
        for step in range(1, GY):
            pl.semaphore_signal(
                sem_leaders,
                inc=1,
                device_id=(octant, (slot_own + step) % GY),
                device_id_type=MESH,
            )
        pl.semaphore_wait(sem_leaders, GY - 1)
        for other in octants[:-1]:
            pl.semaphore_signal(
                sem_all, inc=1, device_id=(other, slot_own), device_id_type=MESH
            )

    for copy in table_copies:
        copy.wait()

    def row_body(step, carry):
        field = step // 2
        part = step % 2
        top = pl.multiple_of(part * 16, 16)
        chunk = [
            grid_rows[field, c // 4, pl.ds(top, 16), (c % 4) * 128 : (c % 4) * 128 + 128].astype(F32)
            for c in range(32)
        ]
        spectrum = real_transform(chunk)
        rows = pl.ds(pl.multiple_of(step * 16, 16), 16)
        for slot in range(GY):
            if slot == 0:
                real, imag = spectrum[0][0], spectrum[16][0]
            else:
                wave_real, wave_imag = spectrum[slot]
                cosine = floats[32 * slot : 32 * slot + 16, :]
                sine = floats[32 * slot + 16 : 32 * slot + 32, :]
                real = wave_real * cosine + wave_imag * sine
                imag = wave_imag * cosine - wave_real * sine
            for side, value in ((0, real), (128, imag)):
                high, low = parts(value)
                head[slot, rows, side : side + 128] = high
                tail[slot, rows, side : side + 128] = low
        return carry

    for field in range(FIELDS):
        pltpu.make_async_copy(
            grid_rows.at[field], grid_rows.at[field], sem_rows_in.at[field]
        ).wait()
        lax.fori_loop(2 * field, 2 * field + 2, row_body, 0)

    @pl.when(octant != 0)
    def wait_all():
        pl.semaphore_wait(sem_all, 1)

    sides = (pl.ds(0, FIRST // 8), pl.ds(FIRST // 8, (SLAB - FIRST) // 8))

    def send_slot(side, slot, others, target, out_sem, in_sem):
        for other in others:
            pltpu.make_async_remote_copy(
                src_ref=slabs.at[slot * GX + other, sides[side]],
                dst_ref=target.at[own, sides[side]],
                send_sem=out_sem.at[side],
                recv_sem=in_sem.at[side, slot_own],
                device_id=(other, slot),
                device_id_type=MESH,
            ).start()

    def keep_own(side, target, in_sem):
        pltpu.make_async_copy(
            slabs.at[own, sides[side]], target.at[own, sides[side]], in_sem.at[side, slot_own]
        ).start()

    def wait_group(side, slot, target, in_sem):
        group = target.at[pl.ds(slot * GX, GX), sides[side]]
        pltpu.make_async_copy(group, group, in_sem.at[side, slot]).wait()

    def wait_sent(side, out_sem):
        sent = slabs.at[pl.ds(0, DEVICES - 1), sides[side]]
        pltpu.make_async_copy(sent, sent, out_sem.at[side]).wait()

    def slot_products(slots):
        loaded = [
            (matrix_pair(matrices, FWD_AT, jnp.minimum(slot, 1)), (head[slot], tail[slot]))
            for slot in slots
        ]
        codes = []
        for left, right in loaded:
            spectrum = product3(left, right, NT).reshape(GX, SLAB, 128)
            codes.append([encode(spectrum[:, :FIRST]), encode(spectrum[:, FIRST:])])
        for slot, pieces in zip(slots, codes):
            for side in range(2):
                slabs[pl.ds(slot * GX, GX), sides[side]] = pieces[side]

    steps = GY // 2

    def slot_body(step, carry):
        slots = slots_at(step)
        slot_products(slots)
        for slot in slots:
            send_slot(0, slot, octants, landed, sem_out, sem_in)
        return carry

    lax.fori_loop(0, steps - 1, slot_body, 0)
    twin = slots_at(steps - 1)[0]
    slot_products([twin, slot_own])
    send_slot(0, twin, octants, landed, sem_out, sem_in)
    send_slot(0, slot_own, octants[:-1], landed, sem_out, sem_in)
    keep_own(0, landed, sem_in)

    def second_body(step, carry):
        for slot in slots_at(step):
            send_slot(1, slot, octants, landed, sem_out, sem_in)
        return carry

    lax.fori_loop(0, steps - 1, second_body, 0)
    send_slot(1, twin, octants, landed, sem_out, sem_in)
    send_slot(1, slot_own, octants[:-1], landed, sem_out, sem_in)
    keep_own(1, landed, sem_in)

    def spread(side):
        first = 0 if side == 0 else FIRST
        count = FIRST if side == 0 else SLAB - FIRST

        def body(step, carry):
            for slot in slots_before(step):
                wait_group(side, slot, landed, sem_in)
                values = decode(landed[pl.ds(slot * GX, GX), sides[side]])
                for source in range(GX):
                    columns[
                        pl.ds(first * PLANE + slot * GX + source, count, stride=PLANE), :
                    ] = values[source]
            return carry

        return body

    def plane(row):
        return slice(row * 128, row * 128 + 128)

    def column_rows(row):
        return slice(row * PLANE, row * PLANE + 128)

    def stack_pair(reals, imags):
        return jnp.concatenate(
            [jnp.concatenate(reals, axis=1), jnp.concatenate(imags, axis=1)], axis=0
        )

    def work_columns(groups):
        members = [member for group in groups for member in group]
        cosine = floats[SPIN_AT : SPIN_AT + 128, :]
        sine = floats[SPIN_AT + 128 : SPIN_AT + 256, :]
        loaded = [
            stack_pair(
                [columns[column_rows(REAL_ROWS[member]), :] for member in group],
                [columns[column_rows(IMAG_ROWS[member]), :] for member in group],
            )
            for group in groups
        ]
        turned = []
        for group, values in zip(groups, loaded):
            mixed = product3(square_pair(matrices, 0), parts(values), NN)
            for index in range(len(group)):
                real, imag = mixed[:128, plane(index)], mixed[128:, plane(index)]
                turned.append(
                    jnp.concatenate(
                        [real * cosine + imag * sine, imag * cosine - real * sine], axis=1
                    )
                )
        modes = product3(
            parts(jnp.concatenate(turned, axis=0)), square_pair(matrices, 2), NN
        )
        changed = []
        for index, member in enumerate(members):
            piece = modes[plane(index)]
            real, imag = apply_gains(gains, member, piece[:, :128], piece[:, 128:])
            changed.append(jnp.concatenate([real, imag], axis=1))
        mixed = product3(
            parts(jnp.concatenate(changed, axis=0)), square_pair(matrices, 3), NN
        )
        start = 0
        done = []
        for group in groups:
            reals, imags = [], []
            for index in range(start, start + len(group)):
                piece = mixed[plane(index)]
                real, imag = piece[:, :128], piece[:, 128:]
                reals.append(real * cosine - imag * sine)
                imags.append(imag * cosine + real * sine)
            start += len(group)
            done.append(
                product3(square_pair(matrices, 1), parts(stack_pair(reals, imags)), NN)
            )
        for group, values in zip(groups, done):
            for index, member in enumerate(group):
                columns[column_rows(REAL_ROWS[member]), :] = values[:128, plane(index)]
                columns[column_rows(IMAG_ROWS[member]), :] = values[128:, plane(index)]

    def collect(side, slot):
        first = 0 if side == 0 else FIRST
        count = FIRST if side == 0 else SLAB - FIRST
        values = jnp.stack(
            [
                columns[pl.ds(first * PLANE + slot * GX + source, count, stride=PLANE), :]
                for source in range(GX)
            ]
        )
        slabs[pl.ds(slot * GX, GX), sides[side]] = encode(values)

    def send_back(side):
        def body(step, carry):
            slots = slots_at(step)
            for slot in slots:
                collect(side, slot)
                send_slot(side, slot, octants, returned, sem_back_out, sem_back_in)
            return carry

        wait_sent(side, sem_out)
        lax.fori_loop(0, steps - 1, body, 0)
        collect(side, twin)
        send_slot(side, twin, octants, returned, sem_back_out, sem_back_in)
        collect(side, slot_own)
        send_slot(side, slot_own, octants[:-1], returned, sem_back_out, sem_back_in)
        keep_own(side, returned, sem_back_in)

    lax.fori_loop(0, steps, spread(0), 0)
    columns[column_rows(FIRST - 1), :] = jnp.zeros((128, 128), F32)
    work_columns([(0, 1), (2, 3), (4, 5)])
    lax.fori_loop(0, steps, spread(1), 0)
    columns[column_rows(SLAB - 1), :] = jnp.zeros((128, 128), F32)
    work_columns([(6, 7)])
    send_back(0)
    work_columns([(8, 9), (10,)])
    send_back(1)

    def wave_part(side, slots):
        start = INV_AT if side == 0 else INV_AT + GX * FIRST
        count = GX * FIRST if side == 0 else GX * (SLAB - FIRST)
        loaded = [
            (
                returned[pl.ds(slot * GX, GX), sides[side]],
                matrix_pair(matrices, start, jnp.minimum(slot, 1), count),
            )
            for slot in slots
        ]
        return [
            product3(parts(decode(codes).reshape(count, 128)), right, TN)
            for codes, right in loaded
        ]

    def first_wave(step, carry):
        slots = slots_before(step)
        for slot in slots:
            wait_group(0, slot, returned, sem_back_in)
        for slot, values in zip(slots, wave_part(0, slots)):
            waves[slot] = values
        return carry

    def second_wave(step, carry):
        slots = slots_before(step)
        for slot in slots:
            wait_group(1, slot, returned, sem_back_in)
        before = [waves[slot] for slot in slots]
        done = []
        for slot, values, base in zip(slots, wave_part(1, slots), before):
            values = values + base
            cosine = floats[pl.ds(32 * slot, 1), :]
            sine = floats[pl.ds(32 * slot + 16, 1), :]
            real, imag = values[:, :128], values[:, 128:]
            done.append((real * cosine - imag * sine, imag * cosine + real * sine))
        for slot, (real, imag) in zip(slots, done):
            waves[slot, :, 0:128] = real
            waves[slot, :, 128:256] = imag
        return carry

    lax.fori_loop(0, steps, first_wave, 0)
    lax.fori_loop(0, steps, second_wave, 0)

    def grid_body(step, carry):
        field = step // 2
        part = step % 2
        rows = pl.ds(pl.multiple_of(step * 16, 16), 16)
        spectrum = [(waves[0, rows, 0:128], None)]
        for slot in range(1, GY):
            spectrum.append((waves[slot, rows, 0:128], waves[slot, rows, 128:256]))
        spectrum.append((waves[0, rows, 128:256], None))
        values = real_inverse(spectrum)
        top = pl.ds(pl.multiple_of(part * 16, 16), 16)
        for c in range(32):
            new_rows[field, c // 4, top, (c % 4) * 128 : (c % 4) * 128 + 128] = values[c].astype(BF16)
        return carry

    for field in range(FIELDS):
        lax.fori_loop(2 * field, 2 * field + 2, grid_body, 0)
        for other in octants[:-1]:
            pltpu.make_async_remote_copy(
                src_ref=new_rows.at[field, other],
                dst_ref=results[field].at[own_rows, :],
                send_sem=sem_last_out.at[field],
                recv_sem=sem_last_in.at[field],
                device_id=(other, slot_own),
                device_id_type=MESH,
            ).start()
        pltpu.make_async_copy(
            new_rows.at[field, octant], results[field].at[own_rows, :], sem_last_in.at[field]
        ).start()

    for side in range(2):
        wait_sent(side, sem_back_out)
    for field in range(FIELDS):
        moved = new_rows.at[field, pl.ds(0, GX - 1)]
        pltpu.make_async_copy(moved, moved, sem_rows_out.at[field]).wait()
        pltpu.make_async_copy(moved, moved, sem_last_out.at[field]).wait()
        pltpu.make_async_copy(results[field], results[field], sem_last_in.at[field]).wait()


def place_kernel(*refs):
    copies = [
        pltpu.make_async_copy(refs[field], refs[FIELDS + field], refs[2 * FIELDS].at[field])
        for field in range(FIELDS)
    ]
    for copy in copies:
        copy.start()
    for copy in copies:
        copy.wait()


def per_device(east_wind, north_wind, height, tracer):
    constants = [jnp.asarray(value) for value in tables()]
    anywhere = pl.BlockSpec(memory_space=pl.ANY)
    block = jax.ShapeDtypeStruct((NG // GY, COLS), BF16)
    dma = pltpu.SemaphoreType.DMA
    landed = pl.pallas_call(
        step_kernel,
        out_shape=(block,) * 4,
        in_specs=[pl.BlockSpec(memory_space=pltpu.HBM)] * 6,
        out_specs=(anywhere,) * 4,
        scratch_shapes=[
            pltpu.VMEM((MATRIX_ROWS, 256), BF16),
            pltpu.VMEM((FLOAT_ROWS, 128), F32),
            pltpu.VMEM((FIELDS, GX, ROWS, COLS), BF16),
            pltpu.VMEM((GY, 128, 256), BF16),
            pltpu.VMEM((GY, 128, 256), BF16),
            pltpu.VMEM((DEVICES, SLAB // 8, 8, 128), BF16),
            pltpu.VMEM((DEVICES, SLAB // 8, 8, 128), BF16),
            pltpu.VMEM((SLAB * PLANE, 128), F32),
            pltpu.VMEM((KX, 4, 128, 128), F32),
            pltpu.VMEM((DEVICES, SLAB // 8, 8, 128), BF16),
            pltpu.VMEM((GY, 128, 256), F32),
            pltpu.VMEM((FIELDS, GX, ROWS, COLS), BF16),
            dma((2,)),
            dma((FIELDS,)),
            dma((FIELDS,)),
            dma((2,)),
            dma((2, GY)),
            dma((2,)),
            dma((2, GY)),
            dma((FIELDS,)),
            dma((FIELDS,)),
            pltpu.SemaphoreType.REGULAR,
            pltpu.SemaphoreType.REGULAR,
        ],
        compiler_params=pltpu.CompilerParams(
            collective_id=0, has_side_effects=True, vmem_limit_bytes=32 * 1024 * 1024
        ),
    )(*[
        pltpu.with_memory_space_constraint(value, pltpu.HBM)
        for value in (east_wind, north_wind, height, tracer, *constants)
    ])
    return pl.pallas_call(
        place_kernel,
        out_shape=(block,) * 4,
        in_specs=[anywhere] * 4,
        out_specs=(pl.BlockSpec(memory_space=pltpu.HBM),) * 4,
        scratch_shapes=[dma((FIELDS,))],
        compiler_params=pltpu.CompilerParams(vmem_limit_bytes=1024 * 1024),
    )(*landed)


def solution(mesh):
    placed = (P("gy", "gx"),) * 4
    return jax.shard_map(
        per_device, mesh=mesh, in_specs=placed, out_specs=placed, check_vma=False
    )
```

```python
import math

import jax
import jax.numpy as jnp
import numpy as np
from jax import lax
from jax.experimental import pallas as pl
from jax.experimental.pallas import tpu as pltpu
from jax.sharding import PartitionSpec as P

NG = 4096
FIELDS = 4
GX = 8
GY = 16
DEVICES = GX * GY
KX = 11
SLAB = 24
FIRST = 16
PLANE = 136
REAL_ROWS = (0, 1, 2, 3, 4, 5, 6, 7, 17, 18, 19)
IMAG_ROWS = (8, 9, 10, 11, 12, 13, 14, 16, 20, 21, 22)
ROWS = 32
COLS = 512
POWER = 11

coriolis = 0.25
gravity_step = 2.0
depth_step = 2.0
diffusion = 0.02

F32 = jnp.float32
BF16 = jnp.bfloat16
MESH = pl.DeviceIdType.MESH


def split_const(matrix):
    whole = matrix.astype(np.float32)
    high = np.dtype(jnp.bfloat16)
    head = whole.astype(high)
    tail = (whole - head.astype(np.float32)).astype(high)
    return head, tail


def wave_of(slot, place):
    if slot == 0:
        return 32 * place if place < 43 else 16 + 32 * (place - 43)
    return slot + 32 * (place - 43)


def tables():
    turn = 2.0 * np.pi
    lane = np.arange(128)
    forward = np.zeros((2, GX, SLAB, 256))
    inverse = np.zeros((2, GX, SLAB, 256))
    for place in range(86):
        octant, member = place // KX, place % KX
        real_row, imag_row = REAL_ROWS[member], IMAG_ROWS[member]
        low = place - 43
        cosine, sine = np.cos(turn * lane * low / 128), np.sin(turn * lane * low / 128)
        forward[1, octant, real_row] = np.concatenate([cosine, sine])
        forward[1, octant, imag_row] = np.concatenate([-sine, cosine])
        inverse[1, octant, real_row] = np.concatenate([cosine, sine])
        inverse[1, octant, imag_row] = np.concatenate([-sine, cosine])
        wave = wave_of(0, place)
        cosine, sine = np.cos(turn * lane * wave / NG), np.sin(turn * lane * wave / NG)
        half = 0 if place < 43 else 128
        weight = 1.0 if wave == 0 else 2.0
        forward[0, octant, real_row, half : half + 128] = cosine
        forward[0, octant, imag_row, half : half + 128] = -sine
        inverse[0, octant, real_row, half : half + 128] = weight * cosine
        inverse[0, octant, imag_row, half : half + 128] = -weight * sine
    forward = forward.reshape(2, GX * SLAB, 256)
    inverse = np.concatenate(
        [
            inverse[:, :, :FIRST].reshape(2, GX * FIRST, 256),
            inverse[:, :, FIRST:].reshape(2, GX * (SLAB - FIRST), 256),
        ],
        axis=1,
    )
    angle = turn * np.outer(np.arange(GY), lane) / NG
    twist = np.stack([np.cos(angle), np.sin(angle)], axis=1)[:, :, None, :]
    twist = np.broadcast_to(twist, (GY, 2, 16, 128)).astype(np.float32)
    angle = turn * np.outer(lane, lane) / 128
    cosine, sine = np.cos(angle), np.sin(angle)
    gather = np.block([[cosine, sine], [-sine, cosine]])
    scatter = np.block([[cosine, -sine], [sine, cosine]])
    angle = turn * np.outer(np.arange(ROWS), np.arange(ROWS)) / ROWS
    cosine, sine = np.kron(np.eye(4), np.cos(angle)), np.kron(np.eye(4), np.sin(angle))
    fan_in = np.block([[cosine, -sine], [sine, cosine]])
    fan_out = np.block([[cosine, sine], [-sine, cosine]])
    angle = turn * np.outer(lane, lane % ROWS) / NG
    spin = np.stack([np.cos(angle), np.sin(angle)]).astype(np.float32)
    pieces = []
    for matrix in (forward.reshape(-1, 256), inverse.reshape(-1, 256) / NG, gather, scatter, fan_in, fan_out):
        pieces.extend(split_const(matrix))
    floats = np.concatenate([twist.reshape(-1, 128), spin.reshape(-1, 128)], axis=0)
    return np.concatenate(pieces, axis=0), floats


FWD_AT = 0
INV_AT = 4 * GX * SLAB
SQUARE_AT = 8 * GX * SLAB
MATRIX_ROWS = SQUARE_AT + 8 * 256
SPIN_AT = GY * 2 * 16
FLOAT_ROWS = SPIN_AT + 256


def matrix_pair(matrices, start, which, count=GX * SLAB):
    first = pl.multiple_of(start + which * (GX * SLAB), 64)
    second = pl.multiple_of(start + (which + 2) * (GX * SLAB), 64)
    return matrices[pl.ds(first, count), :], matrices[pl.ds(second, count), :]


def square_pair(matrices, which):
    first = SQUARE_AT + which * 512
    return matrices[first : first + 256, :], matrices[first + 256 : first + 512, :]


def encode(values):
    rows = values.shape[1]
    largest = jnp.max(jnp.abs(values), axis=1, keepdims=True)
    scale = (jnp.maximum(largest, 1e-34) * 1.01).astype(BF16).astype(F32)
    level = values * (2048.0 / scale)
    second = level * level
    fourth = second * second
    eighth = fourth * fourth
    code = eighth * second * level
    ending = code[:, rows - 8 :]
    last = lax.broadcasted_iota(jnp.int32, ending.shape, 1) == 7
    ending = jnp.where(last, scale, ending)
    code = jnp.concatenate([code[:, : rows - 8], ending], axis=1) if rows > 8 else ending
    return code.reshape(values.shape[0], rows // 8, 8, 128).astype(BF16)


def decode(codes):
    rows = codes.shape[1] * 8
    code = codes.astype(F32).reshape(codes.shape[0], rows, 128)
    scale = code[:, rows - 1 : rows, :] * (1.0 / 2048.0)
    size = jnp.maximum(jnp.abs(code), 2.0**-126)
    return jnp.exp2(jnp.log2(size) * (1.0 / POWER - 1.0)) * (code * scale)


def real_transform(values):
    count = len(values)
    if count == 2:
        return [(values[0] + values[1], None), (values[0] - values[1], None)]
    even = real_transform(values[0::2])
    odd = real_transform(values[1::2])
    half = count // 2
    result = [None] * (half + 1)
    for index in range(count // 4 + 1):
        even_real, even_imag = even[index]
        odd_real, odd_imag = odd[index]
        if index == 0:
            result[0] = (even_real + odd_real, None)
            result[half] = (even_real - odd_real, None)
        elif index == count // 4:
            result[index] = (even_real, -odd_real)
        else:
            cosine = math.cos(2.0 * math.pi * index / count)
            sine = math.sin(2.0 * math.pi * index / count)
            turned_real = odd_real * cosine + odd_imag * sine
            turned_imag = odd_imag * cosine - odd_real * sine
            result[index] = (even_real + turned_real, even_imag + turned_imag)
            result[half - index] = (even_real - turned_real, turned_imag - even_imag)
    return result


def real_inverse(waves):
    half = len(waves) - 1
    count = 2 * half
    if count == 2:
        return [waves[0][0] + waves[1][0], waves[0][0] - waves[1][0]]
    even = []
    odd = []
    for index in range(count // 4 + 1):
        real, imag = waves[index]
        other_real, other_imag = waves[half - index]
        if index == 0:
            even.append((real + other_real, None))
            odd.append((real - other_real, None))
        elif index == count // 4:
            even.append((real + real, None))
            odd.append((-(imag + imag), None))
        else:
            cosine = math.cos(2.0 * math.pi * index / count)
            sine = math.sin(2.0 * math.pi * index / count)
            even.append((real + other_real, imag - other_imag))
            gap_real = real - other_real
            gap_imag = imag + other_imag
            odd.append((gap_real * cosine - gap_imag * sine, gap_real * sine + gap_imag * cosine))
    outputs = [None] * count
    outputs[0::2] = real_inverse(even)
    outputs[1::2] = real_inverse(odd)
    return outputs


def parts(values):
    head = values.astype(BF16)
    return head, (values - head.astype(F32)).astype(BF16)


def product(left, right, dims):
    return lax.dot_general(left, right, (dims, ((), ())), preferred_element_type=F32)


def product3(left, right, dims):
    left_head, left_tail = left
    right_head, right_tail = right
    left_all = jnp.concatenate([left_head, left_head, left_tail], axis=dims[0][0])
    right_all = jnp.concatenate([right_head, right_tail, right_head], axis=dims[1][0])
    return product(left_all, right_all, dims)


NN = ((1,), (0,))
NT = ((1,), (1,))
TN = ((0,), (0,))


def fill_gains(gains, octant, slot):
    chunk = 32

    def body(step, carry):
        member = step // (128 // chunk)
        top = (step % (128 // chunk)) * chunk
        place = KX * octant + member
        zero_slot = jnp.where(place < 43, 32 * place, 16 + 32 * (place - 43))
        mode_x = jnp.where(slot == 0, zero_slot, slot + 32 * (place - 43))
        lane = lax.broadcasted_iota(jnp.int32, (chunk, 128), 1)
        row = lax.broadcasted_iota(jnp.int32, (chunk, 128), 0) + top
        field = lane // 32
        mode_y = row + 128 * (lane % 32)
        mode_y = jnp.where(mode_y < NG // 2, mode_y, mode_y - NG)
        cutoff = NG // 3
        inside = mode_y * mode_y + mode_x * mode_x <= cutoff * cutoff
        unit = 2.0 * math.pi / NG
        wave_x = mode_x.astype(F32) * unit
        wave_y = mode_y.astype(F32) * unit
        square = wave_x * wave_x + wave_y * wave_y
        scale = 1.0 / NG
        gain = jnp.where(inside, scale / (1.0 + diffusion * square * square), 0.0)
        stiffness = gravity_step * depth_step * square
        below = 1.0 / (1.0 + coriolis * coriolis + stiffness)
        above = (1.0 - coriolis * coriolis - stiffness) * below
        twice = (2.0 * coriolis) * below
        push_u = above * wave_x - twice * wave_y
        push_v = above * wave_y + twice * wave_x
        push_h = (2.0 * gravity_step) * square * below
        sum_u = wave_x + push_u
        sum_v = wave_y + push_v
        curl_u = -wave_y - coriolis * sum_u
        curl_v = wave_x - coriolis * sum_v
        curl_h = -coriolis * push_h
        anchor = square == 0.0
        over = 1.0 / jnp.where(anchor, 1.0, square)
        first = field == 0
        second = field == 1
        third = field == 2
        lead = jnp.where(first, -wave_y, wave_x)
        trail = jnp.where(first, wave_x, wave_y)
        from_u = (lead * curl_u + trail * push_u) * over
        from_v = (lead * curl_v + trail * push_v) * over
        from_h = -(lead * curl_h + trail * push_h) * over
        rotate = 1.0 / (1.0 + coriolis * coriolis)
        keep = (1.0 - coriolis * coriolis) * rotate
        cross = 2.0 * coriolis * rotate
        from_u = jnp.where(anchor, jnp.where(first, keep, -cross), from_u)
        from_v = jnp.where(anchor, jnp.where(first, cross, keep), from_v)
        zero = jnp.zeros_like(gain)
        same = jnp.where(
            first,
            from_u,
            jnp.where(second, from_v, jnp.where(third, 1.0 - depth_step * push_h, 1.0)),
        )
        one = jnp.where(second, from_u, jnp.where(third, -depth_step * sum_v, zero))
        two = jnp.where(first, from_h, jnp.where(third, -depth_step * sum_u, zero))
        three = jnp.where(first, from_v, jnp.where(second, from_h, zero))
        place_rows = pl.ds(pl.multiple_of(top, chunk), chunk)
        gains[member, 0, place_rows, :] = same * gain
        gains[member, 1, place_rows, :] = one * gain
        gains[member, 2, place_rows, :] = two * gain
        gains[member, 3, place_rows, :] = three * gain
        return carry

    lax.fori_loop(0, KX * (128 // chunk), body, 0)


def apply_gains(gains, member, real, imag):
    lane = lax.broadcasted_iota(jnp.int32, (128, 128), 1)
    field = lane // 32
    second = field == 1
    third = field == 2
    gain = gains[member, 0]
    out_real = real * gain
    out_imag = imag * gain
    crossed = [third, None, second]
    for turn in (1, 2, 3):
        gain = gains[member, turn]
        moved_real = pltpu.roll(real, 32 * turn, 1)
        moved_imag = pltpu.roll(imag, 32 * turn, 1)
        swap = crossed[turn - 1]
        if swap is None:
            use_real, use_imag = -moved_imag, moved_real
        else:
            use_real = jnp.where(swap, -moved_imag, moved_real)
            use_imag = jnp.where(swap, moved_real, moved_imag)
        out_real = out_real + gain * use_real
        out_imag = out_imag + gain * use_imag
    return out_real, out_imag


def step_kernel(*refs):
    sources = refs[0:4]
    matrix_source, float_source = refs[4:6]
    results = refs[6:10]
    (
        matrices,
        floats,
        grid_rows,
        head,
        tail,
        slabs,
        landed,
        columns,
        gains,
        returned,
        waves,
        new_rows,
        sem_table,
        sem_rows_out,
        sem_rows_in,
        sem_out,
        sem_in,
        sem_back_out,
        sem_back_in,
        sem_last_out,
        sem_last_in,
        sem_leaders,
        sem_all,
    ) = refs[10:]
    octant = lax.axis_index("gx")
    slot_own = lax.axis_index("gy")
    own = slot_own * GX + octant
    octants = [
        4 * ((octant // 4 + across) % 2) + (octant % 4 + along) % 4
        for across, along in ((1, 2), (1, 1), (1, 3), (0, 2), (1, 0), (0, 1), (0, 3), (0, 0))
    ]
    half_own = slot_own // 8
    level_own = (slot_own // 2) % 4
    core_own = slot_own % 2

    def distance(step):
        turn = step // 2
        odd = step % 2
        far = jnp.where(turn == 3, 0, jnp.where(turn == 2, 3, 2 - turn))
        near = jnp.where(turn == 3, 0, turn + 1)
        return 1 - odd, jnp.where(odd == 1, near, far)

    def slots_at(step):
        half, level = distance(step)
        base = 8 * ((half_own + half) % 2) + 2 * ((level_own + level) % 4)
        return [base + 1 - core_own, base + core_own]

    def slots_before(step):
        half, level = distance(step)
        base = 8 * ((half_own + half) % 2) + 2 * ((level_own + 4 - level) % 4)
        return [base + 1 - core_own, base + core_own]

    barrier = pltpu.get_barrier_semaphore()
    across_own = octant // 4
    for across, along in ((0, 1), (0, 2), (0, 3), (1, 0), (1, 1), (1, 2), (1, 3)):
        other = 4 * ((across_own + across) % 2) + (octant % 4 + along) % 4

        @pl.when(other != 0)
        def greet_member():
            pl.semaphore_signal(
                barrier, inc=1, device_id=(other, slot_own), device_id_type=MESH
            )

    @pl.when(octant == 0)
    def greet_leaders():
        for step in range(1, GY):
            pl.semaphore_signal(
                barrier, inc=1, device_id=(octant, (slot_own + step) % GY), device_id_type=MESH
            )

    table_copies = [
        pltpu.make_async_copy(matrix_source, matrices, sem_table.at[0]),
        pltpu.make_async_copy(float_source, floats, sem_table.at[1]),
    ]
    for copy in table_copies:
        copy.start()
    own_rows = pl.ds(pl.multiple_of(octant * ROWS, ROWS), ROWS)
    for field in range(FIELDS):
        pltpu.make_async_copy(
            sources[field].at[own_rows, :], grid_rows.at[field, octant], sem_rows_in.at[field]
        ).start()

    @pl.when(octant != 0)
    def wait_member():
        pl.semaphore_wait(barrier, GX - 1)

    @pl.when(octant == 1)
    def release_leader():
        pl.semaphore_signal(
            sem_all, inc=1, device_id=(octant - 1, slot_own), device_id_type=MESH
        )

    @pl.when(octant == 0)
    def wait_release():
        pl.semaphore_wait(sem_all, 1)

    for field in range(FIELDS):
        for other in octants[:-1]:
            pltpu.make_async_remote_copy(
                src_ref=sources[field].at[pl.ds(pl.multiple_of(other * ROWS, ROWS), ROWS), :],
                dst_ref=grid_rows.at[field, octant],
                send_sem=sem_rows_out,
                recv_sem=sem_rows_in.at[field],
                device_id=(other, slot_own),
                device_id_type=MESH,
            ).start()

    fill_gains(gains, octant, slot_own)

    @pl.when(octant == 0)
    def tell_members():
        pl.semaphore_wait(barrier, GY - 1)
        for step in range(1, GY):
            pl.semaphore_signal(
                sem_leaders,
                inc=1,
                device_id=(octant, (slot_own + step) % GY),
                device_id_type=MESH,
            )
        pl.semaphore_wait(sem_leaders, GY - 1)
        for other in octants[:-1]:
            pl.semaphore_signal(
                sem_all, inc=1, device_id=(other, slot_own), device_id_type=MESH
            )

    for copy in table_copies:
        copy.wait()

    def row_body(step, carry):
        field = step // 2
        part = step % 2
        top = pl.multiple_of(part * 16, 16)
        chunk = [
            grid_rows[field, c // 4, pl.ds(top, 16), (c % 4) * 128 : (c % 4) * 128 + 128].astype(F32)
            for c in range(32)
        ]
        spectrum = real_transform(chunk)
        rows = pl.ds(pl.multiple_of(step * 16, 16), 16)
        for slot in range(GY):
            if slot == 0:
                real, imag = spectrum[0][0], spectrum[16][0]
            else:
                wave_real, wave_imag = spectrum[slot]
                cosine = floats[32 * slot : 32 * slot + 16, :]
                sine = floats[32 * slot + 16 : 32 * slot + 32, :]
                real = wave_real * cosine + wave_imag * sine
                imag = wave_imag * cosine - wave_real * sine
            for side, value in ((0, real), (128, imag)):
                high, low = parts(value)
                head[slot, rows, side : side + 128] = high
                tail[slot, rows, side : side + 128] = low
        return carry

    for field in range(FIELDS):
        pltpu.make_async_copy(
            grid_rows.at[field], grid_rows.at[field], sem_rows_in.at[field]
        ).wait()
        lax.fori_loop(2 * field, 2 * field + 2, row_body, 0)

    @pl.when(octant != 0)
    def wait_all():
        pl.semaphore_wait(sem_all, 1)

    sides = (pl.ds(0, FIRST // 8), pl.ds(FIRST // 8, (SLAB - FIRST) // 8))

    def send_slot(side, slot, others, target, out_sem, in_sem):
        for other in others:
            pltpu.make_async_remote_copy(
                src_ref=slabs.at[slot * GX + other, sides[side]],
                dst_ref=target.at[own, sides[side]],
                send_sem=out_sem.at[side],
                recv_sem=in_sem.at[side, slot_own // 2],
                device_id=(other, slot),
                device_id_type=MESH,
            ).start()

    def keep_own(side, target, in_sem):
        pltpu.make_async_copy(
            slabs.at[own, sides[side]],
            target.at[own, sides[side]],
            in_sem.at[side, slot_own // 2],
        ).start()

    def wait_group(side, slots, target, in_sem):
        couple = slots[0] // 2
        group = target.at[pl.ds(couple * (2 * GX), 2 * GX), sides[side]]
        pltpu.make_async_copy(group, group, in_sem.at[side, couple]).wait()

    def wait_sent(side, out_sem):
        sent = slabs.at[pl.ds(0, DEVICES - 1), sides[side]]
        pltpu.make_async_copy(sent, sent, out_sem.at[side]).wait()

    def slot_products(slots):
        loaded = [
            (matrix_pair(matrices, FWD_AT, jnp.minimum(slot, 1)), (head[slot], tail[slot]))
            for slot in slots
        ]
        codes = []
        for left, right in loaded:
            spectrum = product3(left, right, NT).reshape(GX, SLAB, 128)
            codes.append([encode(spectrum[:, :FIRST]), encode(spectrum[:, FIRST:])])
        for slot, pieces in zip(slots, codes):
            for side in range(2):
                slabs[pl.ds(slot * GX, GX), sides[side]] = pieces[side]

    steps = GY // 2

    def slot_body(step, carry):
        slots = slots_at(2 * step) + slots_at(2 * step + 1)
        slot_products(slots)
        for slot in slots:
            send_slot(0, slot, octants, landed, sem_out, sem_in)
        return carry

    lax.fori_loop(0, steps // 2 - 1, slot_body, 0)
    twin = slots_at(steps - 1)[0]
    nearby = slots_at(steps - 2)
    slot_products(nearby + [twin, slot_own])
    for slot in nearby:
        send_slot(0, slot, octants, landed, sem_out, sem_in)
    send_slot(0, twin, octants, landed, sem_out, sem_in)
    send_slot(0, slot_own, octants[:-1], landed, sem_out, sem_in)
    keep_own(0, landed, sem_in)

    def second_body(step, carry):
        for slot in slots_at(step):
            send_slot(1, slot, octants, landed, sem_out, sem_in)
        return carry

    lax.fori_loop(0, steps - 1, second_body, 0)
    send_slot(1, twin, octants, landed, sem_out, sem_in)
    send_slot(1, slot_own, octants[:-1], landed, sem_out, sem_in)
    keep_own(1, landed, sem_in)

    def spread(side):
        first = 0 if side == 0 else FIRST
        count = FIRST if side == 0 else SLAB - FIRST

        def body(step, carry):
            slots = slots_before(step)
            wait_group(side, slots, landed, sem_in)
            for slot in slots:
                values = decode(landed[pl.ds(slot * GX, GX), sides[side]])
                for source in range(GX):
                    columns[
                        pl.ds(first * PLANE + slot * GX + source, count, stride=PLANE), :
                    ] = values[source]
            return carry

        return body

    def plane(row):
        return slice(row * 128, row * 128 + 128)

    def column_rows(row):
        return slice(row * PLANE, row * PLANE + 128)

    def stack_pair(reals, imags):
        return jnp.concatenate(
            [jnp.concatenate(reals, axis=1), jnp.concatenate(imags, axis=1)], axis=0
        )

    def work_columns(groups):
        members = [member for group in groups for member in group]
        cosine = floats[SPIN_AT : SPIN_AT + 128, :]
        sine = floats[SPIN_AT + 128 : SPIN_AT + 256, :]
        loaded = [
            stack_pair(
                [columns[column_rows(REAL_ROWS[member]), :] for member in group],
                [columns[column_rows(IMAG_ROWS[member]), :] for member in group],
            )
            for group in groups
        ]
        turned = []
        for group, values in zip(groups, loaded):
            mixed = product3(square_pair(matrices, 0), parts(values), NN)
            for index in range(len(group)):
                real, imag = mixed[:128, plane(index)], mixed[128:, plane(index)]
                turned.append(
                    jnp.concatenate(
                        [real * cosine + imag * sine, imag * cosine - real * sine], axis=1
                    )
                )
        modes = product3(
            parts(jnp.concatenate(turned, axis=0)), square_pair(matrices, 2), NN
        )
        changed = []
        for index, member in enumerate(members):
            piece = modes[plane(index)]
            real, imag = apply_gains(gains, member, piece[:, :128], piece[:, 128:])
            changed.append(jnp.concatenate([real, imag], axis=1))
        mixed = product3(
            parts(jnp.concatenate(changed, axis=0)), square_pair(matrices, 3), NN
        )
        start = 0
        done = []
        for group in groups:
            reals, imags = [], []
            for index in range(start, start + len(group)):
                piece = mixed[plane(index)]
                real, imag = piece[:, :128], piece[:, 128:]
                reals.append(real * cosine - imag * sine)
                imags.append(imag * cosine + real * sine)
            start += len(group)
            done.append(
                product3(square_pair(matrices, 1), parts(stack_pair(reals, imags)), NN)
            )
        for group, values in zip(groups, done):
            for index, member in enumerate(group):
                columns[column_rows(REAL_ROWS[member]), :] = values[:128, plane(index)]
                columns[column_rows(IMAG_ROWS[member]), :] = values[128:, plane(index)]

    def collect(side, slots):
        first = 0 if side == 0 else FIRST
        count = FIRST if side == 0 else SLAB - FIRST
        codes = [
            encode(
                jnp.stack(
                    [
                        columns[
                            pl.ds(first * PLANE + slot * GX + source, count, stride=PLANE), :
                        ]
                        for source in range(GX)
                    ]
                )
            )
            for slot in slots
        ]
        for slot, code in zip(slots, codes):
            slabs[pl.ds(slot * GX, GX), sides[side]] = code

    def send_back(side):
        def body(step, carry):
            slots = slots_at(step)
            collect(side, slots)
            for slot in slots:
                send_slot(side, slot, octants, returned, sem_back_out, sem_back_in)
            return carry

        wait_sent(side, sem_out)
        lax.fori_loop(0, steps - 1, body, 0)
        collect(side, [twin, slot_own])
        send_slot(side, twin, octants, returned, sem_back_out, sem_back_in)
        send_slot(side, slot_own, octants[:-1], returned, sem_back_out, sem_back_in)
        keep_own(side, returned, sem_back_in)

    lax.fori_loop(0, steps, spread(0), 0)
    columns[column_rows(FIRST - 1), :] = jnp.zeros((128, 128), F32)
    work_columns([(0, 1), (2, 3), (4, 5)])
    lax.fori_loop(0, steps, spread(1), 0)
    columns[column_rows(SLAB - 1), :] = jnp.zeros((128, 128), F32)
    work_columns([(6, 7)])
    send_back(0)
    work_columns([(8, 9), (10,)])
    send_back(1)

    def wave_part(side, slots):
        start = INV_AT if side == 0 else INV_AT + GX * FIRST
        count = GX * FIRST if side == 0 else GX * (SLAB - FIRST)
        loaded = [
            (
                returned[pl.ds(slot * GX, GX), sides[side]],
                matrix_pair(matrices, start, jnp.minimum(slot, 1), count),
            )
            for slot in slots
        ]
        return [
            product3(parts(decode(codes).reshape(count, 128)), right, TN)
            for codes, right in loaded
        ]

    def first_wave(step, carry):
        slots = []
        for index in (2 * step, 2 * step + 1):
            couple = slots_before(index)
            wait_group(0, couple, returned, sem_back_in)
            slots.extend(couple)
        for slot, values in zip(slots, wave_part(0, slots)):
            waves[slot] = values
        return carry

    def second_wave(step, carry):
        slots = []
        for index in (2 * step, 2 * step + 1):
            couple = slots_before(index)
            wait_group(1, couple, returned, sem_back_in)
            slots.extend(couple)
        before = [waves[slot] for slot in slots]
        done = []
        for slot, values, base in zip(slots, wave_part(1, slots), before):
            values = values + base
            cosine = floats[pl.ds(32 * slot, 1), :]
            sine = floats[pl.ds(32 * slot + 16, 1), :]
            real, imag = values[:, :128], values[:, 128:]
            done.append((real * cosine - imag * sine, imag * cosine + real * sine))
        for slot, (real, imag) in zip(slots, done):
            waves[slot, :, 0:128] = real
            waves[slot, :, 128:256] = imag
        return carry

    lax.fori_loop(0, steps // 2, first_wave, 0)
    lax.fori_loop(0, steps // 2, second_wave, 0)

    def grid_body(step, carry):
        field = step // 2
        part = step % 2
        rows = pl.ds(pl.multiple_of(step * 16, 16), 16)
        spectrum = [(waves[0, rows, 0:128], None)]
        for slot in range(1, GY):
            spectrum.append((waves[slot, rows, 0:128], waves[slot, rows, 128:256]))
        spectrum.append((waves[0, rows, 128:256], None))
        values = real_inverse(spectrum)
        top = pl.ds(pl.multiple_of(part * 16, 16), 16)
        for c in range(32):
            new_rows[field, c // 4, top, (c % 4) * 128 : (c % 4) * 128 + 128] = values[c].astype(BF16)
        return carry

    for field in range(FIELDS):
        lax.fori_loop(2 * field, 2 * field + 2, grid_body, 0)
        for other in octants[:-1]:
            pltpu.make_async_remote_copy(
                src_ref=new_rows.at[field, other],
                dst_ref=results[field].at[own_rows, :],
                send_sem=sem_last_out,
                recv_sem=sem_last_in.at[field],
                device_id=(other, slot_own),
                device_id_type=MESH,
            ).start()
        pltpu.make_async_copy(
            new_rows.at[field, octant], results[field].at[own_rows, :], sem_last_in.at[field]
        ).start()

    for side in range(2):
        wait_sent(side, sem_back_out)
    moved = new_rows.at[:, pl.ds(0, GX - 1)]
    pltpu.make_async_copy(moved, moved, sem_rows_out).wait()
    pltpu.make_async_copy(moved, moved, sem_last_out).wait()
    for field in range(FIELDS):
        pltpu.make_async_copy(results[field], results[field], sem_last_in.at[field]).wait()


def place_kernel(*refs):
    copies = [
        pltpu.make_async_copy(refs[field], refs[FIELDS + field], refs[2 * FIELDS].at[field])
        for field in range(FIELDS)
    ]
    for copy in copies:
        copy.start()
    for copy in copies:
        copy.wait()


def per_device(east_wind, north_wind, height, tracer):
    constants = [jnp.asarray(value) for value in tables()]
    anywhere = pl.BlockSpec(memory_space=pl.ANY)
    block = jax.ShapeDtypeStruct((NG // GY, COLS), BF16)
    dma = pltpu.SemaphoreType.DMA
    landed = pl.pallas_call(
        step_kernel,
        out_shape=(block,) * 4,
        in_specs=[pl.BlockSpec(memory_space=pltpu.HBM)] * 6,
        out_specs=(anywhere,) * 4,
        scratch_shapes=[
            pltpu.VMEM((MATRIX_ROWS, 256), BF16),
            pltpu.VMEM((FLOAT_ROWS, 128), F32),
            pltpu.VMEM((FIELDS, GX, ROWS, COLS), BF16),
            pltpu.VMEM((GY, 128, 256), BF16),
            pltpu.VMEM((GY, 128, 256), BF16),
            pltpu.VMEM((DEVICES, SLAB // 8, 8, 128), BF16),
            pltpu.VMEM((DEVICES, SLAB // 8, 8, 128), BF16),
            pltpu.VMEM(((SLAB + 1) * PLANE, 128), F32),
            pltpu.VMEM((KX, 4, 128, 128), F32),
            pltpu.VMEM((DEVICES, SLAB // 8, 8, 128), BF16),
            pltpu.VMEM((GY, 128, 256), F32),
            pltpu.VMEM((FIELDS, GX, ROWS, COLS), BF16),
            dma((2,)),
            dma,
            dma((FIELDS,)),
            dma((2,)),
            dma((2, GY // 2)),
            dma((2,)),
            dma((2, GY // 2)),
            dma,
            dma((FIELDS,)),
            pltpu.SemaphoreType.REGULAR,
            pltpu.SemaphoreType.REGULAR,
        ],
        compiler_params=pltpu.CompilerParams(
            collective_id=0, has_side_effects=True, vmem_limit_bytes=32 * 1024 * 1024
        ),
    )(*[
        pltpu.with_memory_space_constraint(value, pltpu.HBM)
        for value in (east_wind, north_wind, height, tracer, *constants)
    ])
    return pl.pallas_call(
        place_kernel,
        out_shape=(block,) * 4,
        in_specs=[anywhere] * 4,
        out_specs=(pl.BlockSpec(memory_space=pltpu.HBM),) * 4,
        scratch_shapes=[dma((FIELDS,))],
        compiler_params=pltpu.CompilerParams(vmem_limit_bytes=1024 * 1024),
    )(*landed)


def solution(mesh):
    placed = (P("gy", "gx"),) * 4
    return jax.shard_map(
        per_device, mesh=mesh, in_specs=placed, out_specs=placed, check_vma=False
    )
```

```python
import math

import jax
import jax.numpy as jnp
import numpy as np
from jax import lax
from jax.experimental import pallas as pl
from jax.experimental.pallas import tpu as pltpu
from jax.sharding import PartitionSpec as P

NG = 4096
FIELDS = 4
GX = 8
GY = 16
DEVICES = GX * GY
KX = 11
SLAB = 24
FIRST = 16
PLANE = 136
REAL_ROWS = (0, 1, 2, 3, 4, 5, 6, 7, 17, 18, 19)
IMAG_ROWS = (8, 9, 10, 11, 12, 13, 14, 16, 20, 21, 22)
ROWS = 32
COLS = 512
POWER = 17
PEAK = 128.0

coriolis = 0.25
gravity_step = 2.0
depth_step = 2.0
diffusion = 0.02

F32 = jnp.float32
BF16 = jnp.bfloat16
MESH = pl.DeviceIdType.MESH


def split_const(matrix):
    whole = matrix.astype(np.float32)
    high = np.dtype(jnp.bfloat16)
    head = whole.astype(high)
    tail = (whole - head.astype(np.float32)).astype(high)
    return head, tail


def wave_of(slot, place):
    if slot == 0:
        return 32 * place if place < 43 else 16 + 32 * (place - 43)
    return slot + 32 * (place - 43)


def tables():
    turn = 2.0 * np.pi
    lane = np.arange(128)
    forward = np.zeros((2, GX, SLAB, 256))
    inverse = np.zeros((2, GX, SLAB, 256))
    for place in range(86):
        octant, member = place // KX, place % KX
        real_row, imag_row = REAL_ROWS[member], IMAG_ROWS[member]
        low = place - 43
        cosine, sine = np.cos(turn * lane * low / 128), np.sin(turn * lane * low / 128)
        forward[1, octant, real_row] = np.concatenate([cosine, sine])
        forward[1, octant, imag_row] = np.concatenate([-sine, cosine])
        inverse[1, octant, real_row] = np.concatenate([cosine, sine])
        inverse[1, octant, imag_row] = np.concatenate([-sine, cosine])
        wave = wave_of(0, place)
        cosine, sine = np.cos(turn * lane * wave / NG), np.sin(turn * lane * wave / NG)
        half = 0 if place < 43 else 128
        weight = 1.0 if wave == 0 else 2.0
        forward[0, octant, real_row, half : half + 128] = cosine
        forward[0, octant, imag_row, half : half + 128] = -sine
        inverse[0, octant, real_row, half : half + 128] = weight * cosine
        inverse[0, octant, imag_row, half : half + 128] = -weight * sine
    forward = forward.reshape(2, GX * SLAB, 256)
    inverse = np.concatenate(
        [
            inverse[:, :, :FIRST].reshape(2, GX * FIRST, 256),
            inverse[:, :, FIRST:].reshape(2, GX * (SLAB - FIRST), 256),
        ],
        axis=1,
    )
    angle = turn * np.outer(np.arange(GY), lane) / NG
    twist = np.stack([np.cos(angle), np.sin(angle)], axis=1)[:, :, None, :]
    twist = np.broadcast_to(twist, (GY, 2, 16, 128)).astype(np.float32)
    angle = turn * np.outer(lane, lane) / 128
    cosine, sine = np.cos(angle), np.sin(angle)
    gather = np.block([[cosine, sine], [-sine, cosine]])
    scatter = np.block([[cosine, -sine], [sine, cosine]])
    angle = turn * np.outer(np.arange(ROWS), np.arange(ROWS)) / ROWS
    cosine, sine = np.kron(np.eye(4), np.cos(angle)), np.kron(np.eye(4), np.sin(angle))
    fan_in = np.block([[cosine, -sine], [sine, cosine]])
    fan_out = np.block([[cosine, sine], [-sine, cosine]])
    angle = turn * np.outer(lane, lane % ROWS) / NG
    spin = np.stack([np.cos(angle), np.sin(angle)]).astype(np.float32)
    pieces = []
    for matrix in (forward.reshape(-1, 256), inverse.reshape(-1, 256) / NG, gather, scatter, fan_in, fan_out):
        pieces.extend(split_const(matrix))
    floats = np.concatenate([twist.reshape(-1, 128), spin.reshape(-1, 128)], axis=0)
    return np.concatenate(pieces, axis=0), floats


FWD_AT = 0
INV_AT = 4 * GX * SLAB
SQUARE_AT = 8 * GX * SLAB
MATRIX_ROWS = SQUARE_AT + 8 * 256
SPIN_AT = GY * 2 * 16
FLOAT_ROWS = SPIN_AT + 256


def matrix_pair(matrices, start, which, count=GX * SLAB):
    first = pl.multiple_of(start + which * (GX * SLAB), 64)
    second = pl.multiple_of(start + (which + 2) * (GX * SLAB), 64)
    return matrices[pl.ds(first, count), :], matrices[pl.ds(second, count), :]


def square_pair(matrices, which):
    first = SQUARE_AT + which * 512
    return matrices[first : first + 256, :], matrices[first + 256 : first + 512, :]


def encode(values):
    rows = values.shape[1]
    largest = jnp.max(jnp.abs(values), axis=1, keepdims=True)
    scale = (jnp.maximum(largest, 1e-34) * 1.01).astype(BF16).astype(F32)
    level = values * (PEAK / scale)
    second = level * level
    fourth = second * second
    eighth = fourth * fourth
    code = eighth * eighth * level
    ending = code[:, rows - 8 :]
    last = lax.broadcasted_iota(jnp.int32, ending.shape, 1) == 7
    ending = jnp.where(last, scale, ending)
    code = jnp.concatenate([code[:, : rows - 8], ending], axis=1) if rows > 8 else ending
    return code.reshape(values.shape[0], rows // 8, 8, 128).astype(BF16)


def decode(codes):
    rows = codes.shape[1] * 8
    code = codes.astype(F32).reshape(codes.shape[0], rows, 128)
    scale = code[:, rows - 1 : rows, :] * (1.0 / PEAK)
    size = jnp.maximum(jnp.abs(code), 2.0**-126)
    return jnp.exp2(jnp.log2(size) * (1.0 / POWER - 1.0)) * (code * scale)


def real_transform(values):
    count = len(values)
    if count == 2:
        return [(values[0] + values[1], None), (values[0] - values[1], None)]
    even = real_transform(values[0::2])
    odd = real_transform(values[1::2])
    half = count // 2
    result = [None] * (half + 1)
    for index in range(count // 4 + 1):
        even_real, even_imag = even[index]
        odd_real, odd_imag = odd[index]
        if index == 0:
            result[0] = (even_real + odd_real, None)
            result[half] = (even_real - odd_real, None)
        elif index == count // 4:
            result[index] = (even_real, -odd_real)
        else:
            cosine = math.cos(2.0 * math.pi * index / count)
            sine = math.sin(2.0 * math.pi * index / count)
            turned_real = odd_real * cosine + odd_imag * sine
            turned_imag = odd_imag * cosine - odd_real * sine
            result[index] = (even_real + turned_real, even_imag + turned_imag)
            result[half - index] = (even_real - turned_real, turned_imag - even_imag)
    return result


def real_inverse(waves):
    half = len(waves) - 1
    count = 2 * half
    if count == 2:
        return [waves[0][0] + waves[1][0], waves[0][0] - waves[1][0]]
    even = []
    odd = []
    for index in range(count // 4 + 1):
        real, imag = waves[index]
        other_real, other_imag = waves[half - index]
        if index == 0:
            even.append((real + other_real, None))
            odd.append((real - other_real, None))
        elif index == count // 4:
            even.append((real + real, None))
            odd.append((-(imag + imag), None))
        else:
            cosine = math.cos(2.0 * math.pi * index / count)
            sine = math.sin(2.0 * math.pi * index / count)
            even.append((real + other_real, imag - other_imag))
            gap_real = real - other_real
            gap_imag = imag + other_imag
            odd.append((gap_real * cosine - gap_imag * sine, gap_real * sine + gap_imag * cosine))
    outputs = [None] * count
    outputs[0::2] = real_inverse(even)
    outputs[1::2] = real_inverse(odd)
    return outputs


def parts(values):
    head = values.astype(BF16)
    return head, (values - head.astype(F32)).astype(BF16)


def product(left, right, dims):
    return lax.dot_general(left, right, (dims, ((), ())), preferred_element_type=F32)


def product3(left, right, dims):
    left_head, left_tail = left
    right_head, right_tail = right
    left_all = jnp.concatenate([left_head, left_head, left_tail], axis=dims[0][0])
    right_all = jnp.concatenate([right_head, right_tail, right_head], axis=dims[1][0])
    return product(left_all, right_all, dims)


NN = ((1,), (0,))
NT = ((1,), (1,))
TN = ((0,), (0,))


def fill_gains(gains, octant, slot):
    chunk = 32

    def body(step, carry):
        member = step // (128 // chunk)
        top = (step % (128 // chunk)) * chunk
        place = KX * octant + member
        zero_slot = jnp.where(place < 43, 32 * place, 16 + 32 * (place - 43))
        mode_x = jnp.where(slot == 0, zero_slot, slot + 32 * (place - 43))
        lane = lax.broadcasted_iota(jnp.int32, (chunk, 128), 1)
        row = lax.broadcasted_iota(jnp.int32, (chunk, 128), 0) + top
        field = lane // 32
        mode_y = row + 128 * (lane % 32)
        mode_y = jnp.where(mode_y < NG // 2, mode_y, mode_y - NG)
        cutoff = NG // 3
        inside = mode_y * mode_y + mode_x * mode_x <= cutoff * cutoff
        unit = 2.0 * math.pi / NG
        wave_x = mode_x.astype(F32) * unit
        wave_y = mode_y.astype(F32) * unit
        square = wave_x * wave_x + wave_y * wave_y
        scale = 1.0 / NG
        gain = jnp.where(inside, scale / (1.0 + diffusion * square * square), 0.0)
        stiffness = gravity_step * depth_step * square
        below = 1.0 / (1.0 + coriolis * coriolis + stiffness)
        above = (1.0 - coriolis * coriolis - stiffness) * below
        twice = (2.0 * coriolis) * below
        push_u = above * wave_x - twice * wave_y
        push_v = above * wave_y + twice * wave_x
        push_h = (2.0 * gravity_step) * square * below
        sum_u = wave_x + push_u
        sum_v = wave_y + push_v
        curl_u = -wave_y - coriolis * sum_u
        curl_v = wave_x - coriolis * sum_v
        curl_h = -coriolis * push_h
        anchor = square == 0.0
        over = 1.0 / jnp.where(anchor, 1.0, square)
        first = field == 0
        second = field == 1
        third = field == 2
        lead = jnp.where(first, -wave_y, wave_x)
        trail = jnp.where(first, wave_x, wave_y)
        from_u = (lead * curl_u + trail * push_u) * over
        from_v = (lead * curl_v + trail * push_v) * over
        from_h = -(lead * curl_h + trail * push_h) * over
        rotate = 1.0 / (1.0 + coriolis * coriolis)
        keep = (1.0 - coriolis * coriolis) * rotate
        cross = 2.0 * coriolis * rotate
        from_u = jnp.where(anchor, jnp.where(first, keep, -cross), from_u)
        from_v = jnp.where(anchor, jnp.where(first, cross, keep), from_v)
        zero = jnp.zeros_like(gain)
        same = jnp.where(
            first,
            from_u,
            jnp.where(second, from_v, jnp.where(third, 1.0 - depth_step * push_h, 1.0)),
        )
        one = jnp.where(second, from_u, jnp.where(third, -depth_step * sum_v, zero))
        two = jnp.where(first, from_h, jnp.where(third, -depth_step * sum_u, zero))
        three = jnp.where(first, from_v, jnp.where(second, from_h, zero))
        place_rows = pl.ds(pl.multiple_of(top, chunk), chunk)
        gains[member, 0, place_rows, :] = same * gain
        gains[member, 1, place_rows, :] = one * gain
        gains[member, 2, place_rows, :] = two * gain
        gains[member, 3, place_rows, :] = three * gain
        return carry

    lax.fori_loop(0, KX * (128 // chunk), body, 0)


def apply_gains(gains, member, real, imag):
    lane = lax.broadcasted_iota(jnp.int32, (128, 128), 1)
    field = lane // 32
    second = field == 1
    third = field == 2
    gain = gains[member, 0]
    out_real = real * gain
    out_imag = imag * gain
    crossed = [third, None, second]
    for turn in (1, 2, 3):
        gain = gains[member, turn]
        moved_real = pltpu.roll(real, 32 * turn, 1)
        moved_imag = pltpu.roll(imag, 32 * turn, 1)
        swap = crossed[turn - 1]
        if swap is None:
            use_real, use_imag = -moved_imag, moved_real
        else:
            use_real = jnp.where(swap, -moved_imag, moved_real)
            use_imag = jnp.where(swap, moved_real, moved_imag)
        out_real = out_real + gain * use_real
        out_imag = out_imag + gain * use_imag
    return out_real, out_imag


def step_kernel(*refs):
    sources = refs[0:4]
    matrix_source, float_source = refs[4:6]
    results = refs[6:10]
    (
        matrices,
        floats,
        grid_rows,
        head,
        tail,
        slabs,
        landed,
        columns,
        gains,
        returned,
        waves,
        new_rows,
        sem_table,
        sem_rows_out,
        sem_rows_in,
        sem_out,
        sem_in,
        sem_back_out,
        sem_back_in,
        sem_last_out,
        sem_last_in,
        sem_leaders,
        sem_all,
    ) = refs[10:]
    octant = lax.axis_index("gx")
    slot_own = lax.axis_index("gy")
    own = slot_own * GX + octant
    octants = [
        4 * ((octant // 4 + across) % 2) + (octant % 4 + along) % 4
        for across, along in ((1, 2), (1, 1), (1, 3), (0, 2), (1, 0), (0, 1), (0, 3), (0, 0))
    ]
    half_own = slot_own // 8
    level_own = (slot_own // 2) % 4
    core_own = slot_own % 2

    def distance(step):
        turn = step // 2
        odd = step % 2
        far = jnp.where(turn == 3, 0, jnp.where(turn == 2, 3, 2 - turn))
        near = jnp.where(turn == 3, 0, turn + 1)
        return 1 - odd, jnp.where(odd == 1, near, far)

    def slots_at(step):
        half, level = distance(step)
        base = 8 * ((half_own + half) % 2) + 2 * ((level_own + level) % 4)
        return [base + 1 - core_own, base + core_own]

    def slots_before(step):
        half, level = distance(step)
        base = 8 * ((half_own + half) % 2) + 2 * ((level_own + 4 - level) % 4)
        return [base + 1 - core_own, base + core_own]

    barrier = pltpu.get_barrier_semaphore()
    across_own = octant // 4
    for across, along in ((0, 1), (0, 2), (0, 3), (1, 0), (1, 1), (1, 2), (1, 3)):
        other = 4 * ((across_own + across) % 2) + (octant % 4 + along) % 4

        @pl.when(other != 0)
        def greet_member():
            pl.semaphore_signal(
                barrier, inc=1, device_id=(other, slot_own), device_id_type=MESH
            )

    @pl.when(octant == 0)
    def greet_leaders():
        for step in range(1, GY):
            pl.semaphore_signal(
                barrier, inc=1, device_id=(octant, (slot_own + step) % GY), device_id_type=MESH
            )

    table_copies = [
        pltpu.make_async_copy(matrix_source, matrices, sem_table.at[0]),
        pltpu.make_async_copy(float_source, floats, sem_table.at[1]),
    ]
    for copy in table_copies:
        copy.start()
    own_rows = pl.ds(pl.multiple_of(octant * ROWS, ROWS), ROWS)
    for field in range(FIELDS):
        pltpu.make_async_copy(
            sources[field].at[own_rows, :], grid_rows.at[field, octant], sem_rows_in.at[field]
        ).start()

    @pl.when(octant != 0)
    def wait_member():
        pl.semaphore_wait(barrier, GX - 1)

    @pl.when(octant == 1)
    def release_leader():
        pl.semaphore_signal(
            sem_all, inc=1, device_id=(octant - 1, slot_own), device_id_type=MESH
        )

    @pl.when(octant == 0)
    def wait_release():
        pl.semaphore_wait(sem_all, 1)

    for field in range(FIELDS):
        for other in octants[:-1]:
            pltpu.make_async_remote_copy(
                src_ref=sources[field].at[pl.ds(pl.multiple_of(other * ROWS, ROWS), ROWS), :],
                dst_ref=grid_rows.at[field, octant],
                send_sem=sem_rows_out,
                recv_sem=sem_rows_in.at[field],
                device_id=(other, slot_own),
                device_id_type=MESH,
            ).start()

    fill_gains(gains, octant, slot_own)

    @pl.when(octant == 0)
    def tell_members():
        pl.semaphore_wait(barrier, GY - 1)
        for step in range(1, GY):
            pl.semaphore_signal(
                sem_leaders,
                inc=1,
                device_id=(octant, (slot_own + step) % GY),
                device_id_type=MESH,
            )
        pl.semaphore_wait(sem_leaders, GY - 1)
        for other in octants[:-1]:
            pl.semaphore_signal(
                sem_all, inc=1, device_id=(other, slot_own), device_id_type=MESH
            )

    for copy in table_copies:
        copy.wait()

    def row_body(step, carry):
        field = step // 2
        part = step % 2
        top = pl.multiple_of(part * 16, 16)
        chunk = [
            grid_rows[field, c // 4, pl.ds(top, 16), (c % 4) * 128 : (c % 4) * 128 + 128].astype(F32)
            for c in range(32)
        ]
        spectrum = real_transform(chunk)
        rows = pl.ds(pl.multiple_of(step * 16, 16), 16)
        for slot in range(GY):
            if slot == 0:
                real, imag = spectrum[0][0], spectrum[16][0]
            else:
                wave_real, wave_imag = spectrum[slot]
                cosine = floats[32 * slot : 32 * slot + 16, :]
                sine = floats[32 * slot + 16 : 32 * slot + 32, :]
                real = wave_real * cosine + wave_imag * sine
                imag = wave_imag * cosine - wave_real * sine
            for side, value in ((0, real), (128, imag)):
                high, low = parts(value)
                head[slot, rows, side : side + 128] = high
                tail[slot, rows, side : side + 128] = low
        return carry

    for field in range(FIELDS):
        pltpu.make_async_copy(
            grid_rows.at[field], grid_rows.at[field], sem_rows_in.at[field]
        ).wait()
        lax.fori_loop(2 * field, 2 * field + 2, row_body, 0)

    @pl.when(octant != 0)
    def wait_all():
        pl.semaphore_wait(sem_all, 1)

    sides = (pl.ds(0, FIRST // 8), pl.ds(FIRST // 8, (SLAB - FIRST) // 8))

    def send_slot(side, slot, others, target, out_sem, in_sem):
        for other in others:
            pltpu.make_async_remote_copy(
                src_ref=slabs.at[slot * GX + other, sides[side]],
                dst_ref=target.at[own, sides[side]],
                send_sem=out_sem.at[side],
                recv_sem=in_sem.at[side, slot_own // 2],
                device_id=(other, slot),
                device_id_type=MESH,
            ).start()

    def keep_own(side, target, in_sem):
        pltpu.make_async_copy(
            slabs.at[own, sides[side]],
            target.at[own, sides[side]],
            in_sem.at[side, slot_own // 2],
        ).start()

    def wait_group(side, slots, target, in_sem):
        couple = slots[0] // 2
        group = target.at[pl.ds(couple * (2 * GX), 2 * GX), sides[side]]
        pltpu.make_async_copy(group, group, in_sem.at[side, couple]).wait()

    def wait_sent(side, out_sem):
        sent = slabs.at[pl.ds(0, DEVICES - 1), sides[side]]
        pltpu.make_async_copy(sent, sent, out_sem.at[side]).wait()

    def slot_products(slots):
        loaded = [
            (matrix_pair(matrices, FWD_AT, jnp.minimum(slot, 1)), (head[slot], tail[slot]))
            for slot in slots
        ]
        codes = []
        for left, right in loaded:
            spectrum = product3(left, right, NT).reshape(GX, SLAB, 128)
            codes.append([encode(spectrum[:, :FIRST]), encode(spectrum[:, FIRST:])])
        for slot, pieces in zip(slots, codes):
            for side in range(2):
                slabs[pl.ds(slot * GX, GX), sides[side]] = pieces[side]

    steps = GY // 2

    def slot_body(step, carry):
        slots = slots_at(2 * step) + slots_at(2 * step + 1)
        slot_products(slots)
        for slot in slots:
            send_slot(0, slot, octants, landed, sem_out, sem_in)
        return carry

    lax.fori_loop(0, steps // 2 - 1, slot_body, 0)
    twin = slots_at(steps - 1)[0]
    nearby = slots_at(steps - 2)
    slot_products(nearby + [twin, slot_own])
    for slot in nearby:
        send_slot(0, slot, octants, landed, sem_out, sem_in)
    send_slot(0, twin, octants, landed, sem_out, sem_in)
    send_slot(0, slot_own, octants[:-1], landed, sem_out, sem_in)
    keep_own(0, landed, sem_in)

    def second_body(step, carry):
        for slot in slots_at(step):
            send_slot(1, slot, octants, landed, sem_out, sem_in)
        return carry

    lax.fori_loop(0, steps - 1, second_body, 0)
    send_slot(1, twin, octants, landed, sem_out, sem_in)
    send_slot(1, slot_own, octants[:-1], landed, sem_out, sem_in)
    keep_own(1, landed, sem_in)

    def spread(side):
        first = 0 if side == 0 else FIRST
        count = FIRST if side == 0 else SLAB - FIRST

        def body(step, carry):
            slots = slots_before(step)
            wait_group(side, slots, landed, sem_in)
            for slot in slots:
                values = decode(landed[pl.ds(slot * GX, GX), sides[side]])
                for source in range(GX):
                    columns[
                        pl.ds(first * PLANE + slot * GX + source, count, stride=PLANE), :
                    ] = values[source]
            return carry

        return body

    def plane(row):
        return slice(row * 128, row * 128 + 128)

    def column_rows(row):
        return slice(row * PLANE, row * PLANE + 128)

    def stack_pair(reals, imags):
        return jnp.concatenate(
            [jnp.concatenate(reals, axis=1), jnp.concatenate(imags, axis=1)], axis=0
        )

    def work_columns(groups):
        members = [member for group in groups for member in group]
        cosine = floats[SPIN_AT : SPIN_AT + 128, :]
        sine = floats[SPIN_AT + 128 : SPIN_AT + 256, :]
        loaded = [
            stack_pair(
                [columns[column_rows(REAL_ROWS[member]), :] for member in group],
                [columns[column_rows(IMAG_ROWS[member]), :] for member in group],
            )
            for group in groups
        ]
        turned = []
        for group, values in zip(groups, loaded):
            mixed = product3(square_pair(matrices, 0), parts(values), NN)
            for index in range(len(group)):
                real, imag = mixed[:128, plane(index)], mixed[128:, plane(index)]
                turned.append(
                    jnp.concatenate(
                        [real * cosine + imag * sine, imag * cosine - real * sine], axis=1
                    )
                )
        modes = product3(
            parts(jnp.concatenate(turned, axis=0)), square_pair(matrices, 2), NN
        )
        changed = []
        for index, member in enumerate(members):
            piece = modes[plane(index)]
            real, imag = apply_gains(gains, member, piece[:, :128], piece[:, 128:])
            changed.append(jnp.concatenate([real, imag], axis=1))
        mixed = product3(
            parts(jnp.concatenate(changed, axis=0)), square_pair(matrices, 3), NN
        )
        start = 0
        done = []
        for group in groups:
            reals, imags = [], []
            for index in range(start, start + len(group)):
                piece = mixed[plane(index)]
                real, imag = piece[:, :128], piece[:, 128:]
                reals.append(real * cosine - imag * sine)
                imags.append(imag * cosine + real * sine)
            start += len(group)
            done.append(
                product3(square_pair(matrices, 1), parts(stack_pair(reals, imags)), NN)
            )
        for group, values in zip(groups, done):
            for index, member in enumerate(group):
                columns[column_rows(REAL_ROWS[member]), :] = values[:128, plane(index)]
                columns[column_rows(IMAG_ROWS[member]), :] = values[128:, plane(index)]

    def collect(side, slots):
        first = 0 if side == 0 else FIRST
        count = FIRST if side == 0 else SLAB - FIRST
        codes = [
            encode(
                jnp.stack(
                    [
                        columns[
                            pl.ds(first * PLANE + slot * GX + source, count, stride=PLANE), :
                        ]
                        for source in range(GX)
                    ]
                )
            )
            for slot in slots
        ]
        for slot, code in zip(slots, codes):
            slabs[pl.ds(slot * GX, GX), sides[side]] = code

    def send_back(side):
        def body(step, carry):
            slots = slots_at(step)
            collect(side, slots)
            for slot in slots:
                send_slot(side, slot, octants, returned, sem_back_out, sem_back_in)
            return carry

        wait_sent(side, sem_out)
        lax.fori_loop(0, steps - 1, body, 0)
        collect(side, [twin, slot_own])
        send_slot(side, twin, octants, returned, sem_back_out, sem_back_in)
        send_slot(side, slot_own, octants[:-1], returned, sem_back_out, sem_back_in)
        keep_own(side, returned, sem_back_in)

    lax.fori_loop(0, steps, spread(0), 0)
    columns[column_rows(FIRST - 1), :] = jnp.zeros((128, 128), F32)
    work_columns([(0, 1), (2, 3), (4, 5)])
    lax.fori_loop(0, steps, spread(1), 0)
    columns[column_rows(SLAB - 1), :] = jnp.zeros((128, 128), F32)
    work_columns([(6, 7)])
    send_back(0)
    work_columns([(8, 9), (10,)])
    send_back(1)

    def wave_part(side, slots):
        start = INV_AT if side == 0 else INV_AT + GX * FIRST
        count = GX * FIRST if side == 0 else GX * (SLAB - FIRST)
        loaded = [
            (
                returned[pl.ds(slot * GX, GX), sides[side]],
                matrix_pair(matrices, start, jnp.minimum(slot, 1), count),
            )
            for slot in slots
        ]
        return [
            product3(parts(decode(codes).reshape(count, 128)), right, TN)
            for codes, right in loaded
        ]

    def first_wave(step, carry):
        slots = []
        for index in (2 * step, 2 * step + 1):
            couple = slots_before(index)
            wait_group(0, couple, returned, sem_back_in)
            slots.extend(couple)
        for slot, values in zip(slots, wave_part(0, slots)):
            waves[slot] = values
        return carry

    def second_wave(step, carry):
        slots = []
        for index in (2 * step, 2 * step + 1):
            couple = slots_before(index)
            wait_group(1, couple, returned, sem_back_in)
            slots.extend(couple)
        before = [waves[slot] for slot in slots]
        done = []
        for slot, values, base in zip(slots, wave_part(1, slots), before):
            values = values + base
            cosine = floats[pl.ds(32 * slot, 1), :]
            sine = floats[pl.ds(32 * slot + 16, 1), :]
            real, imag = values[:, :128], values[:, 128:]
            done.append((real * cosine - imag * sine, imag * cosine + real * sine))
        for slot, (real, imag) in zip(slots, done):
            waves[slot, :, 0:128] = real
            waves[slot, :, 128:256] = imag
        return carry

    lax.fori_loop(0, steps // 2, first_wave, 0)
    lax.fori_loop(0, steps // 2, second_wave, 0)

    def grid_body(step, carry):
        field = step // 2
        part = step % 2
        rows = pl.ds(pl.multiple_of(step * 16, 16), 16)
        spectrum = [(waves[0, rows, 0:128], None)]
        for slot in range(1, GY):
            spectrum.append((waves[slot, rows, 0:128], waves[slot, rows, 128:256]))
        spectrum.append((waves[0, rows, 128:256], None))
        values = real_inverse(spectrum)
        top = pl.ds(pl.multiple_of(part * 16, 16), 16)
        for c in range(32):
            new_rows[field, c // 4, top, (c % 4) * 128 : (c % 4) * 128 + 128] = values[c].astype(BF16)
        return carry

    for field in range(FIELDS):
        lax.fori_loop(2 * field, 2 * field + 2, grid_body, 0)
        for other in octants[:-1]:
            pltpu.make_async_remote_copy(
                src_ref=new_rows.at[field, other],
                dst_ref=results[field].at[own_rows, :],
                send_sem=sem_last_out,
                recv_sem=sem_last_in.at[field],
                device_id=(other, slot_own),
                device_id_type=MESH,
            ).start()
        pltpu.make_async_copy(
            new_rows.at[field, octant], results[field].at[own_rows, :], sem_last_in.at[field]
        ).start()

    for side in range(2):
        wait_sent(side, sem_back_out)
    moved = new_rows.at[:, pl.ds(0, GX - 1)]
    pltpu.make_async_copy(moved, moved, sem_rows_out).wait()
    pltpu.make_async_copy(moved, moved, sem_last_out).wait()
    for field in range(FIELDS):
        pltpu.make_async_copy(results[field], results[field], sem_last_in.at[field]).wait()


def place_kernel(*refs):
    copies = [
        pltpu.make_async_copy(refs[field], refs[FIELDS + field], refs[2 * FIELDS].at[field])
        for field in range(FIELDS)
    ]
    for copy in copies:
        copy.start()
    for copy in copies:
        copy.wait()


def per_device(east_wind, north_wind, height, tracer):
    constants = [jnp.asarray(value) for value in tables()]
    anywhere = pl.BlockSpec(memory_space=pl.ANY)
    block = jax.ShapeDtypeStruct((NG // GY, COLS), BF16)
    dma = pltpu.SemaphoreType.DMA
    landed = pl.pallas_call(
        step_kernel,
        out_shape=(block,) * 4,
        in_specs=[pl.BlockSpec(memory_space=pltpu.HBM)] * 6,
        out_specs=(anywhere,) * 4,
        scratch_shapes=[
            pltpu.VMEM((MATRIX_ROWS, 256), BF16),
            pltpu.VMEM((FLOAT_ROWS, 128), F32),
            pltpu.VMEM((FIELDS, GX, ROWS, COLS), BF16),
            pltpu.VMEM((GY, 128, 256), BF16),
            pltpu.VMEM((GY, 128, 256), BF16),
            pltpu.VMEM((DEVICES, SLAB // 8, 8, 128), BF16),
            pltpu.VMEM((DEVICES, SLAB // 8, 8, 128), BF16),
            pltpu.VMEM(((SLAB + 1) * PLANE, 128), F32),
            pltpu.VMEM((KX, 4, 128, 128), F32),
            pltpu.VMEM((DEVICES, SLAB // 8, 8, 128), BF16),
            pltpu.VMEM((GY, 128, 256), F32),
            pltpu.VMEM((FIELDS, GX, ROWS, COLS), BF16),
            dma((2,)),
            dma,
            dma((FIELDS,)),
            dma((2,)),
            dma((2, GY // 2)),
            dma((2,)),
            dma((2, GY // 2)),
            dma,
            dma((FIELDS,)),
            pltpu.SemaphoreType.REGULAR,
            pltpu.SemaphoreType.REGULAR,
        ],
        compiler_params=pltpu.CompilerParams(
            collective_id=0, has_side_effects=True, vmem_limit_bytes=32 * 1024 * 1024
        ),
    )(*[
        pltpu.with_memory_space_constraint(value, pltpu.HBM)
        for value in (east_wind, north_wind, height, tracer, *constants)
    ])
    return pl.pallas_call(
        place_kernel,
        out_shape=(block,) * 4,
        in_specs=[anywhere] * 4,
        out_specs=(pl.BlockSpec(memory_space=pltpu.HBM),) * 4,
        scratch_shapes=[dma((FIELDS,))],
        compiler_params=pltpu.CompilerParams(vmem_limit_bytes=1024 * 1024),
    )(*landed)


def solution(mesh):
    placed = (P("gy", "gx"),) * 4
    return jax.shard_map(
        per_device, mesh=mesh, in_specs=placed, out_specs=placed, check_vma=False
    )
```

```python
import math

import jax
import jax.numpy as jnp
import numpy as np
from jax import lax
from jax.experimental import pallas as pl
from jax.experimental.pallas import tpu as pltpu
from jax.sharding import PartitionSpec as P

NG = 4096
FIELDS = 4
GX = 8
GY = 16
DEVICES = GX * GY
KX = 11
SLAB = 24
FIRST = 16
PLANE = 136
REAL_ROWS = (0, 1, 2, 3, 4, 5, 6, 7, 17, 18, 19)
IMAG_ROWS = (8, 9, 10, 11, 12, 13, 14, 16, 20, 21, 22)
ROWS = 32
COLS = 512
POWER = 15
PEAK = 256.0

coriolis = 0.25
gravity_step = 2.0
depth_step = 2.0
diffusion = 0.02

F32 = jnp.float32
BF16 = jnp.bfloat16
MESH = pl.DeviceIdType.MESH


def split_const(matrix):
    whole = matrix.astype(np.float32)
    high = np.dtype(jnp.bfloat16)
    head = whole.astype(high)
    tail = (whole - head.astype(np.float32)).astype(high)
    return head, tail


def wave_of(slot, place):
    if slot == 0:
        return 32 * place if place < 43 else 16 + 32 * (place - 43)
    return slot + 32 * (place - 43)


def tables():
    turn = 2.0 * np.pi
    lane = np.arange(128)
    forward = np.zeros((2, GX, SLAB, 256))
    inverse = np.zeros((2, GX, SLAB, 256))
    for place in range(86):
        octant, member = place // KX, place % KX
        real_row, imag_row = REAL_ROWS[member], IMAG_ROWS[member]
        low = place - 43
        cosine, sine = np.cos(turn * lane * low / 128), np.sin(turn * lane * low / 128)
        forward[1, octant, real_row] = np.concatenate([cosine, sine])
        forward[1, octant, imag_row] = np.concatenate([-sine, cosine])
        inverse[1, octant, real_row] = np.concatenate([cosine, sine])
        inverse[1, octant, imag_row] = np.concatenate([-sine, cosine])
        wave = wave_of(0, place)
        cosine, sine = np.cos(turn * lane * wave / NG), np.sin(turn * lane * wave / NG)
        half = 0 if place < 43 else 128
        weight = 1.0 if wave == 0 else 2.0
        forward[0, octant, real_row, half : half + 128] = cosine
        forward[0, octant, imag_row, half : half + 128] = -sine
        inverse[0, octant, real_row, half : half + 128] = weight * cosine
        inverse[0, octant, imag_row, half : half + 128] = -weight * sine
    forward = forward.reshape(2, GX * SLAB, 256)
    inverse = np.concatenate(
        [
            inverse[:, :, :FIRST].reshape(2, GX * FIRST, 256),
            inverse[:, :, FIRST:].reshape(2, GX * (SLAB - FIRST), 256),
        ],
        axis=1,
    )
    angle = turn * np.outer(np.arange(GY), lane) / NG
    twist = np.stack([np.cos(angle), np.sin(angle)], axis=1)[:, :, None, :]
    twist = np.broadcast_to(twist, (GY, 2, 16, 128)).astype(np.float32)
    angle = turn * np.outer(lane, lane) / 128
    cosine, sine = np.cos(angle), np.sin(angle)
    gather = np.block([[cosine, sine], [-sine, cosine]])
    scatter = np.block([[cosine, -sine], [sine, cosine]])
    angle = turn * np.outer(np.arange(ROWS), np.arange(ROWS)) / ROWS
    cosine, sine = np.kron(np.eye(4), np.cos(angle)), np.kron(np.eye(4), np.sin(angle))
    fan_in = np.block([[cosine, -sine], [sine, cosine]])
    fan_out = np.block([[cosine, sine], [-sine, cosine]])
    angle = turn * np.outer(lane, lane % ROWS) / NG
    spin = np.stack([np.cos(angle), np.sin(angle)]).astype(np.float32)
    pieces = []
    for matrix in (forward.reshape(-1, 256), inverse.reshape(-1, 256) / NG, gather, scatter, fan_in, fan_out):
        pieces.extend(split_const(matrix))
    floats = np.concatenate([twist.reshape(-1, 128), spin.reshape(-1, 128)], axis=0)
    return np.concatenate(pieces, axis=0), floats


FWD_AT = 0
INV_AT = 4 * GX * SLAB
SQUARE_AT = 8 * GX * SLAB
MATRIX_ROWS = SQUARE_AT + 8 * 256
SPIN_AT = GY * 2 * 16
FLOAT_ROWS = SPIN_AT + 256


def matrix_pair(matrices, start, which, count=GX * SLAB):
    first = pl.multiple_of(start + which * (GX * SLAB), 64)
    second = pl.multiple_of(start + (which + 2) * (GX * SLAB), 64)
    return matrices[pl.ds(first, count), :], matrices[pl.ds(second, count), :]


def square_pair(matrices, which):
    first = SQUARE_AT + which * 512
    return matrices[first : first + 256, :], matrices[first + 256 : first + 512, :]


def encode(values):
    rows = values.shape[1]
    largest = jnp.max(jnp.abs(values), axis=1, keepdims=True)
    scale = (jnp.maximum(largest, 1e-34) * 1.01).astype(BF16).astype(F32)
    level = values * (PEAK / scale)
    second = level * level
    fourth = second * second
    eighth = fourth * fourth
    code = eighth * fourth * (second * level)
    ending = code[:, rows - 8 :]
    last = lax.broadcasted_iota(jnp.int32, ending.shape, 1) == 7
    ending = jnp.where(last, scale, ending)
    code = jnp.concatenate([code[:, : rows - 8], ending], axis=1) if rows > 8 else ending
    return code.reshape(values.shape[0], rows // 8, 8, 128).astype(BF16)


def decode(codes):
    rows = codes.shape[1] * 8
    code = codes.astype(F32).reshape(codes.shape[0], rows, 128)
    scale = code[:, rows - 1 : rows, :] * (1.0 / PEAK)
    size = jnp.maximum(jnp.abs(code), 2.0**-126)
    return jnp.exp2(jnp.log2(size) * (1.0 / POWER - 1.0)) * (code * scale)


def real_transform(values):
    count = len(values)
    if count == 2:
        return [(values[0] + values[1], None), (values[0] - values[1], None)]
    even = real_transform(values[0::2])
    odd = real_transform(values[1::2])
    half = count // 2
    result = [None] * (half + 1)
    for index in range(count // 4 + 1):
        even_real, even_imag = even[index]
        odd_real, odd_imag = odd[index]
        if index == 0:
            result[0] = (even_real + odd_real, None)
            result[half] = (even_real - odd_real, None)
        elif index == count // 4:
            result[index] = (even_real, -odd_real)
        else:
            cosine = math.cos(2.0 * math.pi * index / count)
            sine = math.sin(2.0 * math.pi * index / count)
            turned_real = odd_real * cosine + odd_imag * sine
            turned_imag = odd_imag * cosine - odd_real * sine
            result[index] = (even_real + turned_real, even_imag + turned_imag)
            result[half - index] = (even_real - turned_real, turned_imag - even_imag)
    return result


def real_inverse(waves):
    half = len(waves) - 1
    count = 2 * half
    if count == 2:
        return [waves[0][0] + waves[1][0], waves[0][0] - waves[1][0]]
    even = []
    odd = []
    for index in range(count // 4 + 1):
        real, imag = waves[index]
        other_real, other_imag = waves[half - index]
        if index == 0:
            even.append((real + other_real, None))
            odd.append((real - other_real, None))
        elif index == count // 4:
            even.append((real + real, None))
            odd.append((-(imag + imag), None))
        else:
            cosine = math.cos(2.0 * math.pi * index / count)
            sine = math.sin(2.0 * math.pi * index / count)
            even.append((real + other_real, imag - other_imag))
            gap_real = real - other_real
            gap_imag = imag + other_imag
            odd.append((gap_real * cosine - gap_imag * sine, gap_real * sine + gap_imag * cosine))
    outputs = [None] * count
    outputs[0::2] = real_inverse(even)
    outputs[1::2] = real_inverse(odd)
    return outputs


def parts(values):
    head = values.astype(BF16)
    return head, (values - head.astype(F32)).astype(BF16)


def product(left, right, dims):
    return lax.dot_general(left, right, (dims, ((), ())), preferred_element_type=F32)


def product3(left, right, dims):
    left_head, left_tail = left
    right_head, right_tail = right
    left_all = jnp.concatenate([left_head, left_head, left_tail], axis=dims[0][0])
    right_all = jnp.concatenate([right_head, right_tail, right_head], axis=dims[1][0])
    return product(left_all, right_all, dims)


NN = ((1,), (0,))
NT = ((1,), (1,))
TN = ((0,), (0,))


def fill_gains(gains, octant, slot):
    chunk = 32

    def body(step, carry):
        member = step // (128 // chunk)
        top = (step % (128 // chunk)) * chunk
        place = KX * octant + member
        zero_slot = jnp.where(place < 43, 32 * place, 16 + 32 * (place - 43))
        mode_x = jnp.where(slot == 0, zero_slot, slot + 32 * (place - 43))
        lane = lax.broadcasted_iota(jnp.int32, (chunk, 128), 1)
        row = lax.broadcasted_iota(jnp.int32, (chunk, 128), 0) + top
        field = lane // 32
        mode_y = row + 128 * (lane % 32)
        mode_y = jnp.where(mode_y < NG // 2, mode_y, mode_y - NG)
        cutoff = NG // 3
        inside = mode_y * mode_y + mode_x * mode_x <= cutoff * cutoff
        unit = 2.0 * math.pi / NG
        wave_x = mode_x.astype(F32) * unit
        wave_y = mode_y.astype(F32) * unit
        square = wave_x * wave_x + wave_y * wave_y
        scale = 1.0 / NG
        gain = jnp.where(inside, scale / (1.0 + diffusion * square * square), 0.0)
        stiffness = gravity_step * depth_step * square
        below = 1.0 / (1.0 + coriolis * coriolis + stiffness)
        above = (1.0 - coriolis * coriolis - stiffness) * below
        twice = (2.0 * coriolis) * below
        push_u = above * wave_x - twice * wave_y
        push_v = above * wave_y + twice * wave_x
        push_h = (2.0 * gravity_step) * square * below
        sum_u = wave_x + push_u
        sum_v = wave_y + push_v
        curl_u = -wave_y - coriolis * sum_u
        curl_v = wave_x - coriolis * sum_v
        curl_h = -coriolis * push_h
        anchor = square == 0.0
        over = 1.0 / jnp.where(anchor, 1.0, square)
        first = field == 0
        second = field == 1
        third = field == 2
        lead = jnp.where(first, -wave_y, wave_x)
        trail = jnp.where(first, wave_x, wave_y)
        from_u = (lead * curl_u + trail * push_u) * over
        from_v = (lead * curl_v + trail * push_v) * over
        from_h = -(lead * curl_h + trail * push_h) * over
        rotate = 1.0 / (1.0 + coriolis * coriolis)
        keep = (1.0 - coriolis * coriolis) * rotate
        cross = 2.0 * coriolis * rotate
        from_u = jnp.where(anchor, jnp.where(first, keep, -cross), from_u)
        from_v = jnp.where(anchor, jnp.where(first, cross, keep), from_v)
        zero = jnp.zeros_like(gain)
        same = jnp.where(
            first,
            from_u,
            jnp.where(second, from_v, jnp.where(third, 1.0 - depth_step * push_h, 1.0)),
        )
        one = jnp.where(second, from_u, jnp.where(third, -depth_step * sum_v, zero))
        two = jnp.where(first, from_h, jnp.where(third, -depth_step * sum_u, zero))
        three = jnp.where(first, from_v, jnp.where(second, from_h, zero))
        place_rows = pl.ds(pl.multiple_of(top, chunk), chunk)
        gains[member, 0, place_rows, :] = same * gain
        gains[member, 1, place_rows, :] = one * gain
        gains[member, 2, place_rows, :] = two * gain
        gains[member, 3, place_rows, :] = three * gain
        return carry

    lax.fori_loop(0, KX * (128 // chunk), body, 0)


def apply_gains(gains, member, real, imag):
    lane = lax.broadcasted_iota(jnp.int32, (128, 128), 1)
    field = lane // 32
    second = field == 1
    third = field == 2
    gain = gains[member, 0]
    out_real = real * gain
    out_imag = imag * gain
    crossed = [third, None, second]
    for turn in (1, 2, 3):
        gain = gains[member, turn]
        moved_real = pltpu.roll(real, 32 * turn, 1)
        moved_imag = pltpu.roll(imag, 32 * turn, 1)
        swap = crossed[turn - 1]
        if swap is None:
            use_real, use_imag = -moved_imag, moved_real
        else:
            use_real = jnp.where(swap, -moved_imag, moved_real)
            use_imag = jnp.where(swap, moved_real, moved_imag)
        out_real = out_real + gain * use_real
        out_imag = out_imag + gain * use_imag
    return out_real, out_imag


def step_kernel(*refs):
    sources = refs[0:4]
    matrix_source, float_source = refs[4:6]
    results = refs[6:10]
    (
        matrices,
        floats,
        grid_rows,
        head,
        tail,
        slabs,
        landed,
        columns,
        gains,
        returned,
        waves,
        new_rows,
        sem_table,
        sem_rows_out,
        sem_rows_in,
        sem_out,
        sem_in,
        sem_back_out,
        sem_back_in,
        sem_last_out,
        sem_last_in,
        sem_leaders,
        sem_all,
    ) = refs[10:]
    octant = lax.axis_index("gx")
    slot_own = lax.axis_index("gy")
    own = slot_own * GX + octant
    octants = [
        4 * ((octant // 4 + across) % 2) + (octant % 4 + along) % 4
        for across, along in ((1, 2), (1, 1), (1, 3), (0, 2), (1, 0), (0, 1), (0, 3), (0, 0))
    ]
    half_own = slot_own // 8
    level_own = (slot_own // 2) % 4
    core_own = slot_own % 2

    def distance(step):
        turn = step // 2
        odd = step % 2
        far = jnp.where(turn == 3, 0, jnp.where(turn == 2, 3, 2 - turn))
        near = jnp.where(turn == 3, 0, turn + 1)
        return 1 - odd, jnp.where(odd == 1, near, far)

    def slots_at(step):
        half, level = distance(step)
        base = 8 * ((half_own + half) % 2) + 2 * ((level_own + level) % 4)
        return [base + 1 - core_own, base + core_own]

    def slots_before(step):
        half, level = distance(step)
        base = 8 * ((half_own + half) % 2) + 2 * ((level_own + 4 - level) % 4)
        return [base + 1 - core_own, base + core_own]

    barrier = pltpu.get_barrier_semaphore()
    across_own = octant // 4
    for across, along in ((0, 1), (0, 2), (0, 3), (1, 0), (1, 1), (1, 2), (1, 3)):
        other = 4 * ((across_own + across) % 2) + (octant % 4 + along) % 4

        @pl.when(other != 0)
        def greet_member():
            pl.semaphore_signal(
                barrier, inc=1, device_id=(other, slot_own), device_id_type=MESH
            )

    @pl.when(octant == 0)
    def greet_leaders():
        for step in range(1, GY):
            pl.semaphore_signal(
                barrier, inc=1, device_id=(octant, (slot_own + step) % GY), device_id_type=MESH
            )

    table_copies = [
        pltpu.make_async_copy(matrix_source, matrices, sem_table.at[0]),
        pltpu.make_async_copy(float_source, floats, sem_table.at[1]),
    ]
    for copy in table_copies:
        copy.start()
    own_rows = pl.ds(pl.multiple_of(octant * ROWS, ROWS), ROWS)
    for field in range(FIELDS):
        pltpu.make_async_copy(
            sources[field].at[own_rows, :], grid_rows.at[field, octant], sem_rows_in.at[field]
        ).start()

    @pl.when(octant != 0)
    def wait_member():
        pl.semaphore_wait(barrier, GX - 1)

    @pl.when(octant == 1)
    def release_leader():
        pl.semaphore_signal(
            sem_all, inc=1, device_id=(octant - 1, slot_own), device_id_type=MESH
        )

    @pl.when(octant == 0)
    def wait_release():
        pl.semaphore_wait(sem_all, 1)

    for field in range(FIELDS):
        for other in octants[:-1]:
            pltpu.make_async_remote_copy(
                src_ref=sources[field].at[pl.ds(pl.multiple_of(other * ROWS, ROWS), ROWS), :],
                dst_ref=grid_rows.at[field, octant],
                send_sem=sem_rows_out,
                recv_sem=sem_rows_in.at[field],
                device_id=(other, slot_own),
                device_id_type=MESH,
            ).start()

    fill_gains(gains, octant, slot_own)

    @pl.when(octant == 0)
    def tell_members():
        pl.semaphore_wait(barrier, GY - 1)
        for step in range(1, GY):
            pl.semaphore_signal(
                sem_leaders,
                inc=1,
                device_id=(octant, (slot_own + step) % GY),
                device_id_type=MESH,
            )
        pl.semaphore_wait(sem_leaders, GY - 1)
        for other in octants[:-1]:
            pl.semaphore_signal(
                sem_all, inc=1, device_id=(other, slot_own), device_id_type=MESH
            )

    for copy in table_copies:
        copy.wait()

    def row_body(step, carry):
        field = step // 2
        part = step % 2
        top = pl.multiple_of(part * 16, 16)
        chunk = [
            grid_rows[field, c // 4, pl.ds(top, 16), (c % 4) * 128 : (c % 4) * 128 + 128].astype(F32)
            for c in range(32)
        ]
        spectrum = real_transform(chunk)
        rows = pl.ds(pl.multiple_of(step * 16, 16), 16)
        for slot in range(GY):
            if slot == 0:
                real, imag = spectrum[0][0], spectrum[16][0]
            else:
                wave_real, wave_imag = spectrum[slot]
                cosine = floats[32 * slot : 32 * slot + 16, :]
                sine = floats[32 * slot + 16 : 32 * slot + 32, :]
                real = wave_real * cosine + wave_imag * sine
                imag = wave_imag * cosine - wave_real * sine
            for side, value in ((0, real), (128, imag)):
                high, low = parts(value)
                head[slot, rows, side : side + 128] = high
                tail[slot, rows, side : side + 128] = low
        return carry

    for field in range(FIELDS):
        pltpu.make_async_copy(
            grid_rows.at[field], grid_rows.at[field], sem_rows_in.at[field]
        ).wait()
        lax.fori_loop(2 * field, 2 * field + 2, row_body, 0)

    @pl.when(octant != 0)
    def wait_all():
        pl.semaphore_wait(sem_all, 1)

    sides = (pl.ds(0, FIRST // 8), pl.ds(FIRST // 8, (SLAB - FIRST) // 8))

    def send_slot(side, slot, others, target, out_sem, in_sem):
        for other in others:
            pltpu.make_async_remote_copy(
                src_ref=slabs.at[slot * GX + other, sides[side]],
                dst_ref=target.at[own, sides[side]],
                send_sem=out_sem.at[side],
                recv_sem=in_sem.at[side, slot_own // 2],
                device_id=(other, slot),
                device_id_type=MESH,
            ).start()

    def keep_own(side, target, in_sem):
        pltpu.make_async_copy(
            slabs.at[own, sides[side]],
            target.at[own, sides[side]],
            in_sem.at[side, slot_own // 2],
        ).start()

    def wait_group(side, slots, target, in_sem):
        couple = slots[0] // 2
        group = target.at[pl.ds(couple * (2 * GX), 2 * GX), sides[side]]
        pltpu.make_async_copy(group, group, in_sem.at[side, couple]).wait()

    def wait_sent(side, out_sem):
        sent = slabs.at[pl.ds(0, DEVICES - 1), sides[side]]
        pltpu.make_async_copy(sent, sent, out_sem.at[side]).wait()

    def slot_products(slots):
        loaded = [
            (matrix_pair(matrices, FWD_AT, jnp.minimum(slot, 1)), (head[slot], tail[slot]))
            for slot in slots
        ]
        codes = []
        for left, right in loaded:
            spectrum = product3(left, right, NT).reshape(GX, SLAB, 128)
            codes.append([encode(spectrum[:, :FIRST]), encode(spectrum[:, FIRST:])])
        for slot, pieces in zip(slots, codes):
            for side in range(2):
                slabs[pl.ds(slot * GX, GX), sides[side]] = pieces[side]

    steps = GY // 2

    def slot_body(step, carry):
        slots = slots_at(2 * step) + slots_at(2 * step + 1)
        slot_products(slots)
        for slot in slots:
            send_slot(0, slot, octants, landed, sem_out, sem_in)
        return carry

    lax.fori_loop(0, steps // 2 - 1, slot_body, 0)
    twin = slots_at(steps - 1)[0]
    nearby = slots_at(steps - 2)
    slot_products(nearby + [twin, slot_own])
    for slot in nearby:
        send_slot(0, slot, octants, landed, sem_out, sem_in)
    send_slot(0, twin, octants, landed, sem_out, sem_in)
    send_slot(0, slot_own, octants[:-1], landed, sem_out, sem_in)
    keep_own(0, landed, sem_in)

    def second_body(step, carry):
        for slot in slots_at(step):
            send_slot(1, slot, octants, landed, sem_out, sem_in)
        return carry

    lax.fori_loop(0, steps - 1, second_body, 0)
    send_slot(1, twin, octants, landed, sem_out, sem_in)
    send_slot(1, slot_own, octants[:-1], landed, sem_out, sem_in)
    keep_own(1, landed, sem_in)

    def spread(side):
        first = 0 if side == 0 else FIRST
        count = FIRST if side == 0 else SLAB - FIRST

        def body(step, carry):
            slots = slots_before(step)
            wait_group(side, slots, landed, sem_in)
            for slot in slots:
                values = decode(landed[pl.ds(slot * GX, GX), sides[side]])
                for source in range(GX):
                    columns[
                        pl.ds(first * PLANE + slot * GX + source, count, stride=PLANE), :
                    ] = values[source]
            return carry

        return body

    def plane(row):
        return slice(row * 128, row * 128 + 128)

    def column_rows(row):
        return slice(row * PLANE, row * PLANE + 128)

    def stack_pair(reals, imags):
        return jnp.concatenate(
            [jnp.concatenate(reals, axis=1), jnp.concatenate(imags, axis=1)], axis=0
        )

    def work_columns(groups):
        members = [member for group in groups for member in group]
        cosine = floats[SPIN_AT : SPIN_AT + 128, :]
        sine = floats[SPIN_AT + 128 : SPIN_AT + 256, :]
        loaded = [
            stack_pair(
                [columns[column_rows(REAL_ROWS[member]), :] for member in group],
                [columns[column_rows(IMAG_ROWS[member]), :] for member in group],
            )
            for group in groups
        ]
        turned = []
        for group, values in zip(groups, loaded):
            mixed = product3(square_pair(matrices, 0), parts(values), NN)
            for index in range(len(group)):
                real, imag = mixed[:128, plane(index)], mixed[128:, plane(index)]
                turned.append(
                    jnp.concatenate(
                        [real * cosine + imag * sine, imag * cosine - real * sine], axis=1
                    )
                )
        modes = product3(
            parts(jnp.concatenate(turned, axis=0)), square_pair(matrices, 2), NN
        )
        changed = []
        for index, member in enumerate(members):
            piece = modes[plane(index)]
            real, imag = apply_gains(gains, member, piece[:, :128], piece[:, 128:])
            changed.append(jnp.concatenate([real, imag], axis=1))
        mixed = product3(
            parts(jnp.concatenate(changed, axis=0)), square_pair(matrices, 3), NN
        )
        start = 0
        done = []
        for group in groups:
            reals, imags = [], []
            for index in range(start, start + len(group)):
                piece = mixed[plane(index)]
                real, imag = piece[:, :128], piece[:, 128:]
                reals.append(real * cosine - imag * sine)
                imags.append(imag * cosine + real * sine)
            start += len(group)
            done.append(
                product3(square_pair(matrices, 1), parts(stack_pair(reals, imags)), NN)
            )
        for group, values in zip(groups, done):
            for index, member in enumerate(group):
                columns[column_rows(REAL_ROWS[member]), :] = values[:128, plane(index)]
                columns[column_rows(IMAG_ROWS[member]), :] = values[128:, plane(index)]

    def collect(side, slots):
        first = 0 if side == 0 else FIRST
        count = FIRST if side == 0 else SLAB - FIRST
        codes = [
            encode(
                jnp.stack(
                    [
                        columns[
                            pl.ds(first * PLANE + slot * GX + source, count, stride=PLANE), :
                        ]
                        for source in range(GX)
                    ]
                )
            )
            for slot in slots
        ]
        for slot, code in zip(slots, codes):
            slabs[pl.ds(slot * GX, GX), sides[side]] = code

    def send_back(side):
        def body(step, carry):
            slots = slots_at(step)
            collect(side, slots)
            for slot in slots:
                send_slot(side, slot, octants, returned, sem_back_out, sem_back_in)
            return carry

        wait_sent(side, sem_out)
        lax.fori_loop(0, steps - 1, body, 0)
        collect(side, [twin, slot_own])
        send_slot(side, twin, octants, returned, sem_back_out, sem_back_in)
        send_slot(side, slot_own, octants[:-1], returned, sem_back_out, sem_back_in)
        keep_own(side, returned, sem_back_in)

    lax.fori_loop(0, steps, spread(0), 0)
    columns[column_rows(FIRST - 1), :] = jnp.zeros((128, 128), F32)
    work_columns([(0, 1), (2, 3), (4, 5)])
    lax.fori_loop(0, steps, spread(1), 0)
    columns[column_rows(SLAB - 1), :] = jnp.zeros((128, 128), F32)
    work_columns([(6, 7)])
    send_back(0)
    work_columns([(8, 9), (10,)])
    send_back(1)

    def wave_part(side, slots):
        start = INV_AT if side == 0 else INV_AT + GX * FIRST
        count = GX * FIRST if side == 0 else GX * (SLAB - FIRST)
        loaded = [
            (
                returned[pl.ds(slot * GX, GX), sides[side]],
                matrix_pair(matrices, start, jnp.minimum(slot, 1), count),
            )
            for slot in slots
        ]
        return [
            product3(parts(decode(codes).reshape(count, 128)), right, TN)
            for codes, right in loaded
        ]

    def first_wave(step, carry):
        slots = []
        for index in (2 * step, 2 * step + 1):
            couple = slots_before(index)
            wait_group(0, couple, returned, sem_back_in)
            slots.extend(couple)
        for slot, values in zip(slots, wave_part(0, slots)):
            waves[slot] = values
        return carry

    def second_wave(step, carry):
        slots = []
        for index in (2 * step, 2 * step + 1):
            couple = slots_before(index)
            wait_group(1, couple, returned, sem_back_in)
            slots.extend(couple)
        before = [waves[slot] for slot in slots]
        done = []
        for slot, values, base in zip(slots, wave_part(1, slots), before):
            values = values + base
            cosine = floats[pl.ds(32 * slot, 1), :]
            sine = floats[pl.ds(32 * slot + 16, 1), :]
            real, imag = values[:, :128], values[:, 128:]
            done.append((real * cosine - imag * sine, imag * cosine + real * sine))
        for slot, (real, imag) in zip(slots, done):
            waves[slot, :, 0:128] = real
            waves[slot, :, 128:256] = imag
        return carry

    lax.fori_loop(0, steps // 2, first_wave, 0)
    lax.fori_loop(0, steps // 2, second_wave, 0)

    def grid_body(step, carry):
        field = step // 2
        part = step % 2
        rows = pl.ds(pl.multiple_of(step * 16, 16), 16)
        spectrum = [(waves[0, rows, 0:128], None)]
        for slot in range(1, GY):
            spectrum.append((waves[slot, rows, 0:128], waves[slot, rows, 128:256]))
        spectrum.append((waves[0, rows, 128:256], None))
        values = real_inverse(spectrum)
        top = pl.ds(pl.multiple_of(part * 16, 16), 16)
        for c in range(32):
            new_rows[field, c // 4, top, (c % 4) * 128 : (c % 4) * 128 + 128] = values[c].astype(BF16)
        return carry

    for field in range(FIELDS):
        lax.fori_loop(2 * field, 2 * field + 2, grid_body, 0)
        for other in octants[:-1]:
            pltpu.make_async_remote_copy(
                src_ref=new_rows.at[field, other],
                dst_ref=results[field].at[own_rows, :],
                send_sem=sem_last_out,
                recv_sem=sem_last_in.at[field],
                device_id=(other, slot_own),
                device_id_type=MESH,
            ).start()
        pltpu.make_async_copy(
            new_rows.at[field, octant], results[field].at[own_rows, :], sem_last_in.at[field]
        ).start()

    for side in range(2):
        wait_sent(side, sem_back_out)
    moved = new_rows.at[:, pl.ds(0, GX - 1)]
    pltpu.make_async_copy(moved, moved, sem_rows_out).wait()
    pltpu.make_async_copy(moved, moved, sem_last_out).wait()
    for field in range(FIELDS):
        pltpu.make_async_copy(results[field], results[field], sem_last_in.at[field]).wait()


def place_kernel(*refs):
    copies = [
        pltpu.make_async_copy(refs[field], refs[FIELDS + field], refs[2 * FIELDS].at[field])
        for field in range(FIELDS)
    ]
    for copy in copies:
        copy.start()
    for copy in copies:
        copy.wait()


def per_device(east_wind, north_wind, height, tracer):
    constants = [jnp.asarray(value) for value in tables()]
    anywhere = pl.BlockSpec(memory_space=pl.ANY)
    block = jax.ShapeDtypeStruct((NG // GY, COLS), BF16)
    dma = pltpu.SemaphoreType.DMA
    landed = pl.pallas_call(
        step_kernel,
        out_shape=(block,) * 4,
        in_specs=[pl.BlockSpec(memory_space=pltpu.HBM)] * 6,
        out_specs=(anywhere,) * 4,
        scratch_shapes=[
            pltpu.VMEM((MATRIX_ROWS, 256), BF16),
            pltpu.VMEM((FLOAT_ROWS, 128), F32),
            pltpu.VMEM((FIELDS, GX, ROWS, COLS), BF16),
            pltpu.VMEM((GY, 128, 256), BF16),
            pltpu.VMEM((GY, 128, 256), BF16),
            pltpu.VMEM((DEVICES, SLAB // 8, 8, 128), BF16),
            pltpu.VMEM((DEVICES, SLAB // 8, 8, 128), BF16),
            pltpu.VMEM(((SLAB + 1) * PLANE, 128), F32),
            pltpu.VMEM((KX, 4, 128, 128), F32),
            pltpu.VMEM((DEVICES, SLAB // 8, 8, 128), BF16),
            pltpu.VMEM((GY, 128, 256), F32),
            pltpu.VMEM((FIELDS, GX, ROWS, COLS), BF16),
            dma((2,)),
            dma,
            dma((FIELDS,)),
            dma((2,)),
            dma((2, GY // 2)),
            dma((2,)),
            dma((2, GY // 2)),
            dma,
            dma((FIELDS,)),
            pltpu.SemaphoreType.REGULAR,
            pltpu.SemaphoreType.REGULAR,
        ],
        compiler_params=pltpu.CompilerParams(
            collective_id=0, has_side_effects=True, vmem_limit_bytes=32 * 1024 * 1024
        ),
    )(*[
        pltpu.with_memory_space_constraint(value, pltpu.HBM)
        for value in (east_wind, north_wind, height, tracer, *constants)
    ])
    return pl.pallas_call(
        place_kernel,
        out_shape=(block,) * 4,
        in_specs=[anywhere] * 4,
        out_specs=(pl.BlockSpec(memory_space=pltpu.HBM),) * 4,
        scratch_shapes=[dma((FIELDS,))],
        compiler_params=pltpu.CompilerParams(vmem_limit_bytes=1024 * 1024),
    )(*landed)


def solution(mesh):
    placed = (P("gy", "gx"),) * 4
    return jax.shard_map(
        per_device, mesh=mesh, in_specs=placed, out_specs=placed, check_vma=False
    )
```

```python
import math

import jax
import jax.numpy as jnp
import numpy as np
from jax import lax
from jax.experimental import pallas as pl
from jax.experimental.pallas import tpu as pltpu
from jax.sharding import PartitionSpec as P

NG = 4096
FIELDS = 4
GX = 8
GY = 16
DEVICES = GX * GY
KX = 11
SLAB = 24
FIRST = 16
PLANE = 136
REAL_ROWS = (0, 1, 2, 3, 4, 5, 6, 7, 17, 18, 19)
IMAG_ROWS = (8, 9, 10, 11, 12, 13, 14, 16, 20, 21, 22)
ROWS = 32
COLS = 512
POWER = 17
PEAK = 128.0

coriolis = 0.25
gravity_step = 2.0
depth_step = 2.0
diffusion = 0.02

F32 = jnp.float32
BF16 = jnp.bfloat16
MESH = pl.DeviceIdType.MESH


def split_const(matrix):
    whole = matrix.astype(np.float32)
    high = np.dtype(jnp.bfloat16)
    head = whole.astype(high)
    tail = (whole - head.astype(np.float32)).astype(high)
    return head, tail


def wave_of(slot, place):
    if slot == 0:
        return 32 * place if place < 43 else 16 + 32 * (place - 43)
    return slot + 32 * (place - 43)


def tables():
    turn = 2.0 * np.pi
    lane = np.arange(128)
    forward = np.zeros((2, GX, SLAB, 256))
    inverse = np.zeros((2, GX, SLAB, 256))
    for place in range(86):
        octant, member = place // KX, place % KX
        real_row, imag_row = REAL_ROWS[member], IMAG_ROWS[member]
        low = place - 43
        cosine, sine = np.cos(turn * lane * low / 128), np.sin(turn * lane * low / 128)
        forward[1, octant, real_row] = np.concatenate([cosine, sine])
        forward[1, octant, imag_row] = np.concatenate([-sine, cosine])
        inverse[1, octant, real_row] = np.concatenate([cosine, sine])
        inverse[1, octant, imag_row] = np.concatenate([-sine, cosine])
        wave = wave_of(0, place)
        cosine, sine = np.cos(turn * lane * wave / NG), np.sin(turn * lane * wave / NG)
        half = 0 if place < 43 else 128
        weight = 1.0 if wave == 0 else 2.0
        forward[0, octant, real_row, half : half + 128] = cosine
        forward[0, octant, imag_row, half : half + 128] = -sine
        inverse[0, octant, real_row, half : half + 128] = weight * cosine
        inverse[0, octant, imag_row, half : half + 128] = -weight * sine
    forward = forward.reshape(2, GX * SLAB, 256)
    inverse = np.concatenate(
        [
            inverse[:, :, :FIRST].reshape(2, GX * FIRST, 256),
            inverse[:, :, FIRST:].reshape(2, GX * (SLAB - FIRST), 256),
        ],
        axis=1,
    )
    angle = turn * np.outer(np.arange(GY), lane) / NG
    twist = np.stack([np.cos(angle), np.sin(angle)], axis=1)[:, :, None, :]
    twist = np.broadcast_to(twist, (GY, 2, 16, 128)).astype(np.float32)
    angle = turn * np.outer(lane, lane) / 128
    cosine, sine = np.cos(angle), np.sin(angle)
    gather = np.block([[cosine, sine], [-sine, cosine]])
    scatter = np.block([[cosine, -sine], [sine, cosine]])
    angle = turn * np.outer(np.arange(ROWS), np.arange(ROWS)) / ROWS
    cosine, sine = np.kron(np.eye(4), np.cos(angle)), np.kron(np.eye(4), np.sin(angle))
    fan_in = np.block([[cosine, -sine], [sine, cosine]])
    fan_out = np.block([[cosine, sine], [-sine, cosine]])
    angle = turn * np.outer(lane, lane % ROWS) / NG
    spin = np.stack([np.cos(angle), np.sin(angle)]).astype(np.float32)
    pieces = []
    for matrix in (forward.reshape(-1, 256), inverse.reshape(-1, 256) / NG, gather, scatter, fan_in, fan_out):
        pieces.extend(split_const(matrix))
    floats = np.concatenate([twist.reshape(-1, 128), spin.reshape(-1, 128)], axis=0)
    return np.concatenate(pieces, axis=0), floats


FWD_AT = 0
INV_AT = 4 * GX * SLAB
SQUARE_AT = 8 * GX * SLAB
MATRIX_ROWS = SQUARE_AT + 8 * 256
SPIN_AT = GY * 2 * 16
FLOAT_ROWS = SPIN_AT + 256


def matrix_pair(matrices, start, which, count=GX * SLAB):
    first = pl.multiple_of(start + which * (GX * SLAB), 64)
    second = pl.multiple_of(start + (which + 2) * (GX * SLAB), 64)
    return matrices[pl.ds(first, count), :], matrices[pl.ds(second, count), :]


def square_pair(matrices, which):
    first = SQUARE_AT + which * 512
    return matrices[first : first + 256, :], matrices[first + 256 : first + 512, :]


def encode(values):
    rows = values.shape[1]
    largest = jnp.max(jnp.abs(values), axis=1, keepdims=True)
    scale = (jnp.maximum(largest, 1e-34) * 1.01).astype(BF16).astype(F32)
    level = values * (PEAK / scale)
    second = level * level
    fourth = second * second
    eighth = fourth * fourth
    code = eighth * eighth * level
    ending = code[:, rows - 8 :]
    last = lax.broadcasted_iota(jnp.int32, ending.shape, 1) == 7
    ending = jnp.where(last, scale, ending)
    code = jnp.concatenate([code[:, : rows - 8], ending], axis=1) if rows > 8 else ending
    return code.reshape(values.shape[0], rows // 8, 8, 128).astype(BF16)


def decode(codes):
    rows = codes.shape[1] * 8
    code = codes.astype(F32).reshape(codes.shape[0], rows, 128)
    scale = code[:, rows - 1 : rows, :] * (1.0 / PEAK)
    size = jnp.maximum(jnp.abs(code), 2.0**-126)
    return jnp.exp2(jnp.log2(size) * (1.0 / POWER - 1.0)) * (code * scale)


def real_transform(values):
    count = len(values)
    if count == 2:
        return [(values[0] + values[1], None), (values[0] - values[1], None)]
    even = real_transform(values[0::2])
    odd = real_transform(values[1::2])
    half = count // 2
    result = [None] * (half + 1)
    for index in range(count // 4 + 1):
        even_real, even_imag = even[index]
        odd_real, odd_imag = odd[index]
        if index == 0:
            result[0] = (even_real + odd_real, None)
            result[half] = (even_real - odd_real, None)
        elif index == count // 4:
            result[index] = (even_real, -odd_real)
        else:
            cosine = math.cos(2.0 * math.pi * index / count)
            sine = math.sin(2.0 * math.pi * index / count)
            turned_real = odd_real * cosine + odd_imag * sine
            turned_imag = odd_imag * cosine - odd_real * sine
            result[index] = (even_real + turned_real, even_imag + turned_imag)
            result[half - index] = (even_real - turned_real, turned_imag - even_imag)
    return result


def real_inverse(waves):
    half = len(waves) - 1
    count = 2 * half
    if count == 2:
        return [waves[0][0] + waves[1][0], waves[0][0] - waves[1][0]]
    even = []
    odd = []
    for index in range(count // 4 + 1):
        real, imag = waves[index]
        other_real, other_imag = waves[half - index]
        if index == 0:
            even.append((real + other_real, None))
            odd.append((real - other_real, None))
        elif index == count // 4:
            even.append((real + real, None))
            odd.append((-(imag + imag), None))
        else:
            cosine = math.cos(2.0 * math.pi * index / count)
            sine = math.sin(2.0 * math.pi * index / count)
            even.append((real + other_real, imag - other_imag))
            gap_real = real - other_real
            gap_imag = imag + other_imag
            odd.append((gap_real * cosine - gap_imag * sine, gap_real * sine + gap_imag * cosine))
    outputs = [None] * count
    outputs[0::2] = real_inverse(even)
    outputs[1::2] = real_inverse(odd)
    return outputs


def parts(values):
    head = values.astype(BF16)
    return head, (values - head.astype(F32)).astype(BF16)


def product(left, right, dims):
    return lax.dot_general(left, right, (dims, ((), ())), preferred_element_type=F32)


def product3(left, right, dims):
    left_head, left_tail = left
    right_head, right_tail = right
    left_all = jnp.concatenate([left_head, left_head, left_tail], axis=dims[0][0])
    right_all = jnp.concatenate([right_head, right_tail, right_head], axis=dims[1][0])
    return product(left_all, right_all, dims)


NN = ((1,), (0,))
NT = ((1,), (1,))
TN = ((0,), (0,))


def fill_gains(gains, octant, slot):
    chunk = 32

    def body(step, carry):
        member = step // (128 // chunk)
        top = (step % (128 // chunk)) * chunk
        place = KX * octant + member
        zero_slot = jnp.where(place < 43, 32 * place, 16 + 32 * (place - 43))
        mode_x = jnp.where(slot == 0, zero_slot, slot + 32 * (place - 43))
        lane = lax.broadcasted_iota(jnp.int32, (chunk, 128), 1)
        row = lax.broadcasted_iota(jnp.int32, (chunk, 128), 0) + top
        field = lane // 32
        mode_y = row + 128 * (lane % 32)
        mode_y = jnp.where(mode_y < NG // 2, mode_y, mode_y - NG)
        cutoff = NG // 3
        inside = mode_y * mode_y + mode_x * mode_x <= cutoff * cutoff
        unit = 2.0 * math.pi / NG
        wave_x = mode_x.astype(F32) * unit
        wave_y = mode_y.astype(F32) * unit
        square = wave_x * wave_x + wave_y * wave_y
        scale = 1.0 / NG
        gain = jnp.where(inside, scale / (1.0 + diffusion * square * square), 0.0)
        stiffness = gravity_step * depth_step * square
        below = 1.0 / (1.0 + coriolis * coriolis + stiffness)
        above = (1.0 - coriolis * coriolis - stiffness) * below
        twice = (2.0 * coriolis) * below
        push_u = above * wave_x - twice * wave_y
        push_v = above * wave_y + twice * wave_x
        push_h = (2.0 * gravity_step) * square * below
        sum_u = wave_x + push_u
        sum_v = wave_y + push_v
        curl_u = -wave_y - coriolis * sum_u
        curl_v = wave_x - coriolis * sum_v
        curl_h = -coriolis * push_h
        anchor = square == 0.0
        over = 1.0 / jnp.where(anchor, 1.0, square)
        first = field == 0
        second = field == 1
        third = field == 2
        lead = jnp.where(first, -wave_y, wave_x)
        trail = jnp.where(first, wave_x, wave_y)
        from_u = (lead * curl_u + trail * push_u) * over
        from_v = (lead * curl_v + trail * push_v) * over
        from_h = -(lead * curl_h + trail * push_h) * over
        rotate = 1.0 / (1.0 + coriolis * coriolis)
        keep = (1.0 - coriolis * coriolis) * rotate
        cross = 2.0 * coriolis * rotate
        from_u = jnp.where(anchor, jnp.where(first, keep, -cross), from_u)
        from_v = jnp.where(anchor, jnp.where(first, cross, keep), from_v)
        zero = jnp.zeros_like(gain)
        same = jnp.where(
            first,
            from_u,
            jnp.where(second, from_v, jnp.where(third, 1.0 - depth_step * push_h, 1.0)),
        )
        one = jnp.where(second, from_u, jnp.where(third, -depth_step * sum_v, zero))
        two = jnp.where(first, from_h, jnp.where(third, -depth_step * sum_u, zero))
        three = jnp.where(first, from_v, jnp.where(second, from_h, zero))
        place_rows = pl.ds(pl.multiple_of(top, chunk), chunk)
        gains[member, 0, place_rows, :] = same * gain
        gains[member, 1, place_rows, :] = one * gain
        gains[member, 2, place_rows, :] = two * gain
        gains[member, 3, place_rows, :] = three * gain
        return carry

    lax.fori_loop(0, KX * (128 // chunk), body, 0)


def apply_gains(gains, member, real, imag):
    lane = lax.broadcasted_iota(jnp.int32, (128, 128), 1)
    field = lane // 32
    second = field == 1
    third = field == 2
    gain = gains[member, 0]
    out_real = real * gain
    out_imag = imag * gain
    crossed = [third, None, second]
    for turn in (1, 2, 3):
        gain = gains[member, turn]
        moved_real = pltpu.roll(real, 32 * turn, 1)
        moved_imag = pltpu.roll(imag, 32 * turn, 1)
        swap = crossed[turn - 1]
        if swap is None:
            use_real, use_imag = -moved_imag, moved_real
        else:
            use_real = jnp.where(swap, -moved_imag, moved_real)
            use_imag = jnp.where(swap, moved_real, moved_imag)
        out_real = out_real + gain * use_real
        out_imag = out_imag + gain * use_imag
    return out_real, out_imag


def step_kernel(*refs):
    sources = refs[0:4]
    matrix_source, float_source = refs[4:6]
    results = refs[6:10]
    (
        matrices,
        floats,
        grid_rows,
        head,
        tail,
        slabs,
        landed,
        columns,
        gains,
        returned,
        waves,
        new_rows,
        sem_table,
        sem_rows_out,
        sem_rows_in,
        sem_out,
        sem_in,
        sem_back_out,
        sem_back_in,
        sem_last_out,
        sem_last_in,
        sem_leaders,
        sem_all,
    ) = refs[10:]
    octant = lax.axis_index("gx")
    slot_own = lax.axis_index("gy")
    own = slot_own * GX + octant
    octants = [
        4 * ((octant // 4 + across) % 2) + (octant % 4 + along) % 4
        for across, along in ((1, 2), (1, 1), (1, 3), (0, 2), (1, 0), (0, 1), (0, 3), (0, 0))
    ]
    half_own = slot_own // 8
    level_own = (slot_own // 2) % 4
    core_own = slot_own % 2

    def distance(step):
        turn = step // 2
        odd = step % 2
        far = jnp.where(turn == 3, 0, jnp.where(turn == 2, 3, 2 - turn))
        near = jnp.where(turn == 3, 0, turn + 1)
        return 1 - odd, jnp.where(odd == 1, near, far)

    def slots_at(step):
        half, level = distance(step)
        base = 8 * ((half_own + half) % 2) + 2 * ((level_own + level) % 4)
        return [base + 1 - core_own, base + core_own]

    def slots_before(step):
        half, level = distance(step)
        base = 8 * ((half_own + half) % 2) + 2 * ((level_own + 4 - level) % 4)
        return [base + 1 - core_own, base + core_own]

    barrier = pltpu.get_barrier_semaphore()
    across_own = octant // 4
    for across, along in ((0, 1), (0, 2), (0, 3), (1, 0), (1, 1), (1, 2), (1, 3)):
        other = 4 * ((across_own + across) % 2) + (octant % 4 + along) % 4

        @pl.when(other != 0)
        def greet_member():
            pl.semaphore_signal(
                barrier, inc=1, device_id=(other, slot_own), device_id_type=MESH
            )

    @pl.when(octant == 0)
    def greet_leaders():
        for step in range(1, GY):
            pl.semaphore_signal(
                barrier, inc=1, device_id=(octant, (slot_own + step) % GY), device_id_type=MESH
            )

    table_copies = [
        pltpu.make_async_copy(matrix_source, matrices, sem_table.at[0]),
        pltpu.make_async_copy(float_source, floats, sem_table.at[1]),
    ]
    for copy in table_copies:
        copy.start()
    own_rows = pl.ds(pl.multiple_of(octant * ROWS, ROWS), ROWS)
    for field in range(FIELDS):
        pltpu.make_async_copy(
            sources[field].at[own_rows, :], grid_rows.at[field, octant], sem_rows_in.at[field]
        ).start()

    @pl.when(octant != 0)
    def wait_member():
        pl.semaphore_wait(barrier, GX - 1)

    @pl.when(octant == 1)
    def release_leader():
        pl.semaphore_signal(
            sem_all, inc=1, device_id=(octant - 1, slot_own), device_id_type=MESH
        )

    @pl.when(octant == 0)
    def wait_release():
        pl.semaphore_wait(sem_all, 1)

    for field in range(FIELDS):
        for other in octants[:-1]:
            pltpu.make_async_remote_copy(
                src_ref=sources[field].at[pl.ds(pl.multiple_of(other * ROWS, ROWS), ROWS), :],
                dst_ref=grid_rows.at[field, octant],
                send_sem=sem_rows_out,
                recv_sem=sem_rows_in.at[field],
                device_id=(other, slot_own),
                device_id_type=MESH,
            ).start()

    fill_gains(gains, octant, slot_own)

    @pl.when(octant == 0)
    def tell_members():
        pl.semaphore_wait(barrier, GY - 1)
        for step in range(1, GY):
            pl.semaphore_signal(
                sem_leaders,
                inc=1,
                device_id=(octant, (slot_own + step) % GY),
                device_id_type=MESH,
            )
        pl.semaphore_wait(sem_leaders, GY - 1)
        for other in octants[:-1]:
            pl.semaphore_signal(
                sem_all, inc=1, device_id=(other, slot_own), device_id_type=MESH
            )

    for copy in table_copies:
        copy.wait()

    def row_body(step, carry):
        field = step // 2
        part = step % 2
        top = pl.multiple_of(part * 16, 16)
        chunk = [
            grid_rows[field, c // 4, pl.ds(top, 16), (c % 4) * 128 : (c % 4) * 128 + 128].astype(F32)
            for c in range(32)
        ]
        spectrum = real_transform(chunk)
        rows = pl.ds(pl.multiple_of(step * 16, 16), 16)
        for slot in range(GY):
            if slot == 0:
                real, imag = spectrum[0][0], spectrum[16][0]
            else:
                wave_real, wave_imag = spectrum[slot]
                cosine = floats[32 * slot : 32 * slot + 16, :]
                sine = floats[32 * slot + 16 : 32 * slot + 32, :]
                real = wave_real * cosine + wave_imag * sine
                imag = wave_imag * cosine - wave_real * sine
            for side, value in ((0, real), (128, imag)):
                high, low = parts(value)
                head[slot, rows, side : side + 128] = high
                tail[slot, rows, side : side + 128] = low
        return carry

    for field in range(FIELDS):
        pltpu.make_async_copy(
            grid_rows.at[field], grid_rows.at[field], sem_rows_in.at[field]
        ).wait()
        lax.fori_loop(2 * field, 2 * field + 2, row_body, 0)

    @pl.when(octant != 0)
    def wait_all():
        pl.semaphore_wait(sem_all, 1)

    sides = (pl.ds(0, FIRST // 8), pl.ds(FIRST // 8, (SLAB - FIRST) // 8))

    def send_slot(side, slot, others, target, out_sem, in_sem):
        for other in others:
            pltpu.make_async_remote_copy(
                src_ref=slabs.at[slot * GX + other, sides[side]],
                dst_ref=target.at[own, sides[side]],
                send_sem=out_sem.at[side],
                recv_sem=in_sem.at[side, slot_own // 2],
                device_id=(other, slot),
                device_id_type=MESH,
            ).start()

    def keep_own(side, target, in_sem):
        pltpu.make_async_copy(
            slabs.at[own, sides[side]],
            target.at[own, sides[side]],
            in_sem.at[side, slot_own // 2],
        ).start()

    def wait_group(side, slots, target, in_sem):
        couple = slots[0] // 2
        group = target.at[pl.ds(couple * (2 * GX), 2 * GX), sides[side]]
        pltpu.make_async_copy(group, group, in_sem.at[side, couple]).wait()

    def wait_sent(side, out_sem):
        sent = slabs.at[pl.ds(0, DEVICES - 1), sides[side]]
        pltpu.make_async_copy(sent, sent, out_sem.at[side]).wait()

    def slot_products(slots):
        loaded = [
            (matrix_pair(matrices, FWD_AT, jnp.minimum(slot, 1)), (head[slot], tail[slot]))
            for slot in slots
        ]
        codes = []
        for left, right in loaded:
            spectrum = product3(left, right, NT).reshape(GX, SLAB, 128)
            codes.append([encode(spectrum[:, :FIRST]), encode(spectrum[:, FIRST:])])
        for slot, pieces in zip(slots, codes):
            for side in range(2):
                slabs[pl.ds(slot * GX, GX), sides[side]] = pieces[side]

    steps = GY // 2

    def slot_body(step, carry):
        slots = slots_at(2 * step) + slots_at(2 * step + 1)
        slot_products(slots)
        for slot in slots:
            send_slot(0, slot, octants, landed, sem_out, sem_in)
        return carry

    lax.fori_loop(0, steps // 2 - 1, slot_body, 0)
    twin = slots_at(steps - 1)[0]
    nearby = slots_at(steps - 2)
    slot_products(nearby + [twin, slot_own])
    for slot in nearby:
        send_slot(0, slot, octants, landed, sem_out, sem_in)
    send_slot(0, twin, octants, landed, sem_out, sem_in)
    send_slot(0, slot_own, octants[:-1], landed, sem_out, sem_in)
    keep_own(0, landed, sem_in)

    def second_body(step, carry):
        for slot in slots_at(step):
            send_slot(1, slot, octants, landed, sem_out, sem_in)
        return carry

    lax.fori_loop(0, steps - 1, second_body, 0)
    send_slot(1, twin, octants, landed, sem_out, sem_in)
    send_slot(1, slot_own, octants[:-1], landed, sem_out, sem_in)
    keep_own(1, landed, sem_in)

    def spread(side):
        first = 0 if side == 0 else FIRST
        count = FIRST if side == 0 else SLAB - FIRST

        def body(step, carry):
            slots = slots_before(step)
            wait_group(side, slots, landed, sem_in)
            for slot in slots:
                values = decode(landed[pl.ds(slot * GX, GX), sides[side]])
                for source in range(GX):
                    columns[
                        pl.ds(first * PLANE + slot * GX + source, count, stride=PLANE), :
                    ] = values[source]
            return carry

        return body

    def plane(row):
        return slice(row * 128, row * 128 + 128)

    def column_rows(row):
        return slice(row * PLANE, row * PLANE + 128)

    def stack_pair(reals, imags):
        return jnp.concatenate(
            [jnp.concatenate(reals, axis=1), jnp.concatenate(imags, axis=1)], axis=0
        )

    def work_columns(groups):
        members = [member for group in groups for member in group]
        cosine = floats[SPIN_AT : SPIN_AT + 128, :]
        sine = floats[SPIN_AT + 128 : SPIN_AT + 256, :]
        loaded = [
            stack_pair(
                [columns[column_rows(REAL_ROWS[member]), :] for member in group],
                [columns[column_rows(IMAG_ROWS[member]), :] for member in group],
            )
            for group in groups
        ]
        turned = []
        for group, values in zip(groups, loaded):
            mixed = product3(square_pair(matrices, 0), parts(values), NN)
            for index in range(len(group)):
                real, imag = mixed[:128, plane(index)], mixed[128:, plane(index)]
                turned.append(
                    jnp.concatenate(
                        [real * cosine + imag * sine, imag * cosine - real * sine], axis=1
                    )
                )
        modes = product3(
            parts(jnp.concatenate(turned, axis=0)), square_pair(matrices, 2), NN
        )
        changed = []
        for index, member in enumerate(members):
            piece = modes[plane(index)]
            real, imag = apply_gains(gains, member, piece[:, :128], piece[:, 128:])
            changed.append(jnp.concatenate([real, imag], axis=1))
        mixed = product3(
            parts(jnp.concatenate(changed, axis=0)), square_pair(matrices, 3), NN
        )
        start = 0
        done = []
        for group in groups:
            reals, imags = [], []
            for index in range(start, start + len(group)):
                piece = mixed[plane(index)]
                real, imag = piece[:, :128], piece[:, 128:]
                reals.append(real * cosine - imag * sine)
                imags.append(imag * cosine + real * sine)
            start += len(group)
            done.append(
                product3(square_pair(matrices, 1), parts(stack_pair(reals, imags)), NN)
            )
        for group, values in zip(groups, done):
            for index, member in enumerate(group):
                columns[column_rows(REAL_ROWS[member]), :] = values[:128, plane(index)]
                columns[column_rows(IMAG_ROWS[member]), :] = values[128:, plane(index)]

    def collect(side, slots):
        first = 0 if side == 0 else FIRST
        count = FIRST if side == 0 else SLAB - FIRST
        codes = [
            encode(
                jnp.stack(
                    [
                        columns[
                            pl.ds(first * PLANE + slot * GX + source, count, stride=PLANE), :
                        ]
                        for source in range(GX)
                    ]
                )
            )
            for slot in slots
        ]
        for slot, code in zip(slots, codes):
            slabs[pl.ds(slot * GX, GX), sides[side]] = code

    def send_back(side):
        def body(step, carry):
            slots = slots_at(step)
            collect(side, slots)
            for slot in slots:
                send_slot(side, slot, octants, returned, sem_back_out, sem_back_in)
            return carry

        wait_sent(side, sem_out)
        lax.fori_loop(0, steps - 1, body, 0)
        collect(side, [twin, slot_own])
        send_slot(side, twin, octants, returned, sem_back_out, sem_back_in)
        send_slot(side, slot_own, octants[:-1], returned, sem_back_out, sem_back_in)
        keep_own(side, returned, sem_back_in)

    lax.fori_loop(0, steps, spread(0), 0)
    columns[column_rows(FIRST - 1), :] = jnp.zeros((128, 128), F32)
    work_columns([(0, 1), (2, 3), (4, 5)])
    lax.fori_loop(0, steps, spread(1), 0)
    columns[column_rows(SLAB - 1), :] = jnp.zeros((128, 128), F32)
    work_columns([(6, 7)])
    send_back(0)
    work_columns([(8, 9), (10,)])
    send_back(1)

    def wave_part(side, slots):
        start = INV_AT if side == 0 else INV_AT + GX * FIRST
        count = GX * FIRST if side == 0 else GX * (SLAB - FIRST)
        loaded = [
            (
                returned[pl.ds(slot * GX, GX), sides[side]],
                matrix_pair(matrices, start, jnp.minimum(slot, 1), count),
            )
            for slot in slots
        ]
        return [
            product3(parts(decode(codes).reshape(count, 128)), right, TN)
            for codes, right in loaded
        ]

    def first_wave(step, carry):
        slots = []
        for index in (2 * step, 2 * step + 1):
            couple = slots_before(index)
            wait_group(0, couple, returned, sem_back_in)
            slots.extend(couple)
        for slot, values in zip(slots, wave_part(0, slots)):
            waves[slot] = values
        return carry

    def second_wave(step, carry):
        slots = []
        for index in (4 * step, 4 * step + 1, 4 * step + 2, 4 * step + 3):
            couple = slots_before(index)
            wait_group(1, couple, returned, sem_back_in)
            slots.extend(couple)
        before = [waves[slot] for slot in slots]
        done = []
        for slot, values, base in zip(slots, wave_part(1, slots), before):
            values = values + base
            cosine = floats[pl.ds(32 * slot, 1), :]
            sine = floats[pl.ds(32 * slot + 16, 1), :]
            real, imag = values[:, :128], values[:, 128:]
            done.append((real * cosine - imag * sine, imag * cosine + real * sine))
        for slot, (real, imag) in zip(slots, done):
            waves[slot, :, 0:128] = real
            waves[slot, :, 128:256] = imag
        return carry

    lax.fori_loop(0, steps // 2, first_wave, 0)
    lax.fori_loop(0, steps // 4, second_wave, 0)

    def grid_body(step, carry):
        field = step // 2
        part = step % 2
        rows = pl.ds(pl.multiple_of(step * 16, 16), 16)
        spectrum = [(waves[0, rows, 0:128], None)]
        for slot in range(1, GY):
            spectrum.append((waves[slot, rows, 0:128], waves[slot, rows, 128:256]))
        spectrum.append((waves[0, rows, 128:256], None))
        values = real_inverse(spectrum)
        top = pl.ds(pl.multiple_of(part * 16, 16), 16)
        for c in range(32):
            new_rows[field, c // 4, top, (c % 4) * 128 : (c % 4) * 128 + 128] = values[c].astype(BF16)
        return carry

    for field in range(FIELDS):
        lax.fori_loop(2 * field, 2 * field + 2, grid_body, 0)
        for other in octants[:-1]:
            pltpu.make_async_remote_copy(
                src_ref=new_rows.at[field, other],
                dst_ref=results[field].at[own_rows, :],
                send_sem=sem_last_out,
                recv_sem=sem_last_in.at[field],
                device_id=(other, slot_own),
                device_id_type=MESH,
            ).start()
        pltpu.make_async_copy(
            new_rows.at[field, octant], results[field].at[own_rows, :], sem_last_in.at[field]
        ).start()

    for side in range(2):
        wait_sent(side, sem_back_out)
    moved = new_rows.at[:, pl.ds(0, GX - 1)]
    pltpu.make_async_copy(moved, moved, sem_rows_out).wait()
    pltpu.make_async_copy(moved, moved, sem_last_out).wait()
    for field in range(FIELDS):
        pltpu.make_async_copy(results[field], results[field], sem_last_in.at[field]).wait()


def place_kernel(*refs):
    copies = [
        pltpu.make_async_copy(refs[field], refs[FIELDS + field], refs[2 * FIELDS].at[field])
        for field in range(FIELDS)
    ]
    for copy in copies:
        copy.start()
    for copy in copies:
        copy.wait()


def per_device(east_wind, north_wind, height, tracer):
    constants = [jnp.asarray(value) for value in tables()]
    anywhere = pl.BlockSpec(memory_space=pl.ANY)
    block = jax.ShapeDtypeStruct((NG // GY, COLS), BF16)
    dma = pltpu.SemaphoreType.DMA
    landed = pl.pallas_call(
        step_kernel,
        out_shape=(block,) * 4,
        in_specs=[pl.BlockSpec(memory_space=pltpu.HBM)] * 6,
        out_specs=(anywhere,) * 4,
        scratch_shapes=[
            pltpu.VMEM((MATRIX_ROWS, 256), BF16),
            pltpu.VMEM((FLOAT_ROWS, 128), F32),
            pltpu.VMEM((FIELDS, GX, ROWS, COLS), BF16),
            pltpu.VMEM((GY, 128, 256), BF16),
            pltpu.VMEM((GY, 128, 256), BF16),
            pltpu.VMEM((DEVICES, SLAB // 8, 8, 128), BF16),
            pltpu.VMEM((DEVICES, SLAB // 8, 8, 128), BF16),
            pltpu.VMEM(((SLAB + 1) * PLANE, 128), F32),
            pltpu.VMEM((KX, 4, 128, 128), F32),
            pltpu.VMEM((DEVICES, SLAB // 8, 8, 128), BF16),
            pltpu.VMEM((GY, 128, 256), F32),
            pltpu.VMEM((FIELDS, GX, ROWS, COLS), BF16),
            dma((2,)),
            dma,
            dma((FIELDS,)),
            dma((2,)),
            dma((2, GY // 2)),
            dma((2,)),
            dma((2, GY // 2)),
            dma,
            dma((FIELDS,)),
            pltpu.SemaphoreType.REGULAR,
            pltpu.SemaphoreType.REGULAR,
        ],
        compiler_params=pltpu.CompilerParams(
            collective_id=0, has_side_effects=True, vmem_limit_bytes=32 * 1024 * 1024
        ),
    )(*[
        pltpu.with_memory_space_constraint(value, pltpu.HBM)
        for value in (east_wind, north_wind, height, tracer, *constants)
    ])
    return pl.pallas_call(
        place_kernel,
        out_shape=(block,) * 4,
        in_specs=[anywhere] * 4,
        out_specs=(pl.BlockSpec(memory_space=pltpu.HBM),) * 4,
        scratch_shapes=[dma((FIELDS,))],
        compiler_params=pltpu.CompilerParams(vmem_limit_bytes=1024 * 1024),
    )(*landed)


def solution(mesh):
    placed = (P("gy", "gx"),) * 4
    return jax.shard_map(
        per_device, mesh=mesh, in_specs=placed, out_specs=placed, check_vma=False
    )
```
